32 devices in a mesh: region: 8 (over z, y), depth: 4 (over x, core).
Axes of the slice: x: 2, y: 2, z: 4, core: 2. Of those that a mesh axis runs over, the one named last changes fastest.
Arguments:
- displacement: float32 [16, 16, 3, 1024], P('depth', None, None, 'region'), may hold values from -1.5 to 1.5
- velocity: float32 [16, 16, 3, 1024], P('depth', None, None, 'region'), may hold values from -4 to 4
- growth: float32 [16, 16, 1024], P('depth', None, 'region'), may hold values from 1 to 1.6
- shear_modulus: float32 [16, 16, 1024], P('depth', None, 'region'), may hold values from 0.3 to 3
- pair_slots: int32 [4, 8, 3, 16], P('depth', 'region'), may hold values from 0 to 63, as said below
- pair_count: int32 [4, 8], P('depth', 'region'), may hold values from 12 to 16, as said below
- separation: float32 [4, 8, 3, 16], P('depth', 'region'), may hold values from -1 to 1, as said below
Outputs:
- new_velocity: float32 [16, 16, 3, 1024], P('depth', None, None, 'region')
- new_displacement: float32 [16, 16, 3, 1024], P('depth', None, None, 'region')
The draws below stay inside these ranges and needn't reach their ends.
Inputs may be any that keep to these rules, and one draw needn't show every extreme that they name: `pair_slots`: row 0 of a slot is a patch of the own region below 64, row 1 a region, row 2 a patch of that region below 64. Slots k < pair_count[s, r] are live and name another region; the rest hold arbitrary values in the same ranges. Contact is symmetric: a live slot (l, m, q) with separation o on (s, r) comes with a live slot (q, r, l) with separation -o on (s, m). At most 4 live slots of one region and slab name the same region; in every slab some region has exactly 4 live slots for every region it names. `pair_count`: in every slab some region has 16 live slots. `separation`: opposite on the two sides of a contact, as stated for pair_slots.
All inputs are finite; a program needn't handle non-finite values.
Results may differ from the reference program's by a relative error of at most 0.0003.
Values sent between devices are 32-bit elements; how exact they have to be, the bound alone decides.
No kernel may reach another device: no remote copies, remote signals or barrier semaphores. Data moves between devices by JAX's collectives and lax.ppermute only.
A program may use at most 64 MiB of HBM per device.

```python
import math
import jax
import jax.numpy as jnp
from jax import lax

PATCH = 128
SZ = 4
SY = 16
CAP = 4
SLABS = 4
REGIONS = 8
NZ = 16
NX = 1024
PATCH_DEV = 64
PAIRS = 16


def pair_tables(key):
    base = jax.random.fold_in(key, 4411)
    key_perm, key_level, key_hot, key_first, key_second, key_junk = jax.random.split(base, 6)
    half = REGIONS // 2
    perm_keys = jax.random.split(key_perm, SLABS)
    perms = jax.vmap(lambda single: jax.random.permutation(single, REGIONS - 1))(perm_keys)
    masks = perms[:, :half].astype(jnp.int32) + 1
    region = jnp.arange(REGIONS, dtype=jnp.int32)
    partner = jnp.bitwise_xor(region[None, :, None], masks[:, None, :])
    level = jax.random.randint(key_level, (SLABS, REGIONS), max(1, CAP - 1), CAP + 1).astype(jnp.int32)
    hot = jax.random.randint(key_hot, (SLABS,), 0, REGIONS).astype(jnp.int32)
    other_level = jnp.take_along_axis(level, partner.reshape(SLABS, REGIONS * half), axis=1).reshape(SLABS, REGIONS, half)
    count = jnp.minimum(level[:, :, None], other_level)
    is_hot = (region[None, :, None] == hot[:, None, None]) | (partner == hot[:, None, None])
    count = jnp.where(is_hot, CAP, count)
    full_shape = (SLABS, REGIONS, half, CAP)
    lower_full = jnp.broadcast_to((region[None, :, None] < partner)[..., None], full_shape)
    low_full = jnp.broadcast_to(jnp.minimum(region[None, :, None], partner)[..., None], full_shape)
    first = jax.random.randint(key_first, full_shape, 0, PATCH_DEV).astype(jnp.int32)
    second = jax.random.randint(key_second, full_shape, 0, PATCH_DEV).astype(jnp.int32)
    first_low = jnp.take_along_axis(first, low_full, axis=1)
    second_low = jnp.take_along_axis(second, low_full, axis=1)
    own_patch = jnp.where(lower_full, first_low, second_low).reshape(SLABS, REGIONS, PAIRS)
    peer_patch = jnp.where(lower_full, second_low, first_low).reshape(SLABS, REGIONS, PAIRS)
    peer = jnp.broadcast_to(partner[..., None], full_shape).reshape(SLABS, REGIONS, PAIRS)
    live = (jnp.arange(CAP, dtype=jnp.int32)[None, None, None, :] < count[..., None]).reshape(SLABS, REGIONS, PAIRS)
    slot_ids = jnp.arange(PAIRS, dtype=jnp.int32)
    score = jnp.where(live, 0, 1) * PAIRS + slot_ids[None, None, :]
    order = jnp.argsort(score, axis=-1, stable=True).astype(jnp.int32)
    total = jnp.sum(live.astype(jnp.int32), axis=-1).astype(jnp.int32)
    own_patch = jnp.take_along_axis(own_patch, order, axis=2)
    peer_patch = jnp.take_along_axis(peer_patch, order, axis=2)
    peer = jnp.take_along_axis(peer, order, axis=2)
    junk_a, junk_b, junk_c = jax.random.split(key_junk, 3)
    dead = slot_ids[None, None, :] >= total[..., None]
    small_shape = (SLABS, REGIONS, PAIRS)
    own_patch = jnp.where(dead, jax.random.randint(junk_a, small_shape, 0, PATCH_DEV).astype(jnp.int32), own_patch)
    peer = jnp.where(dead, jax.random.randint(junk_b, small_shape, 0, REGIONS).astype(jnp.int32), peer)
    peer_patch = jnp.where(dead, jax.random.randint(junk_c, small_shape, 0, PATCH_DEV).astype(jnp.int32), peer_patch)
    return (own_patch, peer, peer_patch, total, order, low_full, lower_full)


def draw_pair_slots(key, part):
    tables = pair_tables(key)
    return jnp.stack([tables[0], tables[1], tables[2]], axis=2).astype(jnp.int32)


def draw_pair_count(key, part):
    tables = pair_tables(key)
    return tables[3].astype(jnp.int32)


def draw_separation(key, part):
    tables = pair_tables(key)
    order = tables[4]
    low_full = tables[5]
    lower_full = tables[6]
    sep_key = jax.random.fold_in(key, 9173)
    shape = (SLABS, REGIONS, REGIONS // 2, CAP, 3)
    raw = jax.random.uniform(sep_key, shape, jnp.float32, -1.0, 1.0)
    picked = jnp.take_along_axis(raw, jnp.broadcast_to(low_full[..., None], shape), axis=1)
    signed = jnp.where(lower_full[..., None], picked, -picked)
    flat = signed.reshape(SLABS, REGIONS, PAIRS, 3)
    ordered = jnp.take_along_axis(flat, jnp.broadcast_to(order[..., None], flat.shape), axis=2)
    return jnp.transpose(ordered, (0, 1, 3, 2)).astype(jnp.float32)


def block_scale(rng, dims, pieces, smallest, largest):
    loudness = 1.0
    for dim, shards_of in pieces:
        heights = jax.random.uniform(jax.random.fold_in(jax.random.fold_in(rng, 6), dim), (shards_of,), jnp.float32, smallest / len(pieces), largest / len(pieces))
        loudness = loudness * jnp.repeat(jnp.exp(heights), dims[dim] // shards_of).reshape((-1,) + (1,) * (len(dims) - 1 - dim))
    return loudness


def centred(own_key, dims, scale, reach, pieces=(), held_as=jnp.bfloat16):
    array = jax.random.normal(own_key, dims, jnp.float32) * scale
    if len(pieces) > 0:
        array = block_scale(own_key, dims, pieces, -0.22, 0.18) * array
    return jnp.clip(array, min=-reach, max=reach).astype(held_as)


def setup_inputs(seed: int = 0) -> dict:
    keys = jax.random.split(jax.random.key(seed), 8)
    return {
        "displacement": centred(keys[0], (NZ, SY, 3, NX), 0.1, 1.5, ((0, 4), (3, 8)), jnp.float32),
        "velocity": centred(keys[1], (NZ, SY, 3, NX), 0.5, 4.0, ((0, 4), (3, 8)), jnp.float32),
        "growth": jnp.clip(jnp.exp(math.log(1.6) - 0.47000364 * jax.random.uniform(keys[2], (NZ, SY, NX), jnp.float32) ** block_scale(keys[2], (NZ, SY, NX), ((0, 4), (2, 8)), -0.2, 0.2)), 1.0, 1.6),
        "shear_modulus": jnp.clip(jnp.exp(math.log(3.0) - 2.3025851 * jax.random.uniform(keys[3], (NZ, SY, NX), jnp.float32) ** block_scale(keys[3], (NZ, SY, NX), ((0, 4), (2, 8)), -0.2, 0.2)), 0.3, 3.0),
        "pair_slots": draw_pair_slots(jax.random.fold_in(keys[7], 71), 0),
        "pair_count": draw_pair_count(jax.random.fold_in(keys[7], 71), 0),
        "separation": draw_separation(jax.random.fold_in(keys[7], 71), 0),
    }


PERMUTATIONS = ((0, 1, 2), (0, 2, 1), (1, 0, 2), (1, 2, 0), (2, 0, 1), (2, 1, 0))
CORNER_SET = ((0, 0, 0), (0, 0, 1), (0, 1, 0), (0, 1, 1), (1, 0, 0), (1, 0, 1), (1, 1, 0), (1, 1, 1))
REST_VOLUME = 1.0 / 6.0
STEP_TIME = 0.2


def unit_step(component):
    return tuple(1 if position == 2 - component else 0 for position in range(3))


def joined(first_offset, second_offset):
    return tuple(first_offset[index] + second_offset[index] for index in range(3))


def shifted(field, offset):
    return jnp.roll(field, (-offset[0], -offset[1], -offset[2]), axis=(0, 1, 2))


def cell_forces(displacement, growth, shear, valid):
    fields = [displacement[:, :, index, :] for index in range(3)]
    corners = {offset: [shifted(field, offset) for field in fields] for offset in CORNER_SET}
    inverse = 1.0 / growth
    squared = growth * growth
    weight = valid * REST_VOLUME
    totals = {offset: [jnp.zeros_like(growth) for index in range(3)] for offset in CORNER_SET}
    for ordering in PERMUTATIONS:
        first_axis, second_axis, third_axis = ordering
        start = (0, 0, 0)
        middle = unit_step(first_axis)
        upper = joined(middle, unit_step(second_axis))
        summit = (1, 1, 1)
        columns = [None, None, None]
        columns[first_axis] = [corners[middle][row] - corners[start][row] for row in range(3)]
        columns[second_axis] = [corners[upper][row] - corners[middle][row] for row in range(3)]
        columns[third_axis] = [corners[summit][row] - corners[upper][row] for row in range(3)]
        elastic_f = [[(columns[col][row] + (1.0 if row == col else 0.0)) * (inverse if col < 2 else 1.0) for col in range(3)] for row in range(3)]
        cofactor = [[elastic_f[(row + 1) % 3][(col + 1) % 3] * elastic_f[(row + 2) % 3][(col + 2) % 3]
                     - elastic_f[(row + 1) % 3][(col + 2) % 3] * elastic_f[(row + 2) % 3][(col + 1) % 3]
                     for col in range(3)] for row in range(3)]
        jacobian = elastic_f[0][0] * cofactor[0][0] + elastic_f[0][1] * cofactor[0][1] + elastic_f[0][2] * cofactor[0][2]
        pressure = 4.0 * (jacobian - 1.25)
        stress = [[shear * (elastic_f[row][col] + pressure * cofactor[row][col]) * (growth if col < 2 else squared) * weight
                   for col in range(3)] for row in range(3)]
        for row in range(3):
            col_first = stress[row][first_axis]
            col_second = stress[row][second_axis]
            col_third = stress[row][third_axis]
            totals[start][row] = totals[start][row] + col_first
            totals[middle][row] = totals[middle][row] + (col_second - col_first)
            totals[upper][row] = totals[upper][row] + (col_third - col_second)
            totals[summit][row] = totals[summit][row] - col_third
    result = []
    for row in range(3):
        summed = jnp.zeros_like(growth)
        for offset in CORNER_SET:
            summed = summed + jnp.roll(totals[offset][row], offset, axis=(0, 1, 2))
        result.append(summed)
    return jnp.stack(result, axis=2)


def pair_forces(near, far):
    deltas = [near[:, index, :, None] - far[:, index, None, :] for index in range(3)]
    distance = deltas[0] * deltas[0] + deltas[1] * deltas[1] + deltas[2] * deltas[2]
    kernel = jnp.exp(-distance)
    return jnp.stack([jnp.sum(delta * kernel, axis=2) for delta in deltas], axis=1)


def reference(displacement, velocity, growth, shear_modulus, pair_slots, pair_count, separation):
    z_index = jnp.arange(NZ, dtype=jnp.int32)
    y_index = jnp.arange(SY, dtype=jnp.int32)
    valid = (z_index <= NZ - 2)[:, None, None] & (y_index <= SY - 2)[None, :, None]
    valid = jnp.broadcast_to(valid, (NZ, SY, NX)).astype(displacement.dtype)
    elastic = cell_forces(displacement, growth, shear_modulus, valid)
    component_row = lax.broadcasted_iota(jnp.int32, (3, PATCH), 0)
    along_row = lax.broadcasted_iota(jnp.int32, (3, PATCH), 1).astype(displacement.dtype)
    rest_line = jnp.where(component_row == 0, along_row, jnp.zeros_like(along_row))
    points = displacement.reshape(SLABS, SZ, SY, 3, REGIONS, PATCH).transpose(0, 4, 1, 2, 3, 5)
    points = points.reshape(SLABS, REGIONS, SZ * SY, 3, PATCH) + rest_line
    patch_ids = jnp.arange(SZ * SY, dtype=jnp.int32)
    slot_ids = jnp.arange(PAIRS, dtype=jnp.int32)

    def one_device(index):
        slab = index // REGIONS
        region = index % REGIONS
        slots = pair_slots[slab, region]
        live = slot_ids < pair_count[slab, region]
        offsets = jnp.transpose(separation[slab, region])
        slab_points = points[slab]
        near = slab_points[region][slots[0]]
        far = slab_points[slots[1], slots[2]] + offsets[:, :, None]
        forces = pair_forces(near, far) * live[:, None, None].astype(near.dtype)
        selector = ((slots[0][:, None] == patch_ids[None, :]) & live[:, None]).astype(near.dtype)
        return jnp.einsum("kp,kcx->pcx", selector, forces, precision=lax.Precision.HIGHEST)

    contact = lax.map(one_device, jnp.arange(SLABS * REGIONS, dtype=jnp.int32))
    contact = contact.reshape(SLABS, REGIONS, SZ, SY, 3, PATCH).transpose(0, 2, 3, 4, 1, 5).reshape(NZ, SY, 3, NX)
    new_velocity = velocity + STEP_TIME * (elastic + contact)
    new_displacement = displacement + STEP_TIME * new_velocity
    return (new_velocity, new_displacement)
```

```python
import functools

import jax
import jax.numpy as jnp
from jax import lax
from jax.experimental import pallas as pl
from jax.experimental.pallas import tpu as pltpu
from jax.sharding import PartitionSpec as P

CAP = 4
STEP_TIME = 0.2
REST_VOLUME = 1.0 / 6.0
PERMUTATIONS = ((0, 1, 2), (0, 2, 1), (1, 0, 2), (1, 2, 0), (2, 0, 1), (2, 1, 0))
ROWS = 4

VMEM = pl.BlockSpec(memory_space=pltpu.VMEM)
SMEM = pl.BlockSpec(memory_space=pltpu.SMEM)


def add(total, term):
    return term if total is None else total + term


def unit(axis):
    return tuple(1 if position == 2 - axis else 0 for position in range(3))


def tensions(edges, growth, scale_side, scale_up):
    inverse = 1.0 / growth
    columns = {}
    for (axis, start), rows in edges.items():
        made = []
        for row in range(3):
            value = rows[row] + 1.0 if row == axis else rows[row]
            made.append(value * inverse if axis < 2 else value)
        columns[(axis, start)] = made
    pulls = {}
    for first, second, third in PERMUTATIONS:
        middle = unit(first)
        upper = tuple(a + b for a, b in zip(middle, unit(second)))
        keys = {first: (first, (0, 0, 0)), second: (second, middle), third: (third, upper)}
        fe = [[columns[keys[col]][row] for col in range(3)] for row in range(3)]
        cof = [
            [
                fe[(row + 1) % 3][(col + 1) % 3] * fe[(row + 2) % 3][(col + 2) % 3]
                - fe[(row + 1) % 3][(col + 2) % 3] * fe[(row + 2) % 3][(col + 1) % 3]
                for col in range(3)
            ]
            for row in range(3)
        ]
        jacobian = fe[0][0] * cof[0][0] + fe[0][1] * cof[0][1] + fe[0][2] * cof[0][2]
        pressure = 4.0 * jacobian - 5.0
        for col in range(3):
            key = keys[col]
            for row in range(3):
                pulls.setdefault(key, [None] * 3)
                pulls[key][row] = add(pulls[key][row], fe[row][col] + pressure * cof[row][col])
    return {
        key: [value * (scale_side if key[0] < 2 else scale_up) for value in rows]
        for key, rows in pulls.items()
    }


def roll(value, shift, axis):
    size = value.shape[axis]
    shift = shift % size
    return value if shift == 0 else pltpu.roll(value, shift, axis)


def lane_of(shape):
    return lax.broadcasted_iota(jnp.int32, shape, len(shape) - 1)


def column_pack(fields, lane_from, stride, offset):
    shape = fields[0][0].shape
    lane = lane_of(shape)
    packed = jnp.zeros(shape, jnp.float32)
    for c, layers in enumerate(fields):
        for z, field in enumerate(layers):
            to = c * stride + z + offset
            packed = jnp.where(lane == to, roll(field, to - lane_from, 1), packed)
    return packed


def pack_kernel(dims, disp, growth, shear, slots, count, packet, z_up, z_down, table, face):
    slab_len, width_y, patch_len, regions, slabs, pairs = dims
    region = lax.axis_index("region")
    depth = lax.axis_index("depth")
    patches = slab_len * width_y
    stride = slab_len + 2
    live_slots = count[0, 0]

    z_up[0:3] = disp[slab_len - 1]
    z_up[3] = growth[slab_len - 1]
    z_up[4] = shear[slab_len - 1]
    z_down[...] = disp[0]

    def order_key(k):
        own, other, far = slots[0, 0, 0, k], slots[0, 1, 0, k], slots[0, 2, 0, k]
        code = jnp.where(other > region, own * patches + far, far * patches + own)
        code = (other * (patches * patches) + code) * pairs + k
        return jnp.where(k < live_slots, code, -1)

    def place(k, keys):
        own, other = slots[0, 0, 0, k], slots[0, 1, 0, k]
        mine = keys[k] if isinstance(k, int) else order_key(k)
        floor = other * (patches * patches * pairs)
        if isinstance(k, int):
            rank = jnp.int32(0)
            for t in range(pairs):
                if t != k:
                    rank = rank + jnp.where((keys[t] >= floor) & (keys[t] < mine), 1, 0)
        else:

            def count_one(t, rank):
                key = order_key(t)
                return rank + jnp.where((key >= floor) & (key < mine), 1, 0)

            rank = lax.fori_loop(0, pairs, count_one, jnp.int32(0))
        rank = jnp.minimum(rank, CAP - 1)
        live = k < live_slots
        target = (jnp.where(live, other, region) * slabs + depth) * CAP + jnp.where(live, rank, 0)
        table[0, k] = target
        z, y = own // width_y, own % width_y
        for c in range(3):
            packet[target, c : c + 1, :] = disp[z, c, pl.ds(y, 1), :]

    if pairs <= 16:
        keys = [order_key(k) for k in range(pairs)]
        for k in range(pairs):
            place(k, keys)
    else:

        def place_one(k, carry):
            place(k, None)
            return carry

        lax.fori_loop(0, pairs, place_one, 0)

    groups = width_y // CAP
    width = patch_len // groups
    fields = [[disp[z, c] for z in range(slab_len)] for c in range(3)]
    fields = fields + [[growth[z] for z in range(slab_len)], [shear[z] for z in range(slab_len)]]
    sides = ((patch_len - 1, fields, 1), (0, fields[:3], regions - 1))
    lane = lane_of((CAP, patch_len))
    for side, (lane_from, chosen, step) in enumerate(sides):
        face[side] = column_pack(chosen, lane_from, stride, 1)
        folded = jnp.zeros((CAP, patch_len), jnp.float32)
        for g in range(groups):
            part = roll(face[side, g * CAP : (g + 1) * CAP, :], g * width, 1)
            folded = jnp.where((lane >= g * width) & (lane < (g + 1) * width), part, folded)
        other = lax.rem(region + step, regions)
        for s in range(slabs):
            base = (other * slabs + s) * CAP
            for j in range(CAP):
                packet[base + j, 3:4, :] = folded[j : j + 1, :]


def inner_kernel(
    dims, disp, growth, shear, velocity, below, above, slots, before, near, own_columns
):
    slab_len, width_y, patch_len, regions, slabs, pairs = dims
    depth = lax.axis_index("depth")
    shape = (width_y, patch_len)
    lane = lane_of(shape)
    row_y = lax.broadcasted_iota(jnp.int32, shape, 0)
    inside = (lane < patch_len - 1) & (row_y < width_y - 1)
    nodes = [[below[c] for c in range(3)]]
    nodes += [[disp[z, c] for c in range(3)] for z in range(slab_len)]
    nodes += [[above[c] for c in range(3)]]
    has_below = depth > 0
    has_above = depth < slabs - 1
    cell_growth = [jnp.where(has_below, below[3], 1.0)] + [growth[z] for z in range(slab_len)]
    cell_shear = [below[4]] + [shear[z] for z in range(slab_len)]

    own_columns[0] = column_pack(
        [[nodes[z][c] for z in range(slab_len + 2)] for c in range(3)]
        + [cell_growth, cell_shear],
        patch_len - 1,
        slab_len + 2,
        0,
    )
    own_columns[1] = column_pack(
        [[nodes[z][c] for z in range(slab_len + 2)] for c in range(3)], 0, slab_len + 2, 0
    )

    axis_x, axis_y, axis_z = 0, 1, 2
    pull_x = [[None] * 3 for _ in range(slab_len + 2)]
    pull_y = [[None] * 3 for _ in range(slab_len + 2)]
    pull_z = [[None] * 3 for _ in range(slab_len + 2)]

    def layer_edges(layer):
        along_x, along_y, moved = {}, {}, {}
        for c in range(3):
            base = layer[c]
            next_x = roll(base, -1, 1)
            next_y = roll(base, -1, 0)
            next_xy = roll(next_y, -1, 1)
            moved[c] = {(0, 0): base, (0, 1): next_x, (1, 0): next_y, (1, 1): next_xy}
            along_x[c] = {0: next_x - base, 1: next_xy - next_y}
            along_y[c] = {0: next_y - base, 1: next_xy - next_x}
        return along_x, along_y, moved

    low = layer_edges(nodes[0])
    for zc in range(slab_len + 1):
        high = layer_edges(nodes[zc + 1])
        edges = {}
        for dz, (along_x, along_y, _) in enumerate((low, high)):
            for other in range(2):
                edges[(axis_x, (dz, other, 0))] = [along_x[c][other] for c in range(3)]
                edges[(axis_y, (dz, 0, other))] = [along_y[c][other] for c in range(3)]
        for dy in range(2):
            for dx in range(2):
                edges[(axis_z, (0, dy, dx))] = [
                    high[2][c][(dy, dx)] - low[2][c][(dy, dx)] for c in range(3)
                ]
        growth_here = cell_growth[zc]
        valid = inside
        if zc == 0:
            valid = valid & has_below
        if zc == slab_len:
            valid = valid & has_above
        scale = jnp.where(valid, cell_shear[zc] * REST_VOLUME, 0.0) * growth_here
        pulls = tensions(edges, growth_here, scale, scale * growth_here)
        for c in range(3):
            for dz in range(2):
                near_row = pulls[(axis_x, (dz, 0, 0))][c]
                far_row = pulls[(axis_x, (dz, 1, 0))][c]
                pull_x[zc + dz][c] = add(pull_x[zc + dz][c], near_row + roll(far_row, 1, 0))
                near_row = pulls[(axis_y, (dz, 0, 0))][c]
                far_row = pulls[(axis_y, (dz, 0, 1))][c]
                pull_y[zc + dz][c] = add(pull_y[zc + dz][c], near_row + roll(far_row, 1, 1))
            at_zero = pulls[(axis_z, (0, 0, 0))][c] + roll(pulls[(axis_z, (0, 1, 0))][c], 1, 0)
            at_one = pulls[(axis_z, (0, 0, 1))][c] + roll(pulls[(axis_z, (0, 1, 1))][c], 1, 0)
            pull_z[zc][c] = at_zero + roll(at_one, 1, 1)
        low = high
        if zc > 0:
            for c in range(3):
                force = pull_x[zc][c] - roll(pull_x[zc][c], 1, 1)
                force = force + (pull_y[zc][c] - roll(pull_y[zc][c], 1, 0))
                force = force + (pull_z[zc][c] - pull_z[zc - 1][c])
                before[zc - 1, c] = velocity[zc - 1, c] + STEP_TIME * force

    def fetch(k):
        own = slots[0, 0, 0, k]
        z, y = own // width_y, own % width_y
        for c in range(3):
            near[c, pl.ds(k, 1), :] = disp[z, c, pl.ds(y, 1), :]

    if pairs <= 16:
        for k in range(pairs):
            fetch(k)
    else:

        def fetch_one(k, carry):
            fetch(k)
            return carry

        lax.fori_loop(0, pairs, fetch_one, 0)


def border_forces(dims, arrived, own_columns, unfold):
    slab_len, width_y, patch_len, regions, slabs, pairs = dims
    region = lax.axis_index("region")
    depth = lax.axis_index("depth")
    stride = slab_len + 2
    groups = width_y // CAP
    width = patch_len // groups
    half = patch_len // 2
    fold_lane = lane_of((CAP, patch_len))
    fold_z = lax.rem(lax.rem(fold_lane, width), stride)
    for side, step in enumerate((regions - 1, 1)):
        other = lax.rem(region + step, regions)

        def block(slab):
            base = (other * slabs + slab) * CAP
            return jnp.concatenate([arrived[base + j, 3:4, :] for j in range(CAP)], axis=0)

        merged = block(depth)
        lower = block(lax.rem(depth + slabs - 1, slabs))
        upper = block(lax.rem(depth + 1, slabs))
        merged = jnp.where(fold_z == 0, roll(lower, -slab_len, 1), merged)
        merged = jnp.where(fold_z == slab_len + 1, roll(upper, slab_len, 1), merged)
        for g in range(groups):
            unfold[side, g * CAP : (g + 1) * CAP, :] = roll(merged, -g * width, 1)
    from_left = unfold[0]
    from_right = unfold[1]
    own_last = own_columns[0]
    own_first = own_columns[1]
    shape = (width_y, patch_len)
    lane = lane_of(shape)
    row_y = lax.broadcasted_iota(jnp.int32, shape, 0)
    first_side = lane < half
    z_cell = jnp.where(first_side, lane, lane - half)
    z_global = depth * slab_len + z_cell - 1
    valid = (z_cell <= slab_len) & (z_global >= 0) & (z_global <= slab_len * slabs - 2)
    valid = valid & (row_y < width_y - 1)

    def joined(at_first, at_last, c):
        return jnp.where(
            first_side, roll(at_first, -c * stride, 1), roll(at_last, half - c * stride, 1)
        )

    low_x = [joined(from_left, own_last, c) for c in range(5)]
    high_x = [joined(own_first, from_right, c) for c in range(3)]
    growth = jnp.where(valid, low_x[3], 1.0)
    scale = jnp.where(valid, low_x[4] * REST_VOLUME, 0.0) * growth
    corner = {}
    for c in range(3):
        for dx, base in ((0, low_x[c]), (1, high_x[c])):
            up = roll(base, -1, 1)
            corner[(c, 0, 0, dx)] = base
            corner[(c, 0, 1, dx)] = roll(base, -1, 0)
            corner[(c, 1, 0, dx)] = up
            corner[(c, 1, 1, dx)] = roll(up, -1, 0)
    edges = {}
    for one in range(2):
        for two in range(2):
            for axis, start in ((0, (one, two, 0)), (1, (one, 0, two)), (2, (0, one, two))):
                end = tuple(a + b for a, b in zip(start, unit(axis)))
                edges[(axis, start)] = [corner[(c, *end)] - corner[(c, *start)] for c in range(3)]
    pulls = tensions(edges, growth, scale, scale * growth)
    forces = []
    for c in range(3):

        def chosen(axis, one):
            at = ((one, 0, 0), (one, 0, 1)) if axis == 1 else ((0, one, 0), (0, one, 1))
            return jnp.where(first_side, pulls[(axis, at[1])][c], pulls[(axis, at[0])][c])

        level = []
        for dz in range(2):
            both = pulls[(0, (dz, 0, 0))][c] + roll(pulls[(0, (dz, 1, 0))][c], 1, 0)
            both = jnp.where(first_side, -both, both)
            along_y = chosen(1, dz)
            level.append(both + (along_y - roll(along_y, 1, 0)))
        along_z = chosen(2, 0) + roll(chosen(2, 1), 1, 0)
        forces.append((level[0] + along_z) + roll(level[1] - along_z, 1, 1))
    return forces


def finish_kernel(
    dims,
    arrived,
    before,
    near,
    own_columns,
    disp,
    table,
    separation,
    slots,
    count,
    new_velocity,
    new_disp,
    far,
    unfold,
    pushes,
):
    slab_len, width_y, patch_len, regions, slabs, pairs = dims
    half = patch_len // 2
    patches = slab_len * width_y
    block = min(pairs, 16)

    def fetch(k):
        place = table[0, k]
        for c in range(3):
            far[c, pl.ds(k, 1), :] = arrived[place, c : c + 1, :] + separation[0, c, 0, k]

    if pairs <= 16:
        for k in range(pairs):
            fetch(k)
    else:

        def fetch_one(k, carry):
            fetch(k)
            return carry

        lax.fori_loop(0, pairs, fetch_one, 0)

    live_slots = count[0, 0]
    along = lane_of((block, patch_len)).astype(jnp.float32)
    slot_row = lax.broadcasted_iota(jnp.int32, (block, patch_len), 0)

    def contact(start):
        rows = pl.ds(start, block)
        mine = [near[c, rows, :] for c in range(3)]
        mine[0] = mine[0] + along
        theirs = [far[c, rows, :] for c in range(3)]
        theirs[0] = theirs[0] + along
        inner = 8

        def some(step, carry):
            other, total = carry
            total = list(total)
            for t in range(inner):
                delta = [mine[c] - roll(other[c], t, 1) for c in range(3)]
                square = delta[0] * delta[0] + delta[1] * delta[1] + delta[2] * delta[2]
                weight = jnp.exp(-square)
                for c in range(3):
                    total[c] = total[c] + delta[c] * weight
            return tuple(roll(value, inner, 1) for value in other), tuple(total)

        zero = jnp.zeros((block, patch_len), jnp.float32)
        _, total = lax.fori_loop(
            0, patch_len // inner, some, (tuple(theirs), (zero, zero, zero))
        )
        live = (slot_row + start) < live_slots
        for c in range(3):
            pushes[c, rows, :] = jnp.where(live, total[c], 0.0)

    if pairs <= 16:
        contact(0)
    else:

        def contact_one(step, carry):
            contact(pl.multiple_of(step * block, block))
            return carry

        lax.fori_loop(0, pairs // block, contact_one, 0)

    borders = border_forces(dims, arrived, own_columns, unfold)

    patch_row = lax.broadcasted_iota(jnp.int32, (patches, pairs), 0)
    selector = (patch_row == slots[0, 0]).astype(jnp.float32)
    lane = lane_of((width_y, patch_len))
    for c in range(3):
        push = lax.dot(
            selector,
            pushes[c],
            precision=lax.Precision.HIGHEST,
            preferred_element_type=jnp.float32,
        )
        for z in range(slab_len):
            force = push[z * width_y : (z + 1) * width_y, :]
            edge = borders[c]
            force = force + jnp.where(lane == 0, roll(edge, -(z + 1), 1), 0.0)
            last = patch_len - 1
            force = force + jnp.where(lane == last, roll(edge, last - (half + z + 1), 1), 0.0)
            speed = before[z, c] + STEP_TIME * force
            new_velocity[z, c] = speed
            new_disp[z, c] = disp[z, c] + STEP_TIME * speed


def local(displacement, velocity, growth, shear_modulus, pair_slots, pair_count, separation):
    slab_len, width_y, _, patch_len = displacement.shape
    regions = lax.axis_size("region")
    slabs = lax.axis_size("depth")
    pairs = pair_slots.shape[3]
    dims = (slab_len, width_y, patch_len, regions, slabs, pairs)
    f32 = jnp.float32
    disp = jnp.transpose(displacement, (0, 2, 1, 3))
    speed = jnp.transpose(velocity, (0, 2, 1, 3))
    slots = jnp.transpose(pair_slots, (0, 2, 1, 3))
    apart = jnp.transpose(separation, (0, 2, 1, 3))

    packet, z_up, z_down, table = pl.pallas_call(
        functools.partial(pack_kernel, dims),
        out_shape=(
            jax.ShapeDtypeStruct((regions * slabs * CAP, ROWS, patch_len), f32),
            jax.ShapeDtypeStruct((5, width_y, patch_len), f32),
            jax.ShapeDtypeStruct((3, width_y, patch_len), f32),
            jax.ShapeDtypeStruct((1, pairs), jnp.int32),
        ),
        in_specs=[VMEM, VMEM, VMEM, SMEM, SMEM],
        out_specs=(VMEM, VMEM, VMEM, SMEM),
        scratch_shapes=[pltpu.VMEM((2, width_y, patch_len), f32)],
        name="pack",
    )(disp, growth, shear_modulus, slots, pair_count)

    arrived = lax.all_to_all(packet, ("region", "depth"), 0, 0, tiled=True)
    below = lax.ppermute(z_up, "depth", [(i, i + 1) for i in range(slabs - 1)])
    above = lax.ppermute(z_down, "depth", [(i + 1, i) for i in range(slabs - 1)])

    plane = (width_y, patch_len)
    before, near, own_columns = pl.pallas_call(
        functools.partial(inner_kernel, dims),
        out_shape=(
            jax.ShapeDtypeStruct((slab_len, 3, *plane), f32),
            jax.ShapeDtypeStruct((3, pairs, patch_len), f32),
            jax.ShapeDtypeStruct((2, *plane), f32),
        ),
        in_specs=[VMEM] * 6 + [SMEM],
        out_specs=(VMEM, VMEM, VMEM),
        name="inner",
        cost_estimate=pl.CostEstimate(flops=6000 * 1024, bytes_accessed=1 << 20, transcendentals=0),
    )(disp, growth, shear_modulus, speed, below, above, slots)

    new_velocity, new_disp = pl.pallas_call(
        functools.partial(finish_kernel, dims),
        out_shape=(
            jax.ShapeDtypeStruct((slab_len, 3, *plane), f32),
            jax.ShapeDtypeStruct((slab_len, 3, *plane), f32),
        ),
        in_specs=[VMEM] * 5 + [SMEM, SMEM, VMEM, SMEM],
        out_specs=(VMEM, VMEM),
        scratch_shapes=[
            pltpu.VMEM((3, pairs, patch_len), f32),
            pltpu.VMEM((2, *plane), f32),
            pltpu.VMEM((3, pairs, patch_len), f32),
        ],
        name="finish",
    )(arrived, before, near, own_columns, disp, table, apart, slots, pair_count)
    order = (0, 2, 1, 3)
    return jnp.transpose(new_velocity, order), jnp.transpose(new_disp, order)


def solution(mesh):
    in_specs = (
        P("depth", None, None, "region"),
        P("depth", None, None, "region"),
        P("depth", None, "region"),
        P("depth", None, "region"),
        P("depth", "region", None, None),
        P("depth", "region"),
        P("depth", "region", None, None),
    )
    out_specs = (P("depth", None, None, "region"), P("depth", None, None, "region"))
    return jax.shard_map(local, mesh=mesh, in_specs=in_specs, out_specs=out_specs, check_vma=False)
```

```python
import functools
import math

import jax
import jax.numpy as jnp
from jax import lax
from jax.experimental import pallas as pl
from jax.experimental.pallas import tpu as pltpu
from jax.sharding import PartitionSpec as P

CAP = 4
STEP_TIME = 0.2
REST_VOLUME = 1.0 / 6.0
PERMUTATIONS = ((0, 1, 2), (0, 2, 1), (1, 0, 2), (1, 2, 0), (2, 0, 1), (2, 1, 0))
ROWS = 4

VMEM = pl.BlockSpec(memory_space=pltpu.VMEM)
SMEM = pl.BlockSpec(memory_space=pltpu.SMEM)
HBM = pl.BlockSpec(memory_space=pltpu.HBM)
PARAMS = pltpu.CompilerParams(vmem_limit_bytes=16 << 20)
UNROLL = 32
ROOT = math.sqrt(math.log2(math.e))


def add(total, term):
    return term if total is None else total + term


def unit(axis):
    return tuple(1 if position == 2 - axis else 0 for position in range(3))


def tensions(edges, growth, scale_side, scale_up):
    inverse = 1.0 / growth
    columns = {}
    for (axis, start), rows in edges.items():
        made = []
        for row in range(3):
            value = rows[row] + 1.0 if row == axis else rows[row]
            made.append(value * inverse if axis < 2 else value)
        columns[(axis, start)] = made
    pulls = {}
    for first, second, third in PERMUTATIONS:
        middle = unit(first)
        upper = tuple(a + b for a, b in zip(middle, unit(second)))
        keys = {first: (first, (0, 0, 0)), second: (second, middle), third: (third, upper)}
        fe = [[columns[keys[col]][row] for col in range(3)] for row in range(3)]
        cof = [
            [
                fe[(row + 1) % 3][(col + 1) % 3] * fe[(row + 2) % 3][(col + 2) % 3]
                - fe[(row + 1) % 3][(col + 2) % 3] * fe[(row + 2) % 3][(col + 1) % 3]
                for col in range(3)
            ]
            for row in range(3)
        ]
        jacobian = fe[0][0] * cof[0][0] + fe[0][1] * cof[0][1] + fe[0][2] * cof[0][2]
        pressure = 4.0 * jacobian - 5.0
        for col in range(3):
            key = keys[col]
            for row in range(3):
                pulls.setdefault(key, [None] * 3)
                pulls[key][row] = add(pulls[key][row], fe[row][col] + pressure * cof[row][col])
    return {
        key: [value * (scale_side if key[0] < 2 else scale_up) for value in rows]
        for key, rows in pulls.items()
    }


def roll(value, shift, axis):
    size = value.shape[axis]
    shift = shift % size
    return value if shift == 0 else pltpu.roll(value, shift, axis)


def lane_of(shape):
    return lax.broadcasted_iota(jnp.int32, shape, len(shape) - 1)


def column_pack(fields, lane_from, stride, offset):
    shape = fields[0][0].shape
    lane = lane_of(shape)
    packed = jnp.zeros(shape, jnp.float32)
    for c, layers in enumerate(fields):
        for z, field in enumerate(layers):
            to = c * stride + z + offset
            packed = jnp.where(lane == to, roll(field, to - lane_from, 1), packed)
    return packed


def each(count, body, unrolled):
    if count <= unrolled:
        for index in range(count):
            body(index)
    else:

        def one(index, carry):
            body(index)
            return carry

        lax.fori_loop(0, count, one, 0)


def pack_kernel(
    dims,
    disp_in,
    growth_in,
    shear_in,
    slots_in,
    packet,
    face_a,
    face_b,
    disp,
    growth,
    shear,
    slots,
    counted,
    face,
    sems,
):
    slab_len, width_y, patch_len, regions, slabs, pairs = dims
    region = lax.axis_index("region")
    depth = lax.axis_index("depth")
    stride = slab_len + 2
    moves = [
        pltpu.make_async_copy(source, target, sems.at[index])
        for index, (source, target) in enumerate(
            ((slots_in, slots), (disp_in, disp), (growth_in, growth), (shear_in, shear))
        )
    ]
    for move in moves:
        move.start()
    tall = CAP * ROWS
    blank = jnp.zeros((tall, patch_len), jnp.float32)

    def base_of(m, slab):
        return pl.multiple_of((m * slabs + slab) * tall, tall)

    def clear(m):
        counted[m] = 0
        packet[pl.ds(base_of(m, depth), tall), :] = blank

    each(regions, clear, 16)
    moves[0].wait()
    moves[1].wait()

    def place(k):
        own, other = slots[0, 0, 0, k], slots[0, 1, 0, k]
        position = counted[other]
        counted[other] = position + 1
        fits = position < CAP
        base = (jnp.where(fits, other, region) * slabs + depth) * tall
        base = base + jnp.where(fits, position, 0) * ROWS
        z, y = own // width_y, own % width_y
        for c in range(3):
            packet[pl.ds(base + c, 1), :] = disp[z, c, pl.ds(y, 1), :]
        label = jnp.full((1, patch_len), own, jnp.int32).astype(jnp.float32)
        packet[pl.ds(base + 3, 1), :] = label

    each(pairs, place, 16)
    moves[2].wait()
    moves[3].wait()

    even = lax.rem(depth, 2) == 0
    last = slab_len - 1
    for out, from_z in ((face_a, jnp.where(even, last, 0)), (face_b, jnp.where(even, 0, last))):
        out[0:3] = disp[from_z]
        out[3] = growth[last]
        out[4] = shear[last]

    groups = width_y // CAP
    width = patch_len // groups
    fields = [[disp[z, c] for z in range(slab_len)] for c in range(3)]
    fields = fields + [[growth[z] for z in range(slab_len)], [shear[z] for z in range(slab_len)]]
    sides = ((patch_len - 1, fields, 1), (0, fields[:3], regions - 1))
    lane = lane_of((CAP, patch_len))
    for side, (lane_from, chosen, step) in enumerate(sides):
        face[side] = column_pack(chosen, lane_from, stride, 1)
        folded = jnp.zeros((CAP, patch_len), jnp.float32)
        for g in range(groups):
            part = roll(face[side, g * CAP : (g + 1) * CAP, :], g * width, 1)
            folded = jnp.where((lane >= g * width) & (lane < (g + 1) * width), part, folded)
        other = lax.rem(region + step, regions)
        for s in range(slabs):
            rows = pl.ds(base_of(other, s) + 3, CAP, stride=ROWS)
            packet[rows, :] = jnp.where(lane < patch_len - 1, folded, packet[rows, :])


def inner_kernel(
    dims,
    disp,
    growth,
    shear,
    velocity,
    face_a,
    face_b,
    slots,
    slot_row,
    count,
    separation,
    before,
    near,
    own_columns,
    selector,
):
    slab_len, width_y, patch_len, regions, slabs, pairs = dims
    depth = lax.axis_index("depth")
    shape = (width_y, patch_len)
    lane = lane_of(shape)
    row_y = lax.broadcasted_iota(jnp.int32, shape, 0)
    inside = (lane < patch_len - 1) & (row_y < width_y - 1)
    even = lax.rem(depth, 2) == 0
    below = [jnp.where(even, face_b[c], face_a[c]) for c in range(5)]
    above = [jnp.where(even, face_a[c], face_b[c]) for c in range(3)]
    nodes = [below[0:3]]
    nodes += [[disp[z, c] for c in range(3)] for z in range(slab_len)]
    nodes += [above]
    has_below = depth > 0
    has_above = depth < slabs - 1
    cell_growth = [jnp.where(has_below, below[3], 1.0)] + [growth[z] for z in range(slab_len)]
    cell_shear = [below[4]] + [shear[z] for z in range(slab_len)]

    own_columns[0] = column_pack(
        [[nodes[z][c] for z in range(slab_len + 2)] for c in range(3)]
        + [cell_growth, cell_shear],
        patch_len - 1,
        slab_len + 2,
        0,
    )
    own_columns[1] = column_pack(
        [[nodes[z][c] for z in range(slab_len + 2)] for c in range(3)], 0, slab_len + 2, 0
    )

    axis_x, axis_y, axis_z = 0, 1, 2
    pull_x = [[None] * 3 for _ in range(slab_len + 2)]
    pull_y = [[None] * 3 for _ in range(slab_len + 2)]
    pull_z = [[None] * 3 for _ in range(slab_len + 2)]

    def layer_edges(layer):
        along_x, along_y, moved = {}, {}, {}
        for c in range(3):
            base = layer[c]
            next_x = roll(base, -1, 1)
            next_y = roll(base, -1, 0)
            next_xy = roll(next_y, -1, 1)
            moved[c] = {(0, 0): base, (0, 1): next_x, (1, 0): next_y, (1, 1): next_xy}
            along_x[c] = {0: next_x - base, 1: next_xy - next_y}
            along_y[c] = {0: next_y - base, 1: next_xy - next_x}
        return along_x, along_y, moved

    low = layer_edges(nodes[0])
    for zc in range(slab_len + 1):
        high = layer_edges(nodes[zc + 1])
        edges = {}
        for dz, (along_x, along_y, _) in enumerate((low, high)):
            for other in range(2):
                edges[(axis_x, (dz, other, 0))] = [along_x[c][other] for c in range(3)]
                edges[(axis_y, (dz, 0, other))] = [along_y[c][other] for c in range(3)]
        for dy in range(2):
            for dx in range(2):
                edges[(axis_z, (0, dy, dx))] = [
                    high[2][c][(dy, dx)] - low[2][c][(dy, dx)] for c in range(3)
                ]
        growth_here = cell_growth[zc]
        valid = inside
        if zc == 0:
            valid = valid & has_below
        if zc == slab_len:
            valid = valid & has_above
        scale = jnp.where(valid, cell_shear[zc] * REST_VOLUME, 0.0) * growth_here
        pulls = tensions(edges, growth_here, scale, scale * growth_here)
        for c in range(3):
            for dz in range(2):
                near_row = pulls[(axis_x, (dz, 0, 0))][c]
                far_row = pulls[(axis_x, (dz, 1, 0))][c]
                pull_x[zc + dz][c] = add(pull_x[zc + dz][c], near_row + roll(far_row, 1, 0))
                near_row = pulls[(axis_y, (dz, 0, 0))][c]
                far_row = pulls[(axis_y, (dz, 0, 1))][c]
                pull_y[zc + dz][c] = add(pull_y[zc + dz][c], near_row + roll(far_row, 1, 1))
            at_zero = pulls[(axis_z, (0, 0, 0))][c] + roll(pulls[(axis_z, (0, 1, 0))][c], 1, 0)
            at_one = pulls[(axis_z, (0, 0, 1))][c] + roll(pulls[(axis_z, (0, 1, 1))][c], 1, 0)
            pull_z[zc][c] = at_zero + roll(at_one, 1, 1)
        low = high
        if zc > 0:
            for c in range(3):
                force = pull_x[zc][c] - roll(pull_x[zc][c], 1, 1)
                force = force + (pull_y[zc][c] - roll(pull_y[zc][c], 1, 0))
                force = force + (pull_z[zc][c] - pull_z[zc - 1][c])
                before[zc - 1, c] = velocity[zc - 1, c] + STEP_TIME * force

    along = lane_of((1, patch_len)).astype(jnp.float32)

    def fetch(k):
        own = slots[0, 0, 0, k]
        z, y = own // width_y, own % width_y
        for c in range(3):
            point = disp[z, c, pl.ds(y, 1), :]
            if c == 0:
                point = point + along
            near[c, pl.ds(k, 1), :] = (point - separation[0, c, 0, k]) * ROOT

    each(pairs, fetch, 16)
    patch_row = lax.broadcasted_iota(jnp.int32, selector.shape, 0)
    live = lax.broadcasted_iota(jnp.int32, selector.shape, 1) < count[0, 0]
    selector[...] = jnp.where((patch_row == slot_row[0, 0]) & live, 1.0, 0.0)


def border_forces(dims, arrived, own_columns, unfold):
    slab_len, width_y, patch_len, regions, slabs, pairs = dims
    region = lax.axis_index("region")
    depth = lax.axis_index("depth")
    stride = slab_len + 2
    groups = width_y // CAP
    width = patch_len // groups
    half = patch_len // 2
    fold_lane = lane_of((CAP, patch_len))
    fold_z = lax.rem(lax.rem(fold_lane, width), stride)
    for side, step in enumerate((regions - 1, 1)):
        other = lax.rem(region + step, regions)

        def block(slab):
            base = (other * slabs + slab) * (CAP * ROWS)
            return arrived[pl.ds(base + 3, CAP, stride=ROWS), :]

        merged = block(depth)
        lower = block(lax.rem(depth + slabs - 1, slabs))
        upper = block(lax.rem(depth + 1, slabs))
        merged = jnp.where(fold_z == 0, roll(lower, -slab_len, 1), merged)
        merged = jnp.where(fold_z == slab_len + 1, roll(upper, slab_len, 1), merged)
        for g in range(groups):
            unfold[side, g * CAP : (g + 1) * CAP, :] = roll(merged, -g * width, 1)
    from_left = unfold[0]
    from_right = unfold[1]
    own_last = own_columns[0]
    own_first = own_columns[1]
    shape = (width_y, patch_len)
    lane = lane_of(shape)
    row_y = lax.broadcasted_iota(jnp.int32, shape, 0)
    first_side = lane < half
    z_cell = jnp.where(first_side, lane, lane - half)
    z_global = depth * slab_len + z_cell - 1
    valid = (z_cell <= slab_len) & (z_global >= 0) & (z_global <= slab_len * slabs - 2)
    valid = valid & (row_y < width_y - 1)

    def joined(at_first, at_last, c):
        return jnp.where(
            first_side, roll(at_first, -c * stride, 1), roll(at_last, half - c * stride, 1)
        )

    low_x = [joined(from_left, own_last, c) for c in range(5)]
    high_x = [joined(own_first, from_right, c) for c in range(3)]
    growth = jnp.where(valid, low_x[3], 1.0)
    scale = jnp.where(valid, low_x[4] * REST_VOLUME, 0.0) * growth
    corner = {}
    for c in range(3):
        for dx, base in ((0, low_x[c]), (1, high_x[c])):
            up = roll(base, -1, 1)
            corner[(c, 0, 0, dx)] = base
            corner[(c, 0, 1, dx)] = roll(base, -1, 0)
            corner[(c, 1, 0, dx)] = up
            corner[(c, 1, 1, dx)] = roll(up, -1, 0)
    edges = {}
    for one in range(2):
        for two in range(2):
            for axis, start in ((0, (one, two, 0)), (1, (one, 0, two)), (2, (0, one, two))):
                end = tuple(a + b for a, b in zip(start, unit(axis)))
                edges[(axis, start)] = [corner[(c, *end)] - corner[(c, *start)] for c in range(3)]
    pulls = tensions(edges, growth, scale, scale * growth)
    forces = []
    for c in range(3):

        def chosen(axis, one):
            at = ((one, 0, 0), (one, 0, 1)) if axis == 1 else ((0, one, 0), (0, one, 1))
            return jnp.where(first_side, pulls[(axis, at[1])][c], pulls[(axis, at[0])][c])

        level = []
        for dz in range(2):
            both = pulls[(0, (dz, 0, 0))][c] + roll(pulls[(0, (dz, 1, 0))][c], 1, 0)
            both = jnp.where(first_side, -both, both)
            along_y = chosen(1, dz)
            level.append(both + (along_y - roll(along_y, 1, 0)))
        along_z = chosen(2, 0) + roll(chosen(2, 1), 1, 0)
        forces.append((level[0] + along_z) + roll(level[1] - along_z, 1, 1))
    return forces


def finish_kernel(
    dims,
    inner,
    arrived,
    before,
    near,
    own_columns,
    disp,
    selector,
    slots,
    new_velocity,
    new_disp,
    far,
    unfold,
    pushes,
    tiles,
):
    slab_len, width_y, patch_len, regions, slabs, pairs = dims
    half = patch_len // 2
    block = min(pairs, 16)
    depth = lax.axis_index("depth")
    tall = CAP * ROWS

    def take(m):
        rows = pl.ds(pl.multiple_of((m * slabs + depth) * tall, tall), tall)
        tiles[pl.ds(pl.multiple_of(m * tall, tall), tall), :] = arrived[rows, :]

    each(regions, take, 16)

    total_tiles = regions * CAP
    wide = (total_tiles, pairs)
    label = tiles[pl.ds(3, total_tiles, stride=ROWS), :][:, patch_len - 1 :]
    label = jnp.broadcast_to(label, (total_tiles, max(pairs, patch_len)))
    tile_row = lax.broadcasted_iota(jnp.int32, label.shape, 0)
    again = tile_row < 0
    for back in range(1, CAP):
        same = (roll(label, back, 0) == label) & (lax.rem(tile_row, CAP) >= back)
        again = again | same
    label = jnp.where(again, -1.0, label)[:, 0:pairs]
    tile_row = lax.broadcasted_iota(jnp.int32, wide, 0) // CAP
    wanted = (tile_row == slots[0, 1]) & (label == slots[0, 2].astype(jnp.float32))
    chosen = jnp.where(wanted, 1.0, 0.0)
    for c in range(3):
        far[c] = lax.dot_general(
            chosen,
            tiles[pl.ds(c, total_tiles, stride=ROWS), :],
            (((0,), (0,)), ((), ())),
            precision=lax.Precision.HIGHEST,
            preferred_element_type=jnp.float32,
        )
    borders = border_forces(dims, arrived, own_columns, unfold)
    along = lane_of((block, patch_len)).astype(jnp.float32)

    def contact(start):
        rows = pl.ds(start, block)
        mine = [near[c, rows, :] for c in range(3)]
        theirs = [far[c, rows, :] for c in range(3)]
        theirs = [(theirs[0] + along) * ROOT, theirs[1] * ROOT, theirs[2] * ROOT]

        def some(step, carry):
            other, total = carry
            total = list(total)
            for t in range(inner):
                delta = [mine[c] - roll(other[c], t, 1) for c in range(3)]
                square = delta[0] * delta[0] + delta[1] * delta[1] + delta[2] * delta[2]
                weight = jnp.exp2(-square)
                for c in range(3):
                    total[c] = total[c] + delta[c] * weight
            if inner < patch_len:
                other = tuple(roll(value, inner, 1) for value in other)
            return other, tuple(total)

        zero = jnp.zeros((block, patch_len), jnp.float32)
        carry = (tuple(theirs), (zero, zero, zero))
        if inner == patch_len:
            _, total = some(0, carry)
        else:
            _, total = lax.fori_loop(0, patch_len // inner, some, carry)
        for c in range(3):
            pushes[c, rows, :] = total[c]

    each(pairs // block, lambda step: contact(step * block), 1)

    lane = lane_of((width_y, patch_len))
    for c in range(3):
        push = lax.dot(
            selector[...],
            pushes[c],
            precision=lax.Precision.HIGHEST,
            preferred_element_type=jnp.float32,
        )
        for z in range(slab_len):
            force = push[z * width_y : (z + 1) * width_y, :] * (1.0 / ROOT)
            edge = borders[c]
            force = force + jnp.where(lane == 0, roll(edge, -(z + 1), 1), 0.0)
            last = patch_len - 1
            force = force + jnp.where(lane == last, roll(edge, last - (half + z + 1), 1), 0.0)
            speed = before[z, c] + STEP_TIME * force
            new_velocity[z, c] = speed
            new_disp[z, c] = disp[z, c] + STEP_TIME * speed


def local(displacement, velocity, growth, shear_modulus, pair_slots, pair_count, separation):
    slab_len, width_y, _, patch_len = displacement.shape
    regions = lax.axis_size("region")
    slabs = lax.axis_size("depth")
    pairs = pair_slots.shape[3]
    dims = (slab_len, width_y, patch_len, regions, slabs, pairs)
    f32 = jnp.float32
    i32 = jnp.int32
    disp = jnp.transpose(displacement, (0, 2, 1, 3))
    speed = jnp.transpose(velocity, (0, 2, 1, 3))
    slots = jnp.transpose(pair_slots, (0, 2, 1, 3))
    apart = jnp.transpose(separation, (0, 2, 1, 3))
    plane = (width_y, patch_len)

    packet, face_a, face_b = pl.pallas_call(
        functools.partial(pack_kernel, dims),
        out_shape=(
            jax.ShapeDtypeStruct((regions * slabs * CAP * ROWS, patch_len), f32),
            jax.ShapeDtypeStruct((5, *plane), f32),
            jax.ShapeDtypeStruct((5, *plane), f32),
        ),
        in_specs=[HBM] * 4,
        out_specs=(VMEM, VMEM, VMEM),
        scratch_shapes=[
            pltpu.VMEM((slab_len, 3, *plane), f32),
            pltpu.VMEM((slab_len, *plane), f32),
            pltpu.VMEM((slab_len, *plane), f32),
            pltpu.SMEM(slots.shape, i32),
            pltpu.SMEM((regions,), i32),
            pltpu.VMEM((2, *plane), f32),
            pltpu.SemaphoreType.DMA((4,)),
        ],
        name="pack",
    )(disp, growth, shear_modulus, slots)

    arrived = lax.all_to_all(packet, ("region", "depth"), 0, 0, tiled=True)
    links = [[(i, i + 1) for i in range(first, slabs - 1, 2)] for first in (0, 1)]
    links = [link + [(b, a) for a, b in link] for link in links]
    face_a = lax.ppermute(face_a, "depth", links[0])
    face_b = lax.ppermute(face_b, "depth", links[1])

    face_a, pair_count = lax.optimization_barrier((face_a, pair_count))

    before, near, own_columns, selector = pl.pallas_call(
        functools.partial(inner_kernel, dims),
        out_shape=(
            jax.ShapeDtypeStruct((slab_len, 3, *plane), f32),
            jax.ShapeDtypeStruct((3, pairs, patch_len), f32),
            jax.ShapeDtypeStruct((2, *plane), f32),
            jax.ShapeDtypeStruct((slab_len * width_y, pairs), f32),
        ),
        in_specs=[VMEM] * 6 + [SMEM, VMEM, SMEM, SMEM],
        out_specs=(VMEM,) * 4,
        compiler_params=PARAMS,
        name="inner",
        cost_estimate=pl.CostEstimate(flops=6000 * 1024, bytes_accessed=1 << 20, transcendentals=0),
    )(disp, growth, shear_modulus, speed, face_a, face_b, slots, slots, pair_count, apart)

    new_velocity, new_disp = pl.pallas_call(
        functools.partial(finish_kernel, dims, UNROLL if pairs <= 16 else 8),
        out_shape=(
            jax.ShapeDtypeStruct((slab_len, 3, *plane), f32),
            jax.ShapeDtypeStruct((slab_len, 3, *plane), f32),
        ),
        in_specs=[VMEM] * 7,
        out_specs=(VMEM, VMEM),
        scratch_shapes=[
            pltpu.VMEM((3, pairs, patch_len), f32),
            pltpu.VMEM((2, *plane), f32),
            pltpu.VMEM((3, pairs, patch_len), f32),
            pltpu.VMEM((regions * CAP * ROWS, patch_len), f32),
        ],
        compiler_params=PARAMS,
        name="finish",
    )(arrived, before, near, own_columns, disp, selector, slots)
    order = (0, 2, 1, 3)
    return jnp.transpose(new_velocity, order), jnp.transpose(new_disp, order)


def solution(mesh):
    in_specs = (
        P("depth", None, None, "region"),
        P("depth", None, None, "region"),
        P("depth", None, "region"),
        P("depth", None, "region"),
        P("depth", "region", None, None),
        P("depth", "region"),
        P("depth", "region", None, None),
    )
    out_specs = (P("depth", None, None, "region"), P("depth", None, None, "region"))
    return jax.shard_map(local, mesh=mesh, in_specs=in_specs, out_specs=out_specs, check_vma=False)
```

```python
import functools
import math

import jax
import jax.numpy as jnp
from jax import lax
from jax.experimental import pallas as pl
from jax.experimental.pallas import tpu as pltpu
from jax.sharding import Mesh
from jax.sharding import PartitionSpec as P

CAP = 4
STEP_TIME = 0.2
REST_VOLUME = 1.0 / 6.0
PERMUTATIONS = ((0, 1, 2), (0, 2, 1), (1, 0, 2), (1, 2, 0), (2, 0, 1), (2, 1, 0))
ROWS = 4

VMEM = pl.BlockSpec(memory_space=pltpu.VMEM)
SMEM = pl.BlockSpec(memory_space=pltpu.SMEM)
HBM = pl.BlockSpec(memory_space=pltpu.HBM)
PARAMS = pltpu.CompilerParams(vmem_limit_bytes=16 << 20)
UNROLL = 128
ROOT = math.sqrt(math.log2(math.e))


def add(total, term):
    return term if total is None else total + term


def unit(axis):
    return tuple(1 if position == 2 - axis else 0 for position in range(3))


def tensions(edges, growth, scale_side, scale_up):
    inverse = 1.0 / growth
    columns = {}
    for (axis, start), rows in edges.items():
        made = []
        for row in range(3):
            value = rows[row] + 1.0 if row == axis else rows[row]
            made.append(value * inverse if axis < 2 else value)
        columns[(axis, start)] = made
    pulls = {}
    for first, second, third in PERMUTATIONS:
        middle = unit(first)
        upper = tuple(a + b for a, b in zip(middle, unit(second)))
        keys = {first: (first, (0, 0, 0)), second: (second, middle), third: (third, upper)}
        fe = [[columns[keys[col]][row] for col in range(3)] for row in range(3)]
        cof = [
            [
                fe[(row + 1) % 3][(col + 1) % 3] * fe[(row + 2) % 3][(col + 2) % 3]
                - fe[(row + 1) % 3][(col + 2) % 3] * fe[(row + 2) % 3][(col + 1) % 3]
                for col in range(3)
            ]
            for row in range(3)
        ]
        jacobian = fe[0][0] * cof[0][0] + fe[0][1] * cof[0][1] + fe[0][2] * cof[0][2]
        pressure = 4.0 * jacobian - 5.0
        for col in range(3):
            key = keys[col]
            for row in range(3):
                pulls.setdefault(key, [None] * 3)
                pulls[key][row] = add(pulls[key][row], fe[row][col] + pressure * cof[row][col])
    return {
        key: [value * (scale_side if key[0] < 2 else scale_up) for value in rows]
        for key, rows in pulls.items()
    }


def roll(value, shift, axis):
    size = value.shape[axis]
    shift = shift % size
    return value if shift == 0 else pltpu.roll(value, shift, axis)


def lane_of(shape):
    return lax.broadcasted_iota(jnp.int32, shape, len(shape) - 1)


def column_pack(fields, lane_from, stride, offset):
    shape = fields[0][0].shape
    lane = lane_of(shape)
    packed = jnp.zeros(shape, jnp.float32)
    for c, layers in enumerate(fields):
        for z, field in enumerate(layers):
            to = c * stride + z + offset
            packed = jnp.where(lane == to, roll(field, to - lane_from, 1), packed)
    return packed


def each(count, body, unrolled):
    if count <= unrolled:
        for index in range(count):
            body(index)
    else:

        def one(index, carry):
            body(index)
            return carry

        lax.fori_loop(0, count, one, 0)


def slab_index():
    return lax.axis_index("pair") * lax.axis_size("core") + lax.axis_index("core")


def pack_kernel(
    dims,
    disp_in,
    growth_in,
    shear_in,
    slots_in,
    packet,
    face_a,
    face_b,
    disp,
    growth,
    shear,
    slots,
    counted,
    face,
    sems,
):
    slab_len, width_y, patch_len, regions, slabs, pairs = dims
    region = lax.axis_index("region")
    depth = slab_index()
    pair = lax.axis_index("pair")
    blocks = slabs // 2
    stride = slab_len + 2
    moves = [
        pltpu.make_async_copy(source, target, sems.at[index])
        for index, (source, target) in enumerate(
            ((slots_in, slots), (disp_in, disp), (growth_in, growth), (shear_in, shear))
        )
    ]
    for move in moves:
        move.start()
    tall = CAP * ROWS
    blank = jnp.zeros((tall, patch_len), jnp.float32)

    def base_of(m, block):
        return pl.multiple_of((m * blocks + block) * tall, tall)

    def clear(m):
        counted[m] = 0
        packet[pl.ds(base_of(m, pair), tall), :] = blank

    each(regions, clear, 16)
    for move in moves:
        move.wait()

    def place(k):
        own, other = slots[0, 0, 0, k], slots[0, 1, 0, k]
        position = counted[other]
        counted[other] = position + 1
        fits = position < CAP
        base = (jnp.where(fits, other, region) * blocks + pair) * tall
        base = base + jnp.where(fits, position, 0) * ROWS
        z, y = own // width_y, own % width_y
        for c in range(3):
            packet[pl.ds(base + c, 1), :] = disp[z, c, pl.ds(y, 1), :]
        label = jnp.full((1, patch_len), own, jnp.int32).astype(jnp.float32)
        packet[pl.ds(base + 3, 1), :] = label

    each(pairs, place, 16)

    even = lax.rem(depth, 2) == 0
    last = slab_len - 1
    for out, from_z in ((face_a, jnp.where(even, last, 0)), (face_b, jnp.where(even, 0, last))):
        out[0:3] = disp[from_z]
        out[3] = growth[last]
        out[4] = shear[last]

    groups = width_y // CAP
    width = patch_len // groups
    fields = [[disp[z, c] for z in range(slab_len)] for c in range(3)]
    fields = fields + [[growth[z] for z in range(slab_len)], [shear[z] for z in range(slab_len)]]
    sides = ((patch_len - 1, fields, 1), (0, fields[:3], regions - 1))
    lane = lane_of((CAP, patch_len))
    for side, (lane_from, chosen, step) in enumerate(sides):
        face[side] = column_pack(chosen, lane_from, stride, 1)
        folded = jnp.zeros((CAP, patch_len), jnp.float32)
        for g in range(groups):
            part = roll(face[side, g * CAP : (g + 1) * CAP, :], g * width, 1)
            folded = jnp.where((lane >= g * width) & (lane < (g + 1) * width), part, folded)
        other = lax.rem(region + step, regions)
        for block in range(blocks):
            rows = pl.ds(base_of(other, block) + 3, CAP, stride=ROWS)
            packet[rows, :] = jnp.where(lane < patch_len - 1, folded, packet[rows, :])


def inner_kernel(
    dims,
    disp,
    growth,
    shear,
    velocity,
    face_a,
    face_b,
    slots,
    slot_row,
    count,
    separation,
    before,
    near,
    own_columns,
    selector,
):
    slab_len, width_y, patch_len, regions, slabs, pairs = dims
    depth = slab_index()
    shape = (width_y, patch_len)
    lane = lane_of(shape)
    row_y = lax.broadcasted_iota(jnp.int32, shape, 0)
    inside = (lane < patch_len - 1) & (row_y < width_y - 1)
    even = lax.rem(depth, 2) == 0
    below = [jnp.where(even, face_b[c], face_a[c]) for c in range(5)]
    above = [jnp.where(even, face_a[c], face_b[c]) for c in range(3)]
    nodes = [below[0:3]]
    nodes += [[disp[z, c] for c in range(3)] for z in range(slab_len)]
    nodes += [above]
    has_below = depth > 0
    has_above = depth < slabs - 1
    cell_growth = [jnp.where(has_below, below[3], 1.0)] + [growth[z] for z in range(slab_len)]
    cell_shear = [below[4]] + [shear[z] for z in range(slab_len)]

    own_columns[0] = column_pack(
        [[nodes[z][c] for z in range(slab_len + 2)] for c in range(3)]
        + [cell_growth, cell_shear],
        patch_len - 1,
        slab_len + 2,
        0,
    )
    own_columns[1] = column_pack(
        [[nodes[z][c] for z in range(slab_len + 2)] for c in range(3)], 0, slab_len + 2, 0
    )

    axis_x, axis_y, axis_z = 0, 1, 2
    pull_x = [[None] * 3 for _ in range(slab_len + 2)]
    pull_y = [[None] * 3 for _ in range(slab_len + 2)]
    pull_z = [[None] * 3 for _ in range(slab_len + 2)]

    def layer_edges(layer):
        along_x, along_y, moved = {}, {}, {}
        for c in range(3):
            base = layer[c]
            next_x = roll(base, -1, 1)
            next_y = roll(base, -1, 0)
            next_xy = roll(next_y, -1, 1)
            moved[c] = {(0, 0): base, (0, 1): next_x, (1, 0): next_y, (1, 1): next_xy}
            along_x[c] = {0: next_x - base, 1: next_xy - next_y}
            along_y[c] = {0: next_y - base, 1: next_xy - next_x}
        return along_x, along_y, moved

    low = layer_edges(nodes[0])
    for zc in range(slab_len + 1):
        high = layer_edges(nodes[zc + 1])
        edges = {}
        for dz, (along_x, along_y, _) in enumerate((low, high)):
            for other in range(2):
                edges[(axis_x, (dz, other, 0))] = [along_x[c][other] for c in range(3)]
                edges[(axis_y, (dz, 0, other))] = [along_y[c][other] for c in range(3)]
        for dy in range(2):
            for dx in range(2):
                edges[(axis_z, (0, dy, dx))] = [
                    high[2][c][(dy, dx)] - low[2][c][(dy, dx)] for c in range(3)
                ]
        growth_here = cell_growth[zc]
        valid = inside
        if zc == 0:
            valid = valid & has_below
        if zc == slab_len:
            valid = valid & has_above
        scale = jnp.where(valid, cell_shear[zc] * REST_VOLUME, 0.0) * growth_here
        pulls = tensions(edges, growth_here, scale, scale * growth_here)
        for c in range(3):
            for dz in range(2):
                near_row = pulls[(axis_x, (dz, 0, 0))][c]
                far_row = pulls[(axis_x, (dz, 1, 0))][c]
                pull_x[zc + dz][c] = add(pull_x[zc + dz][c], near_row + roll(far_row, 1, 0))
                near_row = pulls[(axis_y, (dz, 0, 0))][c]
                far_row = pulls[(axis_y, (dz, 0, 1))][c]
                pull_y[zc + dz][c] = add(pull_y[zc + dz][c], near_row + roll(far_row, 1, 1))
            at_zero = pulls[(axis_z, (0, 0, 0))][c] + roll(pulls[(axis_z, (0, 1, 0))][c], 1, 0)
            at_one = pulls[(axis_z, (0, 0, 1))][c] + roll(pulls[(axis_z, (0, 1, 1))][c], 1, 0)
            pull_z[zc][c] = at_zero + roll(at_one, 1, 1)
        low = high
        if zc > 0:
            for c in range(3):
                force = pull_x[zc][c] - roll(pull_x[zc][c], 1, 1)
                force = force + (pull_y[zc][c] - roll(pull_y[zc][c], 1, 0))
                force = force + (pull_z[zc][c] - pull_z[zc - 1][c])
                before[zc - 1, c] = velocity[zc - 1, c] + STEP_TIME * force

    along = lane_of((1, patch_len)).astype(jnp.float32)

    def fetch(k):
        own = slots[0, 0, 0, k]
        z, y = own // width_y, own % width_y
        for c in range(3):
            point = disp[z, c, pl.ds(y, 1), :]
            if c == 0:
                point = point + along
            near[c, pl.ds(k, 1), :] = (point - separation[0, c, 0, k]) * ROOT

    each(pairs, fetch, 16)
    patch_row = lax.broadcasted_iota(jnp.int32, selector.shape, 0)
    live = lax.broadcasted_iota(jnp.int32, selector.shape, 1) < count[0, 0]
    selector[...] = jnp.where((patch_row == slot_row[0, 0]) & live, 1.0, 0.0)


def border_forces(dims, arrived, relayed, own_columns, unfold):
    slab_len, width_y, patch_len, regions, slabs, pairs = dims
    region = lax.axis_index("region")
    depth = slab_index()
    pair = lax.axis_index("pair")
    core = lax.axis_index("core")
    blocks = slabs // 2
    stride = slab_len + 2
    groups = width_y // CAP
    width = patch_len // groups
    half = patch_len // 2
    fold_lane = lane_of((CAP, patch_len))
    fold_z = lax.rem(lax.rem(fold_lane, width), stride)
    for side, step in enumerate((regions - 1, 1)):
        other = lax.rem(region + step, regions)

        def columns(source, block):
            base = (other * blocks + lax.rem(block + blocks, blocks)) * (CAP * ROWS)
            return source[pl.ds(base + 3, CAP, stride=ROWS), :]

        merged = columns(arrived, pair)
        lower = columns(relayed, pair - 1 + core)
        upper = columns(relayed, pair + core)
        merged = jnp.where(fold_z == 0, roll(lower, -slab_len, 1), merged)
        merged = jnp.where(fold_z == slab_len + 1, roll(upper, slab_len, 1), merged)
        for g in range(groups):
            unfold[side, g * CAP : (g + 1) * CAP, :] = roll(merged, -g * width, 1)
    from_left = unfold[0]
    from_right = unfold[1]
    own_last = own_columns[0]
    own_first = own_columns[1]
    shape = (width_y, patch_len)
    lane = lane_of(shape)
    row_y = lax.broadcasted_iota(jnp.int32, shape, 0)
    first_side = lane < half
    z_cell = jnp.where(first_side, lane, lane - half)
    z_global = depth * slab_len + z_cell - 1
    valid = (z_cell <= slab_len) & (z_global >= 0) & (z_global <= slab_len * slabs - 2)
    valid = valid & (row_y < width_y - 1)

    def joined(at_first, at_last, c):
        return jnp.where(
            first_side, roll(at_first, -c * stride, 1), roll(at_last, half - c * stride, 1)
        )

    low_x = [joined(from_left, own_last, c) for c in range(5)]
    high_x = [joined(own_first, from_right, c) for c in range(3)]
    growth = jnp.where(valid, low_x[3], 1.0)
    scale = jnp.where(valid, low_x[4] * REST_VOLUME, 0.0) * growth
    corner = {}
    for c in range(3):
        for dx, base in ((0, low_x[c]), (1, high_x[c])):
            up = roll(base, -1, 1)
            corner[(c, 0, 0, dx)] = base
            corner[(c, 0, 1, dx)] = roll(base, -1, 0)
            corner[(c, 1, 0, dx)] = up
            corner[(c, 1, 1, dx)] = roll(up, -1, 0)
    edges = {}
    for one in range(2):
        for two in range(2):
            for axis, start in ((0, (one, two, 0)), (1, (one, 0, two)), (2, (0, one, two))):
                end = tuple(a + b for a, b in zip(start, unit(axis)))
                edges[(axis, start)] = [corner[(c, *end)] - corner[(c, *start)] for c in range(3)]
    pulls = tensions(edges, growth, scale, scale * growth)
    forces = []
    for c in range(3):

        def chosen(axis, one):
            at = ((one, 0, 0), (one, 0, 1)) if axis == 1 else ((0, one, 0), (0, one, 1))
            return jnp.where(first_side, pulls[(axis, at[1])][c], pulls[(axis, at[0])][c])

        level = []
        for dz in range(2):
            both = pulls[(0, (dz, 0, 0))][c] + roll(pulls[(0, (dz, 1, 0))][c], 1, 0)
            both = jnp.where(first_side, -both, both)
            along_y = chosen(1, dz)
            level.append(both + (along_y - roll(along_y, 1, 0)))
        along_z = chosen(2, 0) + roll(chosen(2, 1), 1, 0)
        forces.append((level[0] + along_z) + roll(level[1] - along_z, 1, 1))
    return forces


def contact_kernel(dims, inner, arrived, near, slots, pushes, far, tiles):
    slab_len, width_y, patch_len, regions, slabs, pairs = dims
    block = min(pairs, 16)
    pair = lax.axis_index("pair")
    blocks = slabs // 2
    tall = CAP * ROWS

    def take(m):
        rows = pl.ds(pl.multiple_of((m * blocks + pair) * tall, tall), tall)
        tiles[pl.ds(pl.multiple_of(m * tall, tall), tall), :] = arrived[rows, :]

    each(regions, take, 16)

    total_tiles = regions * CAP
    wide = (total_tiles, pairs)
    label = tiles[pl.ds(3, total_tiles, stride=ROWS), :][:, patch_len - 1 :]
    label = jnp.broadcast_to(label, (total_tiles, max(pairs, patch_len)))
    tile_row = lax.broadcasted_iota(jnp.int32, label.shape, 0)
    again = tile_row < 0
    for back in range(1, CAP):
        same = (roll(label, back, 0) == label) & (lax.rem(tile_row, CAP) >= back)
        again = again | same
    label = jnp.where(again, -1.0, label)[:, 0:pairs]
    tile_row = lax.broadcasted_iota(jnp.int32, wide, 0) // CAP
    wanted = (tile_row == slots[0, 1]) & (label == slots[0, 2].astype(jnp.float32))
    chosen = jnp.where(wanted, 1.0, 0.0)
    for c in range(3):
        far[c] = lax.dot_general(
            chosen,
            tiles[pl.ds(c, total_tiles, stride=ROWS), :],
            (((0,), (0,)), ((), ())),
            precision=lax.Precision.HIGHEST,
            preferred_element_type=jnp.float32,
        )
    along = lane_of((block, patch_len)).astype(jnp.float32)

    def contact(start):
        rows = pl.ds(start, block)
        mine = [near[c, rows, :] for c in range(3)]
        theirs = [far[c, rows, :] for c in range(3)]
        theirs = [(theirs[0] + along) * ROOT, theirs[1] * ROOT, theirs[2] * ROOT]

        def some(step, carry):
            other, total = carry
            total = list(total)
            for t in range(inner):
                delta = [mine[c] - roll(other[c], t, 1) for c in range(3)]
                square = delta[0] * delta[0] + delta[1] * delta[1] + delta[2] * delta[2]
                weight = jnp.exp2(-square)
                for c in range(3):
                    total[c] = total[c] + delta[c] * weight
            if inner < patch_len:
                other = tuple(roll(value, inner, 1) for value in other)
            return other, tuple(total)

        zero = jnp.zeros((block, patch_len), jnp.float32)
        carry = (tuple(theirs), (zero, zero, zero))
        if inner == patch_len:
            _, total = some(0, carry)
        else:
            _, total = lax.fori_loop(0, patch_len // inner, some, carry)
        for c in range(3):
            pushes[c, rows, :] = total[c]

    each(pairs // block, lambda step: contact(step * block), 1)


def finish_kernel(
    dims,
    arrived,
    relayed,
    before,
    pushes,
    own_columns,
    disp,
    selector,
    new_velocity,
    new_disp,
    unfold,
):
    slab_len, width_y, patch_len, regions, slabs, pairs = dims
    half = patch_len // 2
    borders = border_forces(dims, arrived, relayed, own_columns, unfold)
    lane = lane_of((width_y, patch_len))
    for c in range(3):
        push = lax.dot(
            selector[...],
            pushes[c],
            precision=lax.Precision.HIGHEST,
            preferred_element_type=jnp.float32,
        )
        for z in range(slab_len):
            force = push[z * width_y : (z + 1) * width_y, :] * (1.0 / ROOT)
            edge = borders[c]
            force = force + jnp.where(lane == 0, roll(edge, -(z + 1), 1), 0.0)
            last = patch_len - 1
            force = force + jnp.where(lane == last, roll(edge, last - (half + z + 1), 1), 0.0)
            speed = before[z, c] + STEP_TIME * force
            new_velocity[z, c] = speed
            new_disp[z, c] = disp[z, c] + STEP_TIME * speed


def local(displacement, velocity, growth, shear_modulus, pair_slots, pair_count, separation):
    slab_len, width_y, _, patch_len = displacement.shape
    regions = lax.axis_size("region")
    slabs = lax.axis_size("pair") * lax.axis_size("core")
    pairs = pair_slots.shape[3]
    dims = (slab_len, width_y, patch_len, regions, slabs, pairs)
    f32 = jnp.float32
    i32 = jnp.int32
    disp = jnp.transpose(displacement, (0, 2, 1, 3))
    speed = jnp.transpose(velocity, (0, 2, 1, 3))
    slots = jnp.transpose(pair_slots, (0, 2, 1, 3))
    apart = jnp.transpose(separation, (0, 2, 1, 3))
    plane = (width_y, patch_len)

    packet, face_a, face_b = pl.pallas_call(
        functools.partial(pack_kernel, dims),
        out_shape=(
            jax.ShapeDtypeStruct((regions * (slabs // 2) * CAP * ROWS, patch_len), f32),
            jax.ShapeDtypeStruct((5, *plane), f32),
            jax.ShapeDtypeStruct((5, *plane), f32),
        ),
        in_specs=[HBM] * 4,
        out_specs=(VMEM, VMEM, VMEM),
        scratch_shapes=[
            pltpu.VMEM((slab_len, 3, *plane), f32),
            pltpu.VMEM((slab_len, *plane), f32),
            pltpu.VMEM((slab_len, *plane), f32),
            pltpu.SMEM(slots.shape, i32),
            pltpu.SMEM((regions,), i32),
            pltpu.VMEM((2, *plane), f32),
            pltpu.SemaphoreType.DMA((4,)),
        ],
        name="pack",
    )(disp, growth, shear_modulus, slots)

    arrived = lax.all_to_all(packet, ("region", "pair"), 0, 0, tiled=True)
    links = [[(i, i + 1) for i in range(first, slabs - 1, 2)] for first in (0, 1)]
    links = [link + [(b, a) for a, b in link] for link in links]
    face_a = lax.ppermute(face_a, ("pair", "core"), links[0])
    face_b = lax.ppermute(face_b, ("pair", "core"), links[1])

    face_a, pair_count = lax.optimization_barrier((face_a, pair_count))

    before, near, own_columns, selector = pl.pallas_call(
        functools.partial(inner_kernel, dims),
        out_shape=(
            jax.ShapeDtypeStruct((slab_len, 3, *plane), f32),
            jax.ShapeDtypeStruct((3, pairs, patch_len), f32),
            jax.ShapeDtypeStruct((2, *plane), f32),
            jax.ShapeDtypeStruct((slab_len * width_y, pairs), f32),
        ),
        in_specs=[VMEM] * 6 + [SMEM, VMEM, SMEM, SMEM],
        out_specs=(VMEM,) * 4,
        compiler_params=PARAMS,
        name="inner",
        cost_estimate=pl.CostEstimate(flops=6000 * 1024, bytes_accessed=1 << 20, transcendentals=0),
    )(disp, growth, shear_modulus, speed, face_a, face_b, slots, slots, pair_count, apart)

    arrived, before = lax.optimization_barrier((arrived, before))
    relayed = lax.ppermute(arrived, ("pair", "core"), links[0])

    pushes = pl.pallas_call(
        functools.partial(contact_kernel, dims, UNROLL if pairs <= 16 else 8),
        out_shape=jax.ShapeDtypeStruct((3, pairs, patch_len), f32),
        in_specs=[VMEM] * 3,
        out_specs=VMEM,
        scratch_shapes=[
            pltpu.VMEM((3, pairs, patch_len), f32),
            pltpu.VMEM((regions * CAP * ROWS, patch_len), f32),
        ],
        compiler_params=PARAMS,
        name="contact",
        cost_estimate=pl.CostEstimate(flops=6000 * 1024, bytes_accessed=1 << 20, transcendentals=0),
    )(arrived, near, slots)

    new_velocity, new_disp = pl.pallas_call(
        functools.partial(finish_kernel, dims),
        out_shape=(
            jax.ShapeDtypeStruct((slab_len, 3, *plane), f32),
            jax.ShapeDtypeStruct((slab_len, 3, *plane), f32),
        ),
        in_specs=[VMEM] * 7,
        out_specs=(VMEM, VMEM),
        scratch_shapes=[pltpu.VMEM((2, *plane), f32)],
        compiler_params=PARAMS,
        name="finish",
    )(arrived, relayed, before, pushes, own_columns, disp, selector)
    order = (0, 2, 1, 3)
    return jnp.transpose(new_velocity, order), jnp.transpose(new_disp, order)


def solution(mesh):
    shape = dict(mesh.shape)
    devices = mesh.devices.reshape(shape["region"], shape["depth"] // 2, 2)
    fine = Mesh(devices, ("region", "pair", "core"))
    depth = ("pair", "core")
    in_specs = (
        P(depth, None, None, "region"),
        P(depth, None, None, "region"),
        P(depth, None, "region"),
        P(depth, None, "region"),
        P(depth, "region", None, None),
        P(depth, "region"),
        P(depth, "region", None, None),
    )
    out_specs = (P(depth, None, None, "region"), P(depth, None, None, "region"))
    return jax.shard_map(local, mesh=fine, in_specs=in_specs, out_specs=out_specs, check_vma=False)
```

```python
import functools
import math

import jax
import jax.numpy as jnp
from jax import lax
from jax.experimental import pallas as pl
from jax.experimental.pallas import tpu as pltpu
from jax.sharding import Mesh
from jax.sharding import PartitionSpec as P

CAP = 4
STEP_TIME = 0.2
REST_VOLUME = 1.0 / 6.0
PERMUTATIONS = ((0, 1, 2), (0, 2, 1), (1, 0, 2), (1, 2, 0), (2, 0, 1), (2, 1, 0))
ROWS = 4

VMEM = pl.BlockSpec(memory_space=pltpu.VMEM)
SMEM = pl.BlockSpec(memory_space=pltpu.SMEM)
HBM = pl.BlockSpec(memory_space=pltpu.HBM)
PARAMS = pltpu.CompilerParams(vmem_limit_bytes=16 << 20)
NEAR_TURNS = 4
ROOT = math.sqrt(math.log2(math.e))


def add(total, term):
    return term if total is None else total + term


def unit(axis):
    return tuple(1 if position == 2 - axis else 0 for position in range(3))


def tensions(edges, growth, scale_side, scale_up):
    inverse = 1.0 / growth
    columns = {}
    for (axis, start), rows in edges.items():
        made = []
        for row in range(3):
            value = rows[row] + 1.0 if row == axis else rows[row]
            made.append(value * inverse if axis < 2 else value)
        columns[(axis, start)] = made
    pulls = {}
    for first, second, third in PERMUTATIONS:
        middle = unit(first)
        upper = tuple(a + b for a, b in zip(middle, unit(second)))
        keys = {first: (first, (0, 0, 0)), second: (second, middle), third: (third, upper)}
        fe = [[columns[keys[col]][row] for col in range(3)] for row in range(3)]
        cof = [
            [
                fe[(row + 1) % 3][(col + 1) % 3] * fe[(row + 2) % 3][(col + 2) % 3]
                - fe[(row + 1) % 3][(col + 2) % 3] * fe[(row + 2) % 3][(col + 1) % 3]
                for col in range(3)
            ]
            for row in range(3)
        ]
        jacobian = fe[0][0] * cof[0][0] + fe[0][1] * cof[0][1] + fe[0][2] * cof[0][2]
        pressure = 4.0 * jacobian - 5.0
        for col in range(3):
            key = keys[col]
            for row in range(3):
                pulls.setdefault(key, [None] * 3)
                pulls[key][row] = add(pulls[key][row], fe[row][col] + pressure * cof[row][col])
    return {
        key: [value * (scale_side if key[0] < 2 else scale_up) for value in rows]
        for key, rows in pulls.items()
    }


def roll(value, shift, axis):
    size = value.shape[axis]
    shift = shift % size
    return value if shift == 0 else pltpu.roll(value, shift, axis)


def lane_of(shape):
    return lax.broadcasted_iota(jnp.int32, shape, len(shape) - 1)


def column_pack(fields, lane_from, stride, offset):
    shape = fields[0][0].shape
    lane = lane_of(shape)
    packed = jnp.zeros(shape, jnp.float32)
    for c, layers in enumerate(fields):
        for z, field in enumerate(layers):
            to = c * stride + z + offset
            packed = jnp.where(lane == to, roll(field, to - lane_from, 1), packed)
    return packed


def each(count, body, unrolled):
    if count <= unrolled:
        for index in range(count):
            body(index)
    else:

        def one(index, carry):
            body(index)
            return carry

        lax.fori_loop(0, count, one, 0)


def split(value, size):
    if size & (size - 1):
        return lax.div(value, size), lax.rem(value, size)
    return lax.shift_right_logical(value, size.bit_length() - 1), lax.bitwise_and(value, size - 1)


def slab_index():
    return lax.axis_index("pair") * lax.axis_size("core") + lax.axis_index("core")


def thirds(value):
    high = value.astype(jnp.bfloat16)
    rest = value - high.astype(jnp.float32)
    middle = rest.astype(jnp.bfloat16)
    low = (rest - middle.astype(jnp.float32)).astype(jnp.bfloat16)
    return high, middle, low


def picked(chosen, value, contract):
    chosen = chosen.astype(jnp.bfloat16)
    total = None
    for part in thirds(value):
        term = lax.dot_general(
            chosen,
            part,
            (((contract,), (0,)), ((), ())),
            preferred_element_type=jnp.float32,
        )
        total = add(total, term)
    return total


def shift_y(value, step, half_lanes, first_row, last_row):
    moved = roll(value, step, 0)
    return jnp.where(
        first_row if step > 0 else last_row, roll(moved, step * half_lanes, 1), moved
    )


def pack_kernel(
    dims,
    disp_in,
    growth_in,
    shear_in,
    slots_in,
    packet,
    face_a,
    face_b,
    disp,
    growth,
    shear,
    slots,
    counted,
    face,
    sems,
):
    slab_len, width_y, patch_len, regions, slabs, pairs = dims
    region = lax.axis_index("region")
    depth = slab_index()
    pair = lax.axis_index("pair")
    blocks = slabs // 2
    stride = slab_len + 2
    moves = [
        pltpu.make_async_copy(source, target, sems.at[index])
        for index, (source, target) in enumerate(
            (
                (slots_in, slots),
                (disp_in, disp.at[0 : slab_len * 3 * width_y]),
                (growth_in, growth),
                (shear_in, shear),
            )
        )
    ]
    for move in moves:
        move.start()
    tall = CAP * ROWS
    blank = jnp.zeros((tall, patch_len), jnp.float32)

    def base_of(m, block):
        return pl.multiple_of((m * blocks + block) * tall, tall)

    def clear(m):
        counted[m] = 0
        packet[pl.ds(base_of(m, pair), tall), :] = blank

    disp[slab_len * 3 * width_y :, :] = jnp.zeros((ROWS * width_y, patch_len), jnp.float32)
    each(regions, clear, 16)
    for move in moves:
        move.wait()

    tile_row = lax.broadcasted_iota(jnp.int32, (ROWS, patch_len), 0)

    def place(k):
        own, other = slots[0, 0, 0, k], slots[0, 1, 0, k]
        position = counted[other]
        counted[other] = position + 1
        fits = position < CAP
        base = (jnp.where(fits, other, region) * blocks + pair) * tall
        base = pl.multiple_of(base + jnp.where(fits, position, 0) * ROWS, ROWS)
        z, y = split(own, width_y)
        row = z * (3 * width_y) + y
        tile = disp[pl.ds(row, ROWS, stride=width_y), :]
        label = jnp.full((ROWS, patch_len), own, jnp.int32).astype(jnp.float32)
        packet[pl.ds(base, ROWS), :] = jnp.where(tile_row == 3, label, tile)

    each(pairs, place, 16)

    even = lax.rem(depth, 2) == 0
    last = slab_len - 1
    for out, from_z in ((face_a, jnp.where(even, last, 0)), (face_b, jnp.where(even, 0, last))):
        for c in range(3):
            start = pl.multiple_of((from_z * 3 + c) * width_y, width_y)
            out[c] = disp[pl.ds(start, width_y), :]
        out[3] = growth[last]
        out[4] = shear[last]

    groups = width_y // CAP
    width = patch_len // groups
    def plane(z, c):
        start = (z * 3 + c) * width_y
        return disp[start : start + width_y, :]

    fields = [[plane(z, c) for z in range(slab_len)] for c in range(3)]
    fields = fields + [[growth[z] for z in range(slab_len)], [shear[z] for z in range(slab_len)]]
    sides = ((patch_len - 1, fields, 1), (0, fields[:3], regions - 1))
    lane = lane_of((CAP, patch_len))
    for side, (lane_from, chosen, step) in enumerate(sides):
        ringed = [[layers[-1]] + layers + [layers[0]] for layers in chosen]
        face[side] = column_pack(ringed, lane_from, stride, 0)
        folded = jnp.zeros((CAP, patch_len), jnp.float32)
        for g in range(groups):
            at = (g % 2) * (groups // 2) + g // 2
            part = roll(face[side, at * CAP : (at + 1) * CAP, :], g * width, 1)
            folded = jnp.where((lane >= g * width) & (lane < (g + 1) * width), part, folded)
        other = lax.rem(region + step, regions)
        for block in range(blocks):
            rows = pl.ds(base_of(other, block) + 3, CAP, stride=ROWS)
            packet[rows, :] = jnp.where(lane < patch_len - 1, folded, packet[rows, :])


def layer_edges(layer):
    along_x, along_y, moved = {}, {}, {}
    for c in range(3):
        base = layer[c]
        next_x = roll(base, -1, 1)
        next_y = roll(base, -1, 0)
        next_xy = roll(next_y, -1, 1)
        moved[c] = {(0, 0): base, (0, 1): next_x, (1, 0): next_y, (1, 1): next_xy}
        along_x[c] = {0: next_x - base, 1: next_xy - next_y}
        along_y[c] = {0: next_y - base, 1: next_xy - next_x}
    return along_x, along_y, moved


def cell_layer(low, high, growth, shear, valid):
    edges = {}
    for dz, (along_x, along_y, _) in enumerate((low, high)):
        for other in range(2):
            edges[(0, (dz, other, 0))] = [along_x[c][other] for c in range(3)]
            edges[(1, (dz, 0, other))] = [along_y[c][other] for c in range(3)]
    for dy in range(2):
        for dx in range(2):
            edges[(2, (0, dy, dx))] = [
                high[2][c][(dy, dx)] - low[2][c][(dy, dx)] for c in range(3)
            ]
    scale = jnp.where(valid, shear * REST_VOLUME, 0.0) * growth
    pulls = tensions(edges, growth, scale, scale * growth)
    levels = []
    for dz in range(2):
        level = []
        for c in range(3):
            pull_x = pulls[(0, (dz, 0, 0))][c] + roll(pulls[(0, (dz, 1, 0))][c], 1, 0)
            pull_y = pulls[(1, (dz, 0, 0))][c] + roll(pulls[(1, (dz, 0, 1))][c], 1, 1)
            level.append((pull_x - roll(pull_x, 1, 1)) + (pull_y - roll(pull_y, 1, 0)))
        levels.append(level)
    for c in range(3):
        at_zero = pulls[(2, (0, 0, 0))][c] + roll(pulls[(2, (0, 1, 0))][c], 1, 0)
        at_one = pulls[(2, (0, 0, 1))][c] + roll(pulls[(2, (0, 1, 1))][c], 1, 0)
        pull_z = at_zero + roll(at_one, 1, 1)
        levels[0][c] = levels[0][c] + pull_z
        levels[1][c] = levels[1][c] - pull_z
    return levels


def inner_cells(width_y, patch_len):
    shape = (width_y, patch_len)
    row_y = lax.broadcasted_iota(jnp.int32, shape, 0)
    return (lane_of(shape) < patch_len - 1) & (row_y < width_y - 1)


def inner_kernel(
    dims,
    disp,
    growth,
    shear,
    velocity,
    slots,
    slot_row,
    count,
    separation,
    before,
    near,
    selector,
):
    slab_len, width_y, patch_len, regions, slabs, pairs = dims
    inside = inner_cells(width_y, patch_len)
    forces = [[None] * 3 for _ in range(slab_len)]
    low = layer_edges([disp[0, c] for c in range(3)])
    for z in range(slab_len - 1):
        high = layer_edges([disp[z + 1, c] for c in range(3)])
        levels = cell_layer(low, high, growth[z], shear[z], inside)
        low = high
        for dz in range(2):
            for c in range(3):
                forces[z + dz][c] = add(forces[z + dz][c], levels[dz][c])
        for c in range(3):
            before[z, c] = velocity[z, c] + STEP_TIME * forces[z][c]
    for c in range(3):
        before[slab_len - 1, c] = velocity[slab_len - 1, c] + STEP_TIME * forces[slab_len - 1][c]

    along = lane_of((1, patch_len)).astype(jnp.float32)

    def fetch(k):
        z, y = split(slots[0, 0, 0, k], width_y)
        for c in range(3):
            point = disp[z, c, pl.ds(y, 1), :]
            if c == 0:
                point = point + along
            near[c, pl.ds(k, 1), :] = (point - separation[0, c, 0, k]) * ROOT

    each(pairs, fetch, 16)
    patch_row = lax.broadcasted_iota(jnp.int32, selector.shape, 0)
    live = lax.broadcasted_iota(jnp.int32, selector.shape, 1) < count[0, 0]
    selector[...] = jnp.where((patch_row == slot_row[0, 0]) & live, 1.0, 0.0)


def outer_kernel(dims, disp, growth, shear, face_a, face_b, lowest, highest, own_columns):
    slab_len, width_y, patch_len, regions, slabs, pairs = dims
    depth = slab_index()
    inside = inner_cells(width_y, patch_len)
    even = lax.rem(depth, 2) == 0
    below = [jnp.where(even, face_b[c], face_a[c]) for c in range(5)]
    above = [jnp.where(even, face_a[c], face_b[c]) for c in range(3)]
    has_below = depth > 0
    last = slab_len - 1
    below_growth = jnp.where(has_below, below[3], 1.0)
    first_nodes = [disp[0, c] for c in range(3)]
    last_nodes = [disp[last, c] for c in range(3)]
    low, high = layer_edges(below[0:3]), layer_edges(first_nodes)
    levels = cell_layer(low, high, below_growth, below[4], inside & has_below)
    for c in range(3):
        lowest[c] = levels[1][c]
    low, high = layer_edges(last_nodes), layer_edges(above)
    levels = cell_layer(low, high, growth[last], shear[last], inside & (depth < slabs - 1))
    for c in range(3):
        highest[c] = levels[0][c]

    half_rows = width_y // 2
    stride = slab_len + 2
    lane_half = lane_of((half_rows, patch_len)) < patch_len // 4
    side_fields = [
        [below[c]] + [disp[z, c] for z in range(slab_len)] + [above[c]] for c in range(3)
    ]
    cell_fields = [
        [below_growth] + [growth[z] for z in range(slab_len)],
        [below[4]] + [shear[z] for z in range(slab_len)],
    ]
    for side, (chosen, lane_from) in enumerate(
        ((side_fields + cell_fields, patch_len - 1), (side_fields, 0))
    ):
        column = column_pack(chosen, lane_from, stride, 0)
        upper = roll(column[half_rows:], patch_len // 4, 1)
        own_columns[side] = jnp.where(lane_half, column[:half_rows], upper)


def border_forces(dims, arrived, relayed, own_columns):
    slab_len, width_y, patch_len, regions, slabs, pairs = dims
    region = lax.axis_index("region")
    depth = slab_index()
    pair = lax.axis_index("pair")
    core = lax.axis_index("core")
    blocks = slabs // 2
    stride = slab_len + 2
    groups = width_y // CAP
    width = patch_len // groups
    half = patch_len // 2
    fold_lane = lane_of((CAP, patch_len))
    fold_z = lax.rem(lax.rem(fold_lane, width), stride)
    gathered = []
    for step in (regions - 1, 1):
        other = lax.rem(region + step, regions)

        def columns(block):
            base = (other * blocks + lax.rem(block + blocks, blocks)) * CAP
            return relayed[pl.ds(pl.multiple_of(base, CAP), CAP), :]

        base = (other * blocks + pair) * (CAP * ROWS)
        merged = arrived[pl.ds(base + 3, CAP, stride=ROWS), :]
        merged = jnp.where(fold_z == 0, columns(pair - 1 + core), merged)
        merged = jnp.where(fold_z == slab_len + 1, columns(pair + core), merged)
        gathered.append(jnp.concatenate([merged] * (groups // 2), axis=0))
    from_left, from_right = gathered
    own_last = own_columns[0]
    own_first = own_columns[1]
    half_rows = width_y // 2
    shape = (half_rows, patch_len)
    lane = lane_of(shape)
    row = lax.broadcasted_iota(jnp.int32, shape, 0)
    first_row, last_row = row == 0, row == half_rows - 1
    first_side = lane < half
    quarter = half // 2
    z_cell = lax.rem(lane, quarter)
    row_y = row + jnp.where(lax.rem(lane, half) >= quarter, half_rows, 0)

    def at_y(value, step):
        return shift_y(value, step, quarter, first_row, last_row)

    z_global = depth * slab_len + z_cell - 1
    valid = (z_cell <= slab_len) & (z_global >= 0) & (z_global <= slab_len * slabs - 2)
    valid = valid & (row_y < width_y - 1)

    part = row // CAP

    def unfolded(source, shift):
        value = roll(source, shift, 1)
        for p in range(1, groups // 2):
            value = jnp.where(part == p, roll(source, shift - p * 2 * width, 1), value)
        return value

    low_x = [
        jnp.where(
            first_side, unfolded(from_left, -c * stride), roll(own_last, half - c * stride, 1)
        )
        for c in range(5)
    ]
    high_x = [
        jnp.where(
            first_side, roll(own_first, -c * stride, 1), unfolded(from_right, half - c * stride)
        )
        for c in range(3)
    ]
    growth = jnp.where(valid, low_x[3], 1.0)
    scale = jnp.where(valid, low_x[4] * REST_VOLUME, 0.0) * growth
    corner = {}
    for c in range(3):
        for dx, base in ((0, low_x[c]), (1, high_x[c])):
            up = roll(base, -1, 1)
            corner[(c, 0, 0, dx)] = base
            corner[(c, 0, 1, dx)] = at_y(base, -1)
            corner[(c, 1, 0, dx)] = up
            corner[(c, 1, 1, dx)] = at_y(up, -1)
    edges = {}
    for one in range(2):
        for two in range(2):
            for axis, start in ((0, (one, two, 0)), (1, (one, 0, two)), (2, (0, one, two))):
                end = tuple(a + b for a, b in zip(start, unit(axis)))
                edges[(axis, start)] = [corner[(c, *end)] - corner[(c, *start)] for c in range(3)]
    pulls = tensions(edges, growth, scale, scale * growth)
    forces = []
    for c in range(3):

        def chosen(axis, one):
            at = ((one, 0, 0), (one, 0, 1)) if axis == 1 else ((0, one, 0), (0, one, 1))
            return jnp.where(first_side, pulls[(axis, at[1])][c], pulls[(axis, at[0])][c])

        level = []
        for dz in range(2):
            both = pulls[(0, (dz, 0, 0))][c] + at_y(pulls[(0, (dz, 1, 0))][c], 1)
            both = jnp.where(first_side, -both, both)
            along_y = chosen(1, dz)
            level.append(both + (along_y - at_y(along_y, 1)))
        along_z = chosen(2, 0) + at_y(chosen(2, 1), 1)
        forces.append((level[0] + along_z) + roll(level[1] - along_z, 1, 1))
    return forces


def contact_kernel(
    dims, arrived, near, slots, before, lowest, highest, selector, moved, far, tiles, pushes
):
    slab_len, width_y, patch_len, regions, slabs, pairs = dims
    block = 8
    pair = lax.axis_index("pair")
    blocks = slabs // 2
    tall = CAP * ROWS

    def take(m):
        rows = pl.ds(pl.multiple_of((m * blocks + pair) * tall, tall), tall)
        tiles[pl.ds(pl.multiple_of(m * tall, tall), tall), :] = arrived[rows, :]

    each(regions, take, 16)

    total_tiles = regions * CAP
    wide = (total_tiles, pairs)
    label = tiles[pl.ds(3, total_tiles, stride=ROWS), :][:, patch_len - 1 :]
    label = jnp.broadcast_to(label, (total_tiles, max(pairs, patch_len)))
    tile_row = lax.broadcasted_iota(jnp.int32, label.shape, 0)
    again = tile_row < 0
    for back in range(1, CAP):
        same = (roll(label, back, 0) == label) & (lax.rem(tile_row, CAP) >= back)
        again = again | same
    label = jnp.where(again, -1.0, label)[:, 0:pairs]
    tile_row = lax.broadcasted_iota(jnp.int32, wide, 0) // CAP
    wanted = (tile_row == slots[0, 1]) & (label == slots[0, 2].astype(jnp.float32))
    chosen = jnp.where(wanted, 1.0, 0.0)
    for c in range(3):
        far[c] = picked(chosen, tiles[pl.ds(c, total_tiles, stride=ROWS), :], 0)
    along = lane_of((block, patch_len)).astype(jnp.float32)

    def contact(start):
        rows = pl.ds(start, block)
        mine = [near[c, rows, :] for c in range(3)]
        theirs = [far[c, rows, :] for c in range(3)]
        theirs = [(theirs[0] + along) * ROOT, theirs[1] * ROOT, theirs[2] * ROOT]

        starts = range(0, patch_len, patch_len // NEAR_TURNS)
        turned = [[roll(value, -a, 1) for value in mine] for a in starts]
        sums = [[None] * 3 for _ in starts]
        for b in range(patch_len // NEAR_TURNS):
            other = [roll(value, b, 1) for value in theirs]
            for total, here in zip(sums, turned):
                delta = [here[c] - other[c] for c in range(3)]
                square = delta[0] * delta[0] + delta[1] * delta[1] + delta[2] * delta[2]
                weight = jnp.exp2(-square)
                for c in range(3):
                    total[c] = add(total[c], delta[c] * weight)
        total = [None] * 3
        for a, part in zip(starts, sums):
            for c in range(3):
                total[c] = add(total[c], roll(part[c], a, 1))
        for c in range(3):
            pushes[c, rows, :] = total[c]

    each(pairs // block, lambda step: contact(step * block), 2)

    for c in range(3):
        push = picked(selector[...], pushes[c], 1) * (1.0 / ROOT)
        for z in range(slab_len):
            force = push[z * width_y : (z + 1) * width_y, :]
            if z == 0:
                force = force + lowest[c]
            if z == slab_len - 1:
                force = force + highest[c]
            moved[z, c] = before[z, c] + STEP_TIME * force


def finish_kernel(dims, arrived, relayed, moved, own_columns, disp, new_velocity, new_disp):
    slab_len, width_y, patch_len, regions, slabs, pairs = dims
    half = patch_len // 2
    borders = border_forces(dims, arrived, relayed, own_columns)
    half_rows = width_y // 2
    lane = lane_of((half_rows, patch_len))
    last = patch_len - 1
    for c in range(3):
        edge = borders[c] * STEP_TIME
        for z in range(slab_len):
            for part in range(2):
                at = part * (half // 2) + z + 1
                rows = slice(part * half_rows, (part + 1) * half_rows)
                speed = moved[z, c, rows, :]
                speed = speed + jnp.where(lane == 0, roll(edge, -at, 1), 0.0)
                speed = speed + jnp.where(lane == last, roll(edge, last - half - at, 1), 0.0)
                new_velocity[z, c, rows, :] = speed
                new_disp[z, c, rows, :] = disp[z, c, rows, :] + STEP_TIME * speed


def local(displacement, velocity, growth, shear_modulus, pair_slots, pair_count, separation):
    slab_len, width_y, _, patch_len = displacement.shape
    regions = lax.axis_size("region")
    slabs = lax.axis_size("pair") * lax.axis_size("core")
    pairs = pair_slots.shape[3]
    dims = (slab_len, width_y, patch_len, regions, slabs, pairs)
    f32 = jnp.float32
    i32 = jnp.int32
    disp = jnp.transpose(displacement, (0, 2, 1, 3))
    speed = jnp.transpose(velocity, (0, 2, 1, 3))
    slots = jnp.transpose(pair_slots, (0, 2, 1, 3))
    apart = jnp.transpose(separation, (0, 2, 1, 3))
    plane = (width_y, patch_len)

    packet, face_a, face_b = pl.pallas_call(
        functools.partial(pack_kernel, dims),
        out_shape=(
            jax.ShapeDtypeStruct((regions * (slabs // 2) * CAP * ROWS, patch_len), f32),
            jax.ShapeDtypeStruct((5, *plane), f32),
            jax.ShapeDtypeStruct((5, *plane), f32),
        ),
        in_specs=[HBM] * 4,
        out_specs=(VMEM, VMEM, VMEM),
        scratch_shapes=[
            pltpu.VMEM(((slab_len * 3 + ROWS) * width_y, patch_len), f32),
            pltpu.VMEM((slab_len, *plane), f32),
            pltpu.VMEM((slab_len, *plane), f32),
            pltpu.SMEM(slots.shape, i32),
            pltpu.SMEM((regions,), i32),
            pltpu.VMEM((2, *plane), f32),
            pltpu.SemaphoreType.DMA((4,)),
        ],
        name="pack",
    )(disp.reshape(slab_len * 3 * width_y, patch_len), growth, shear_modulus, slots)

    links = [[(i, i + 1) for i in range(first, slabs - 1, 2)] for first in (0, 1)]
    links = [link + [(b, a) for a, b in link] for link in links]
    face_a = lax.ppermute(face_a, ("pair", "core"), links[0])
    face_b = lax.ppermute(face_b, ("pair", "core"), links[1])

    packet, pair_count = lax.optimization_barrier((packet, pair_count))
    arrived = lax.all_to_all(packet, ("region", "pair"), 0, 0, tiled=True)

    before, near, selector = pl.pallas_call(
        functools.partial(inner_kernel, dims),
        out_shape=(
            jax.ShapeDtypeStruct((slab_len, 3, *plane), f32),
            jax.ShapeDtypeStruct((3, pairs, patch_len), f32),
            jax.ShapeDtypeStruct((slab_len * width_y, pairs), f32),
        ),
        in_specs=[VMEM] * 4 + [SMEM, VMEM, SMEM, SMEM],
        out_specs=(VMEM,) * 3,
        compiler_params=PARAMS,
        name="inner",
        cost_estimate=pl.CostEstimate(flops=4000 * 1024, bytes_accessed=1 << 20, transcendentals=0),
    )(disp, growth, shear_modulus, speed, slots, slots, pair_count, apart)

    lowest, highest, own_columns = pl.pallas_call(
        functools.partial(outer_kernel, dims),
        out_shape=(
            jax.ShapeDtypeStruct((3, *plane), f32),
            jax.ShapeDtypeStruct((3, *plane), f32),
            jax.ShapeDtypeStruct((2, width_y // 2, patch_len), f32),
        ),
        in_specs=[VMEM] * 5,
        out_specs=(VMEM,) * 3,
        compiler_params=PARAMS,
        name="outer",
        cost_estimate=pl.CostEstimate(flops=2000 * 1024, bytes_accessed=1 << 20, transcendentals=0),
    )(disp, growth, shear_modulus, face_a, face_b)

    arrived, before, lowest = lax.optimization_barrier((arrived, before, lowest))
    columns = arrived.reshape(-1, ROWS, patch_len)[:, ROWS - 1, :]
    relayed = lax.ppermute(columns, ("pair", "core"), links[0])

    moved = pl.pallas_call(
        functools.partial(contact_kernel, dims),
        out_shape=jax.ShapeDtypeStruct((slab_len, 3, *plane), f32),
        in_specs=[VMEM] * 7,
        out_specs=VMEM,
        scratch_shapes=[
            pltpu.VMEM((3, pairs, patch_len), f32),
            pltpu.VMEM((regions * CAP * ROWS, patch_len), f32),
            pltpu.VMEM((3, pairs, patch_len), f32),
        ],
        compiler_params=PARAMS,
        name="contact",
        cost_estimate=pl.CostEstimate(flops=6000 * 1024, bytes_accessed=1 << 20, transcendentals=0),
    )(arrived, near, slots, before, lowest, highest, selector)

    new_velocity, new_disp = pl.pallas_call(
        functools.partial(finish_kernel, dims),
        out_shape=(
            jax.ShapeDtypeStruct((slab_len, 3, *plane), f32),
            jax.ShapeDtypeStruct((slab_len, 3, *plane), f32),
        ),
        in_specs=[VMEM] * 5,
        out_specs=(VMEM, VMEM),
        compiler_params=PARAMS,
        name="finish",
    )(arrived, relayed, moved, own_columns, disp)
    order = (0, 2, 1, 3)
    return jnp.transpose(new_velocity, order), jnp.transpose(new_disp, order)


def solution(mesh):
    shape = dict(mesh.shape)
    devices = mesh.devices.reshape(shape["region"], shape["depth"] // 2, 2)
    fine = Mesh(devices, ("region", "pair", "core"))
    depth = ("pair", "core")
    in_specs = (
        P(depth, None, None, "region"),
        P(depth, None, None, "region"),
        P(depth, None, "region"),
        P(depth, None, "region"),
        P(depth, "region", None, None),
        P(depth, "region"),
        P(depth, "region", None, None),
    )
    out_specs = (P(depth, None, None, "region"), P(depth, None, None, "region"))
    return jax.shard_map(local, mesh=fine, in_specs=in_specs, out_specs=out_specs, check_vma=False)
```

```python
import functools
import math

import jax
import jax.numpy as jnp
from jax import lax
from jax.experimental import pallas as pl
from jax.experimental.pallas import tpu as pltpu
from jax.sharding import Mesh
from jax.sharding import PartitionSpec as P

CAP = 4
STEP_TIME = 0.2
REST_VOLUME = 1.0 / 6.0
PERMUTATIONS = ((0, 1, 2), (0, 2, 1), (1, 0, 2), (1, 2, 0), (2, 0, 1), (2, 1, 0))
ROWS = 4
TILES = CAP // 2

VMEM = pl.BlockSpec(memory_space=pltpu.VMEM)
SMEM = pl.BlockSpec(memory_space=pltpu.SMEM)
HBM = pl.BlockSpec(memory_space=pltpu.HBM)
PARAMS = pltpu.CompilerParams(vmem_limit_bytes=16 << 20)
NEAR_TURNS = 4
ROOT = math.sqrt(math.log2(math.e))


def add(total, term):
    return term if total is None else total + term


def unit(axis):
    return tuple(1 if position == 2 - axis else 0 for position in range(3))


def tensions(edges, growth, scale_side, scale_up):
    inverse = 1.0 / growth
    columns = {}
    for (axis, start), rows in edges.items():
        made = []
        for row in range(3):
            value = rows[row] + 1.0 if row == axis else rows[row]
            made.append(value * inverse if axis < 2 else value)
        columns[(axis, start)] = made
    pulls = {}
    for first, second, third in PERMUTATIONS:
        middle = unit(first)
        upper = tuple(a + b for a, b in zip(middle, unit(second)))
        keys = {first: (first, (0, 0, 0)), second: (second, middle), third: (third, upper)}
        fe = [[columns[keys[col]][row] for col in range(3)] for row in range(3)]
        cof = [
            [
                fe[(row + 1) % 3][(col + 1) % 3] * fe[(row + 2) % 3][(col + 2) % 3]
                - fe[(row + 1) % 3][(col + 2) % 3] * fe[(row + 2) % 3][(col + 1) % 3]
                for col in range(3)
            ]
            for row in range(3)
        ]
        jacobian = fe[0][0] * cof[0][0] + fe[0][1] * cof[0][1] + fe[0][2] * cof[0][2]
        pressure = 4.0 * jacobian - 5.0
        for col in range(3):
            key = keys[col]
            for row in range(3):
                pulls.setdefault(key, [None] * 3)
                pulls[key][row] = add(pulls[key][row], fe[row][col] + pressure * cof[row][col])
    return {
        key: [value * (scale_side if key[0] < 2 else scale_up) for value in rows]
        for key, rows in pulls.items()
    }


def roll(value, shift, axis):
    size = value.shape[axis]
    shift = shift % size
    return value if shift == 0 else pltpu.roll(value, shift, axis)


def lane_of(shape):
    return lax.broadcasted_iota(jnp.int32, shape, len(shape) - 1)


def column_pack(fields, lane_from, stride, offset):
    shape = fields[0][0].shape
    lane = lane_of(shape)
    packed = jnp.zeros(shape, jnp.float32)
    for c, layers in enumerate(fields):
        for z, field in enumerate(layers):
            to = c * stride + z + offset
            packed = jnp.where(lane == to, roll(field, to - lane_from, 1), packed)
    return packed


def each(count, body, unrolled):
    if count <= unrolled:
        for index in range(count):
            body(index)
    else:

        def one(index, carry):
            body(index)
            return carry

        lax.fori_loop(0, count, one, 0)


def split(value, size):
    if size & (size - 1):
        return lax.div(value, size), lax.rem(value, size)
    return lax.shift_right_logical(value, size.bit_length() - 1), lax.bitwise_and(value, size - 1)


def slab_index():
    return lax.axis_index("pair") * lax.axis_size("core") + lax.axis_index("core")


def thirds(value):
    high = value.astype(jnp.bfloat16)
    rest = value - high.astype(jnp.float32)
    middle = rest.astype(jnp.bfloat16)
    low = (rest - middle.astype(jnp.float32)).astype(jnp.bfloat16)
    return high, middle, low


def picked(chosen, value, contract):
    chosen = chosen.astype(jnp.bfloat16)
    total = None
    for part in thirds(value):
        term = lax.dot_general(
            chosen,
            part,
            (((contract,), (0,)), ((), ())),
            preferred_element_type=jnp.float32,
        )
        total = add(total, term)
    return total


def shift_y(value, step, half_lanes, first_row, last_row):
    moved = roll(value, step, 0)
    return jnp.where(
        first_row if step > 0 else last_row, roll(moved, step * half_lanes, 1), moved
    )


def pack_kernel(
    dims,
    disp_in,
    growth_in,
    shear_in,
    slots_in,
    packet,
    face_a,
    face_b,
    disp,
    growth,
    shear,
    slots,
    counted,
    face,
    sems,
):
    slab_len, width_y, patch_len, regions, slabs, pairs = dims
    region = lax.axis_index("region")
    depth = slab_index()
    core = lax.axis_index("core")
    partner = depth + 1 - 2 * core
    stride = slab_len + 2
    half = patch_len // 2
    moves = [
        pltpu.make_async_copy(source, target, sems.at[index])
        for index, (source, target) in enumerate(
            (
                (slots_in, slots),
                (disp_in, disp.at[0 : slab_len * 3 * width_y]),
                (growth_in, growth),
                (shear_in, shear),
            )
        )
    ]
    for move in moves:
        move.start()
    tall = TILES * ROWS
    blank = jnp.zeros((tall, patch_len), jnp.float32)

    def base_of(m, slab):
        return pl.multiple_of((m * slabs + slab) * tall, tall)

    def clear(m):
        counted[m] = 0
        packet[pl.ds(base_of(m, depth), tall), :] = blank
        packet[pl.ds(base_of(m, partner), tall), :] = blank

    disp[slab_len * 3 * width_y :, :] = jnp.zeros((ROWS * width_y, patch_len), jnp.float32)
    each(regions, clear, 16)
    for move in moves:
        move.wait()

    tile_row = lax.broadcasted_iota(jnp.int32, (ROWS, patch_len), 0)

    lane = lane_of((ROWS, patch_len))

    def place(k):
        own, other = slots[0, 0, 0, k], slots[0, 1, 0, k]
        position = counted[other]
        counted[other] = position + 1
        fits = position < CAP
        place_in = jnp.where(fits, position, 0)
        side, offset = split(place_in, TILES)
        m = jnp.where(fits, other, region)
        z, y = split(own, width_y)
        tile = disp[pl.ds(z * (3 * width_y) + y, ROWS, stride=width_y), :]
        label = jnp.full((ROWS, patch_len), own, jnp.int32).astype(jnp.float32)
        tile = jnp.where(tile_row == 3, label, tile)
        turned = roll(tile, half, 1)
        mask = (lane >= half) == (side > 0)
        for slab, value in (
            (depth, jnp.where(lane < half, tile, turned)),
            (partner, jnp.where(lane < half, turned, tile)),
        ):
            base = pl.multiple_of((m * slabs + slab) * tall + offset * ROWS, ROWS)
            pltpu.store(packet.at[pl.ds(base, ROWS), :], value, mask=mask)

    each(pairs, place, 16)

    even = lax.rem(depth, 2) == 0
    last = slab_len - 1
    for out, from_z in ((face_a, jnp.where(even, last, 0)), (face_b, jnp.where(even, 0, last))):
        for c in range(3):
            start = pl.multiple_of((from_z * 3 + c) * width_y, width_y)
            out[c] = disp[pl.ds(start, width_y), :]
        out[3] = growth[last]
        out[4] = shear[last]

    half_rows = width_y // 2
    groups = half_rows // TILES
    width = patch_len // groups

    def plane(z, c):
        start = (z * 3 + c) * width_y
        return disp[start : start + width_y, :]

    fields = [[plane(z, c) for z in range(slab_len)] for c in range(3)]
    fields = fields + [[growth[z] for z in range(slab_len)], [shear[z] for z in range(slab_len)]]
    sides = ((patch_len - 1, fields, 1), (0, fields[:3], regions - 1))
    lane = lane_of((TILES, patch_len))
    for side, (lane_from, chosen, step) in enumerate(sides):
        ringed = [[layers[-1]] + layers + [layers[0]] for layers in chosen]
        face[side] = column_pack(ringed, lane_from, stride, 0)
        folded = []
        for part in range(2):
            value = jnp.zeros((TILES, patch_len), jnp.float32)
            for g in range(groups):
                start = part * half_rows + g * TILES
                rows = roll(face[side, start : start + TILES, :], g * width, 1)
                value = jnp.where((lane >= g * width) & (lane < (g + 1) * width), rows, value)
            folded.append(value)
        other = lax.rem(region + step, regions)
        for slab in range(slabs):
            value = jnp.where(core == slab % 2, folded[0], folded[1])
            rows = pl.ds(base_of(other, slab) + 3, TILES, stride=ROWS)
            packet[rows, :] = jnp.where(lax.rem(lane, half) == half - 1, packet[rows, :], value)


def layer_edges(layer):
    along_x, along_y, moved = {}, {}, {}
    for c in range(3):
        base = layer[c]
        next_x = roll(base, -1, 1)
        next_y = roll(base, -1, 0)
        next_xy = roll(next_y, -1, 1)
        moved[c] = {(0, 0): base, (0, 1): next_x, (1, 0): next_y, (1, 1): next_xy}
        along_x[c] = {0: next_x - base, 1: next_xy - next_y}
        along_y[c] = {0: next_y - base, 1: next_xy - next_x}
    return along_x, along_y, moved


def cell_layer(low, high, growth, shear, valid):
    edges = {}
    for dz, (along_x, along_y, _) in enumerate((low, high)):
        for other in range(2):
            edges[(0, (dz, other, 0))] = [along_x[c][other] for c in range(3)]
            edges[(1, (dz, 0, other))] = [along_y[c][other] for c in range(3)]
    for dy in range(2):
        for dx in range(2):
            edges[(2, (0, dy, dx))] = [
                high[2][c][(dy, dx)] - low[2][c][(dy, dx)] for c in range(3)
            ]
    scale = jnp.where(valid, shear * REST_VOLUME, 0.0) * growth
    pulls = tensions(edges, growth, scale, scale * growth)
    levels = []
    for dz in range(2):
        level = []
        for c in range(3):
            pull_x = pulls[(0, (dz, 0, 0))][c] + roll(pulls[(0, (dz, 1, 0))][c], 1, 0)
            pull_y = pulls[(1, (dz, 0, 0))][c] + roll(pulls[(1, (dz, 0, 1))][c], 1, 1)
            level.append((pull_x - roll(pull_x, 1, 1)) + (pull_y - roll(pull_y, 1, 0)))
        levels.append(level)
    for c in range(3):
        at_zero = pulls[(2, (0, 0, 0))][c] + roll(pulls[(2, (0, 1, 0))][c], 1, 0)
        at_one = pulls[(2, (0, 0, 1))][c] + roll(pulls[(2, (0, 1, 1))][c], 1, 0)
        pull_z = at_zero + roll(at_one, 1, 1)
        levels[0][c] = levels[0][c] + pull_z
        levels[1][c] = levels[1][c] - pull_z
    return levels


def inner_cells(width_y, patch_len):
    shape = (width_y, patch_len)
    row_y = lax.broadcasted_iota(jnp.int32, shape, 0)
    return (lane_of(shape) < patch_len - 1) & (row_y < width_y - 1)


def inner_kernel(
    dims,
    disp,
    growth,
    shear,
    velocity,
    slots,
    slot_row,
    count,
    separation,
    before,
    near,
    selector,
):
    slab_len, width_y, patch_len, regions, slabs, pairs = dims
    inside = inner_cells(width_y, patch_len)
    forces = [[None] * 3 for _ in range(slab_len)]
    low = layer_edges([disp[0, c] for c in range(3)])
    for z in range(slab_len - 1):
        high = layer_edges([disp[z + 1, c] for c in range(3)])
        levels = cell_layer(low, high, growth[z], shear[z], inside)
        low = high
        for dz in range(2):
            for c in range(3):
                forces[z + dz][c] = add(forces[z + dz][c], levels[dz][c])
        for c in range(3):
            before[z, c] = velocity[z, c] + STEP_TIME * forces[z][c]
    for c in range(3):
        before[slab_len - 1, c] = velocity[slab_len - 1, c] + STEP_TIME * forces[slab_len - 1][c]

    along = lane_of((1, patch_len)).astype(jnp.float32)

    def fetch(k):
        z, y = split(slots[0, 0, 0, k], width_y)
        for c in range(3):
            point = disp[z, c, pl.ds(y, 1), :]
            if c == 0:
                point = point + along
            near[c, pl.ds(k, 1), :] = (point - separation[0, c, 0, k]) * ROOT

    each(pairs, fetch, 16)
    patch_row = lax.broadcasted_iota(jnp.int32, selector.shape, 0)
    live = lax.broadcasted_iota(jnp.int32, selector.shape, 1) < count[0, 0]
    selector[...] = jnp.where((patch_row == slot_row[0, 0]) & live, 1.0, 0.0)


def outer_kernel(dims, disp, growth, shear, face_a, face_b, lowest, highest, own_columns):
    slab_len, width_y, patch_len, regions, slabs, pairs = dims
    depth = slab_index()
    inside = inner_cells(width_y, patch_len)
    even = lax.rem(depth, 2) == 0
    below = [jnp.where(even, face_b[c], face_a[c]) for c in range(5)]
    above = [jnp.where(even, face_a[c], face_b[c]) for c in range(3)]
    has_below = depth > 0
    last = slab_len - 1
    below_growth = jnp.where(has_below, below[3], 1.0)
    first_nodes = [disp[0, c] for c in range(3)]
    last_nodes = [disp[last, c] for c in range(3)]
    low, high = layer_edges(below[0:3]), layer_edges(first_nodes)
    levels = cell_layer(low, high, below_growth, below[4], inside & has_below)
    for c in range(3):
        lowest[c] = levels[1][c]
    low, high = layer_edges(last_nodes), layer_edges(above)
    levels = cell_layer(low, high, growth[last], shear[last], inside & (depth < slabs - 1))
    for c in range(3):
        highest[c] = levels[0][c]

    half_rows = width_y // 2
    stride = slab_len + 2
    lane_half = lane_of((half_rows, patch_len)) < patch_len // 4
    side_fields = [
        [below[c]] + [disp[z, c] for z in range(slab_len)] + [above[c]] for c in range(3)
    ]
    cell_fields = [
        [below_growth] + [growth[z] for z in range(slab_len)],
        [below[4]] + [shear[z] for z in range(slab_len)],
    ]
    for side, (chosen, lane_from) in enumerate(
        ((side_fields + cell_fields, patch_len - 1), (side_fields, 0))
    ):
        column = column_pack(chosen, lane_from, stride, 0)
        upper = roll(column[half_rows:], patch_len // 4, 1)
        own_columns[side] = jnp.where(lane_half, column[:half_rows], upper)


def border_forces(dims, arrived, relayed, own_columns):
    slab_len, width_y, patch_len, regions, slabs, pairs = dims
    region = lax.axis_index("region")
    depth = slab_index()
    stride = slab_len + 2
    half_rows = width_y // 2
    groups = half_rows // TILES
    width = patch_len // groups
    half = patch_len // 2
    fold_z = lax.rem(lax.rem(lane_of((TILES, patch_len)), width), stride)
    row_group = lax.broadcasted_iota(jnp.int32, (half_rows, patch_len), 0) // TILES
    lower_y = lane_of((half_rows, patch_len)) < half // 2
    gathered = []
    for step in (regions - 1, 1):
        other = lax.rem(region + step, regions)

        def columns(source, slab):
            base = (other * slabs + lax.rem(slab + slabs, slabs)) * (TILES * ROWS)
            return source[pl.ds(base + 3, TILES, stride=ROWS), :]

        total = jnp.zeros((half_rows, patch_len), jnp.float32)
        for part, (direct, across) in enumerate(((arrived, relayed), (relayed, arrived))):
            merged = columns(direct, depth)
            merged = jnp.where(fold_z == 0, columns(across, depth - 1), merged)
            merged = jnp.where(fold_z == slab_len + 1, columns(across, depth + 1), merged)
            merged = jnp.concatenate([merged] * groups, axis=0)
            for g in range(groups):
                here = (row_group == g) & (lower_y if part == 0 else ~lower_y)
                shift = part * (half // 2) - g * width
                total = jnp.where(here, roll(merged, shift, 1), total)
        gathered.append(total)
    from_left, from_right = gathered
    own_last = own_columns[0]
    own_first = own_columns[1]
    shape = (half_rows, patch_len)
    lane = lane_of(shape)
    row = lax.broadcasted_iota(jnp.int32, shape, 0)
    first_row, last_row = row == 0, row == half_rows - 1
    first_side = lane < half
    quarter = half // 2
    z_cell = lax.rem(lane, quarter)
    row_y = row + jnp.where(lax.rem(lane, half) >= quarter, half_rows, 0)

    def at_y(value, step):
        return shift_y(value, step, quarter, first_row, last_row)

    z_global = depth * slab_len + z_cell - 1
    valid = (z_cell <= slab_len) & (z_global >= 0) & (z_global <= slab_len * slabs - 2)
    valid = valid & (row_y < width_y - 1)

    low_x = [
        jnp.where(
            first_side, roll(from_left, -c * stride, 1), roll(own_last, half - c * stride, 1)
        )
        for c in range(5)
    ]
    high_x = [
        jnp.where(
            first_side, roll(own_first, -c * stride, 1), roll(from_right, half - c * stride, 1)
        )
        for c in range(3)
    ]
    growth = jnp.where(valid, low_x[3], 1.0)
    scale = jnp.where(valid, low_x[4] * REST_VOLUME, 0.0) * growth
    corner = {}
    for c in range(3):
        for dx, base in ((0, low_x[c]), (1, high_x[c])):
            up = roll(base, -1, 1)
            corner[(c, 0, 0, dx)] = base
            corner[(c, 0, 1, dx)] = at_y(base, -1)
            corner[(c, 1, 0, dx)] = up
            corner[(c, 1, 1, dx)] = at_y(up, -1)
    edges = {}
    for one in range(2):
        for two in range(2):
            for axis, start in ((0, (one, two, 0)), (1, (one, 0, two)), (2, (0, one, two))):
                end = tuple(a + b for a, b in zip(start, unit(axis)))
                edges[(axis, start)] = [corner[(c, *end)] - corner[(c, *start)] for c in range(3)]
    pulls = tensions(edges, growth, scale, scale * growth)
    forces = []
    for c in range(3):

        def chosen(axis, one):
            at = ((one, 0, 0), (one, 0, 1)) if axis == 1 else ((0, one, 0), (0, one, 1))
            return jnp.where(first_side, pulls[(axis, at[1])][c], pulls[(axis, at[0])][c])

        level = []
        for dz in range(2):
            both = pulls[(0, (dz, 0, 0))][c] + at_y(pulls[(0, (dz, 1, 0))][c], 1)
            both = jnp.where(first_side, -both, both)
            along_y = chosen(1, dz)
            level.append(both + (along_y - at_y(along_y, 1)))
        along_z = chosen(2, 0) + at_y(chosen(2, 1), 1)
        forces.append((level[0] + along_z) + roll(level[1] - along_z, 1, 1))
    return forces


def far_points(dims, source, chosen, tiles):
    slab_len, width_y, patch_len, regions, slabs, pairs = dims
    depth = slab_index()
    half = patch_len // 2
    tall = TILES * ROWS

    def take(m):
        rows = pl.ds(pl.multiple_of((m * slabs + depth) * tall, tall), tall)
        tiles[pl.ds(pl.multiple_of(m * tall, tall), tall), :] = source[rows, :]

    each(regions, take, 16)
    if chosen is None:
        chosen = yield
    lane = lane_of((pairs, patch_len))
    for c in range(3):
        value = picked(chosen, tiles[pl.ds(c, regions * TILES, stride=ROWS), :], 0)
        value = jnp.where(lane < half, value[:pairs], value[pairs:])
        yield value + roll(value, half, 1)


def tile_choice(dims, slots, tiles):
    slab_len, width_y, patch_len, regions, slabs, pairs = dims
    half = patch_len // 2
    rows = regions * TILES
    found = tiles[pl.ds(3, rows, stride=ROWS), :]
    wide = max(pairs, patch_len)
    labels = [
        jnp.broadcast_to(found[:, side * half + half - 1 : side * half + half], (rows, wide))
        for side in range(2)
    ]
    row = lax.broadcasted_iota(jnp.int32, (rows, wide), 0)
    upper = lax.rem(row, TILES) > 0
    others = [jnp.where(upper, roll(label, 1, 0), roll(label, -1, 0)) for label in labels]
    again = [
        upper & (others[0] == labels[0]),
        (labels[1] == labels[0])
        | (labels[1] == others[0])
        | (upper & (others[1] == labels[1])),
    ]
    region_row = lax.broadcasted_iota(jnp.int32, (rows, pairs), 0) // TILES
    named = slots[0, 2].astype(jnp.float32)
    chosen = []
    for label, repeated in zip(labels, again):
        label = jnp.where(repeated, -1.0, label)[:, 0:pairs]
        chosen.append(jnp.where((region_row == slots[0, 1]) & (label == named), 1.0, 0.0))
    return jnp.concatenate(chosen, axis=1)


def contact_half(dims, near, far, part, write):
    slab_len, width_y, patch_len, regions, slabs, pairs = dims
    half = patch_len // 2
    block = 8
    along = lax.rem(lane_of((block, patch_len)), half) + part * half
    along = along.astype(jnp.float32)

    def some(start):
        rows = pl.ds(start, block)
        mine = [near[c, rows, :] for c in range(3)]
        theirs = [far[c, rows, :] for c in range(3)]
        theirs = [(theirs[0] + along) * ROOT, theirs[1] * ROOT, theirs[2] * ROOT]
        starts = range(0, half, half // NEAR_TURNS)
        turned = [[roll(value, -a, 1) for value in mine] for a in starts]
        sums = [[None] * 3 for _ in starts]
        for b in range(half // NEAR_TURNS):
            other = [roll(value, b, 1) for value in theirs]
            for total, here in zip(sums, turned):
                delta = [here[c] - other[c] for c in range(3)]
                square = delta[0] * delta[0] + delta[1] * delta[1] + delta[2] * delta[2]
                weight = jnp.exp2(-square)
                for c in range(3):
                    total[c] = add(total[c], delta[c] * weight)
        for c in range(3):
            total = None
            for a, sum_a in zip(starts, sums):
                total = add(total, roll(sum_a[c], a, 1))
            write(c, rows, total)

    each(pairs // block, lambda step: some(step * block), 2)


def contact_kernel(dims, arrived, near, slots, chosen, pushes, far, tiles):
    points = far_points(dims, arrived, None, tiles)
    next(points)
    chosen[...] = tile_choice(dims, slots, tiles)
    far[0] = points.send(chosen[...])
    far[1] = next(points)
    far[2] = next(points)

    def write(c, rows, total):
        pushes[c, rows, :] = total

    contact_half(dims, near, far, 0, write)


def finish_kernel(
    dims,
    arrived,
    relayed,
    before,
    lowest,
    highest,
    near,
    chosen,
    pushes,
    own_columns,
    disp,
    selector,
    new_velocity,
    new_disp,
    far,
    tiles,
    total_push,
):
    slab_len, width_y, patch_len, regions, slabs, pairs = dims
    half = patch_len // 2
    for c, value in enumerate(far_points(dims, relayed, chosen[...], tiles)):
        far[c] = value

    def write(c, rows, total):
        total_push[c, rows, :] = pushes[c, rows, :] + total

    contact_half(dims, near, far, 1, write)
    borders = border_forces(dims, arrived, relayed, own_columns)
    half_rows = width_y // 2
    lane = lane_of((half_rows, patch_len))
    last = patch_len - 1
    for c in range(3):
        push = picked(selector[...], total_push[c], 1) * (1.0 / ROOT)
        edge = borders[c]
        for z in range(slab_len):
            for part in range(2):
                at = part * (half // 2) + z + 1
                rows = slice(part * half_rows, (part + 1) * half_rows)
                start = z * width_y + part * half_rows
                force = push[start : start + half_rows, :]
                if z == 0:
                    force = force + lowest[c, rows, :]
                if z == slab_len - 1:
                    force = force + highest[c, rows, :]
                force = force + jnp.where(lane == 0, roll(edge, -at, 1), 0.0)
                force = force + jnp.where(lane == last, roll(edge, last - half - at, 1), 0.0)
                speed = before[z, c, rows, :] + STEP_TIME * force
                new_velocity[z, c, rows, :] = speed
                new_disp[z, c, rows, :] = disp[z, c, rows, :] + STEP_TIME * speed


def local(displacement, velocity, growth, shear_modulus, pair_slots, pair_count, separation):
    slab_len, width_y, _, patch_len = displacement.shape
    regions = lax.axis_size("region")
    slabs = lax.axis_size("pair") * lax.axis_size("core")
    pairs = pair_slots.shape[3]
    dims = (slab_len, width_y, patch_len, regions, slabs, pairs)
    f32 = jnp.float32
    i32 = jnp.int32
    disp = jnp.transpose(displacement, (0, 2, 1, 3))
    speed = jnp.transpose(velocity, (0, 2, 1, 3))
    slots = jnp.transpose(pair_slots, (0, 2, 1, 3))
    apart = jnp.transpose(separation, (0, 2, 1, 3))
    plane = (width_y, patch_len)

    packet, face_a, face_b = pl.pallas_call(
        functools.partial(pack_kernel, dims),
        out_shape=(
            jax.ShapeDtypeStruct((regions * slabs * TILES * ROWS, patch_len), f32),
            jax.ShapeDtypeStruct((5, *plane), f32),
            jax.ShapeDtypeStruct((5, *plane), f32),
        ),
        in_specs=[HBM] * 4,
        out_specs=(VMEM, VMEM, VMEM),
        scratch_shapes=[
            pltpu.VMEM(((slab_len * 3 + ROWS) * width_y, patch_len), f32),
            pltpu.VMEM((slab_len, *plane), f32),
            pltpu.VMEM((slab_len, *plane), f32),
            pltpu.SMEM(slots.shape, i32),
            pltpu.SMEM((regions,), i32),
            pltpu.VMEM((2, *plane), f32),
            pltpu.SemaphoreType.DMA((4,)),
        ],
        name="pack",
    )(disp.reshape(slab_len * 3 * width_y, patch_len), growth, shear_modulus, slots)

    links = [[(i, i + 1) for i in range(first, slabs - 1, 2)] for first in (0, 1)]
    links = [link + [(b, a) for a, b in link] for link in links]
    face_a = lax.ppermute(face_a, ("pair", "core"), links[0])
    face_b = lax.ppermute(face_b, ("pair", "core"), links[1])

    packet, pair_count = lax.optimization_barrier((packet, pair_count))
    arrived = lax.all_to_all(packet, ("region", "pair", "core"), 0, 0, tiled=True)

    before, near, selector = pl.pallas_call(
        functools.partial(inner_kernel, dims),
        out_shape=(
            jax.ShapeDtypeStruct((slab_len, 3, *plane), f32),
            jax.ShapeDtypeStruct((3, pairs, patch_len), f32),
            jax.ShapeDtypeStruct((slab_len * width_y, pairs), f32),
        ),
        in_specs=[VMEM] * 4 + [SMEM, VMEM, SMEM, SMEM],
        out_specs=(VMEM,) * 3,
        compiler_params=PARAMS,
        name="inner",
        cost_estimate=pl.CostEstimate(flops=4000 * 1024, bytes_accessed=1 << 20, transcendentals=0),
    )(disp, growth, shear_modulus, speed, slots, slots, pair_count, apart)

    lowest, highest, own_columns = pl.pallas_call(
        functools.partial(outer_kernel, dims),
        out_shape=(
            jax.ShapeDtypeStruct((3, *plane), f32),
            jax.ShapeDtypeStruct((3, *plane), f32),
            jax.ShapeDtypeStruct((2, width_y // 2, patch_len), f32),
        ),
        in_specs=[VMEM] * 5,
        out_specs=(VMEM,) * 3,
        compiler_params=PARAMS,
        name="outer",
        cost_estimate=pl.CostEstimate(flops=2000 * 1024, bytes_accessed=1 << 20, transcendentals=0),
    )(disp, growth, shear_modulus, face_a, face_b)

    arrived, before, lowest = lax.optimization_barrier((arrived, before, lowest))
    relayed = lax.ppermute(arrived, ("pair", "core"), links[0])

    tile_rows = regions * TILES
    chosen, pushes = pl.pallas_call(
        functools.partial(contact_kernel, dims),
        out_shape=(
            jax.ShapeDtypeStruct((tile_rows, 2 * pairs), f32),
            jax.ShapeDtypeStruct((3, pairs, patch_len), f32),
        ),
        in_specs=[VMEM] * 3,
        out_specs=(VMEM,) * 2,
        scratch_shapes=[
            pltpu.VMEM((3, pairs, patch_len), f32),
            pltpu.VMEM((tile_rows * ROWS, patch_len), f32),
        ],
        compiler_params=PARAMS,
        name="contact",
        cost_estimate=pl.CostEstimate(flops=6000 * 1024, bytes_accessed=1 << 20, transcendentals=0),
    )(arrived, near, slots)

    new_velocity, new_disp = pl.pallas_call(
        functools.partial(finish_kernel, dims),
        out_shape=(
            jax.ShapeDtypeStruct((slab_len, 3, *plane), f32),
            jax.ShapeDtypeStruct((slab_len, 3, *plane), f32),
        ),
        in_specs=[VMEM] * 11,
        out_specs=(VMEM, VMEM),
        scratch_shapes=[
            pltpu.VMEM((3, pairs, patch_len), f32),
            pltpu.VMEM((tile_rows * ROWS, patch_len), f32),
            pltpu.VMEM((3, pairs, patch_len), f32),
        ],
        compiler_params=PARAMS,
        name="finish",
    )(
        arrived,
        relayed,
        before,
        lowest,
        highest,
        near,
        chosen,
        pushes,
        own_columns,
        disp,
        selector,
    )
    order = (0, 2, 1, 3)
    return jnp.transpose(new_velocity, order), jnp.transpose(new_disp, order)


def solution(mesh):
    shape = dict(mesh.shape)
    devices = mesh.devices.reshape(shape["region"], shape["depth"] // 2, 2)
    fine = Mesh(devices, ("region", "pair", "core"))
    depth = ("pair", "core")
    in_specs = (
        P(depth, None, None, "region"),
        P(depth, None, None, "region"),
        P(depth, None, "region"),
        P(depth, None, "region"),
        P(depth, "region", None, None),
        P(depth, "region"),
        P(depth, "region", None, None),
    )
    out_specs = (P(depth, None, None, "region"), P(depth, None, None, "region"))
    return jax.shard_map(local, mesh=fine, in_specs=in_specs, out_specs=out_specs, check_vma=False)
```

```python
import functools
import math

import jax
import jax.numpy as jnp
from jax import lax
from jax.experimental import pallas as pl
from jax.experimental.pallas import tpu as pltpu
from jax.sharding import Mesh
from jax.sharding import PartitionSpec as P

CAP = 4
STEP_TIME = 0.2
REST_VOLUME = 1.0 / 6.0
PERMUTATIONS = ((0, 1, 2), (0, 2, 1), (1, 0, 2), (1, 2, 0), (2, 0, 1), (2, 1, 0))
ROWS = 4
TILES = CAP // 2

VMEM = pl.BlockSpec(memory_space=pltpu.VMEM)
SMEM = pl.BlockSpec(memory_space=pltpu.SMEM)
HBM = pl.BlockSpec(memory_space=pltpu.HBM)
PARAMS = pltpu.CompilerParams(vmem_limit_bytes=16 << 20)
NEAR_TURNS = 8
ROOT = math.sqrt(math.log2(math.e))


def add(total, term):
    return term if total is None else total + term


def unit(axis):
    return tuple(1 if position == 2 - axis else 0 for position in range(3))


def tensions(edges, growth, scale_side, scale_up):
    inverse = 1.0 / growth
    columns = {}
    for (axis, start), rows in edges.items():
        made = []
        for row in range(3):
            value = rows[row] + 1.0 if row == axis else rows[row]
            made.append(value * inverse if axis < 2 else value)
        columns[(axis, start)] = made
    pulls = {}
    for first, second, third in PERMUTATIONS:
        middle = unit(first)
        upper = tuple(a + b for a, b in zip(middle, unit(second)))
        keys = {first: (first, (0, 0, 0)), second: (second, middle), third: (third, upper)}
        fe = [[columns[keys[col]][row] for col in range(3)] for row in range(3)]
        cof = [
            [
                fe[(row + 1) % 3][(col + 1) % 3] * fe[(row + 2) % 3][(col + 2) % 3]
                - fe[(row + 1) % 3][(col + 2) % 3] * fe[(row + 2) % 3][(col + 1) % 3]
                for col in range(3)
            ]
            for row in range(3)
        ]
        jacobian = fe[0][0] * cof[0][0] + fe[0][1] * cof[0][1] + fe[0][2] * cof[0][2]
        pressure = 4.0 * jacobian - 5.0
        for col in range(3):
            key = keys[col]
            for row in range(3):
                pulls.setdefault(key, [None] * 3)
                pulls[key][row] = add(pulls[key][row], fe[row][col] + pressure * cof[row][col])
    return {
        key: [value * (scale_side if key[0] < 2 else scale_up) for value in rows]
        for key, rows in pulls.items()
    }


def roll(value, shift, axis):
    size = value.shape[axis]
    shift = shift % size
    return value if shift == 0 else pltpu.roll(value, shift, axis)


def lane_of(shape):
    return lax.broadcasted_iota(jnp.int32, shape, len(shape) - 1)


def column_pack(fields, lane_from, stride, offset):
    shape = fields[0][0].shape
    lane = lane_of(shape)
    packed = jnp.zeros(shape, jnp.float32)
    for c, layers in enumerate(fields):
        for z, field in enumerate(layers):
            to = c * stride + z + offset
            packed = jnp.where(lane == to, roll(field, to - lane_from, 1), packed)
    return packed


def each(count, body, unrolled):
    if count <= unrolled:
        for index in range(count):
            body(index)
    else:

        def one(index, carry):
            body(index)
            return carry

        lax.fori_loop(0, count, one, 0)


def split(value, size):
    if size & (size - 1):
        return lax.div(value, size), lax.rem(value, size)
    return lax.shift_right_logical(value, size.bit_length() - 1), lax.bitwise_and(value, size - 1)


def slab_index():
    return lax.axis_index("pair") * lax.axis_size("core") + lax.axis_index("core")


def thirds(value):
    high = value.astype(jnp.bfloat16)
    rest = value - high.astype(jnp.float32)
    middle = rest.astype(jnp.bfloat16)
    low = (rest - middle.astype(jnp.float32)).astype(jnp.bfloat16)
    return high, middle, low


def picked(chosen, value, contract):
    chosen = chosen.astype(jnp.bfloat16)
    total = None
    for part in thirds(value):
        term = lax.dot_general(
            chosen,
            part,
            (((contract,), (0,)), ((), ())),
            preferred_element_type=jnp.float32,
        )
        total = add(total, term)
    return total


def shift_y(value, step, half_lanes, first_row, last_row):
    moved = roll(value, step, 0)
    return jnp.where(
        first_row if step > 0 else last_row, roll(moved, step * half_lanes, 1), moved
    )


def pack_kernel(
    dims,
    disp_in,
    growth_in,
    shear_in,
    slots_in,
    packet,
    face_a,
    face_b,
    disp,
    growth,
    shear,
    slots,
    counted,
    face,
    sems,
):
    slab_len, width_y, patch_len, regions, slabs, pairs = dims
    region = lax.axis_index("region")
    depth = slab_index()
    core = lax.axis_index("core")
    partner = depth + 1 - 2 * core
    stride = slab_len + 2
    half = patch_len // 2
    moves = [
        pltpu.make_async_copy(source, target, sems.at[index])
        for index, (source, target) in enumerate(
            (
                (slots_in, slots),
                (disp_in, disp.at[0 : slab_len * 3 * width_y]),
                (growth_in, growth),
                (shear_in, shear),
            )
        )
    ]
    for move in moves:
        move.start()
    tall = TILES * ROWS
    span = 1 << pairs.bit_length()
    blank = jnp.zeros((tall, patch_len), jnp.float32)

    def base_of(m, slab):
        return pl.multiple_of((m * slabs + slab) * tall, tall)

    def clear(m):
        counted[m] = m * (slabs * tall * span)
        packet[pl.ds(base_of(m, depth), tall), :] = blank
        packet[pl.ds(base_of(m, partner), tall), :] = blank

    disp[slab_len * 3 * width_y :, :] = jnp.zeros((ROWS * width_y, patch_len), jnp.float32)
    spare = region * (slabs * tall)
    each(regions, clear, 16)
    for move in moves:
        move.wait()

    tile_row = lax.broadcasted_iota(jnp.int32, (ROWS, patch_len), 0)

    lane = lane_of((ROWS, patch_len))

    def place(k):
        own, other = slots[0, 0, 0, k], slots[0, 1, 0, k]
        state = counted[other]
        counted[other] = state + 1
        first, position = split(state, span)
        fits = position < CAP
        first = jnp.where(fits, first, spare)
        side, offset = split(jnp.where(fits, position, 0), TILES)
        first = first + offset * ROWS
        z, y = split(own, width_y)
        tile = disp[pl.ds(z * (3 * width_y) + y, ROWS, stride=width_y), :]
        label = jnp.full((ROWS, patch_len), own, jnp.int32).astype(jnp.float32)
        tile = jnp.where(tile_row == 3, label, tile)
        turned = roll(tile, half, 1)
        mask = (lane >= half) == (side > 0)
        for slab, value in (
            (depth, jnp.where(lane < half, tile, turned)),
            (partner, jnp.where(lane < half, turned, tile)),
        ):
            base = pl.multiple_of(first + slab * tall, ROWS)
            pltpu.store(packet.at[pl.ds(base, ROWS), :], value, mask=mask)

    each(pairs, place, 16)

    even = lax.rem(depth, 2) == 0
    last = slab_len - 1
    for out, from_z in ((face_a, jnp.where(even, last, 0)), (face_b, jnp.where(even, 0, last))):
        for c in range(3):
            start = pl.multiple_of((from_z * 3 + c) * width_y, width_y)
            out[c] = disp[pl.ds(start, width_y), :]
        out[3] = growth[last]
        out[4] = shear[last]

    half_rows = width_y // 2
    groups = half_rows // TILES
    width = patch_len // groups

    def plane(z, c):
        start = (z * 3 + c) * width_y
        return disp[start : start + width_y, :]

    fields = [[plane(z, c) for z in range(slab_len)] for c in range(3)]
    fields = fields + [[growth[z] for z in range(slab_len)], [shear[z] for z in range(slab_len)]]
    sides = ((patch_len - 1, fields, 1), (0, fields[:3], regions - 1))
    lane = lane_of((TILES, patch_len))
    for side, (lane_from, chosen, step) in enumerate(sides):
        ringed = [[layers[-1]] + layers + [layers[0]] for layers in chosen]
        face[side] = column_pack(ringed, lane_from, stride, 0)
        folded = []
        for part in range(2):
            value = jnp.zeros((TILES, patch_len), jnp.float32)
            for g in range(groups):
                start = part * half_rows + g * TILES
                rows = roll(face[side, start : start + TILES, :], g * width, 1)
                value = jnp.where((lane >= g * width) & (lane < (g + 1) * width), rows, value)
            folded.append(value)
        other = lax.rem(region + step, regions)
        for slab in range(slabs):
            value = jnp.where(core == slab % 2, folded[0], folded[1])
            rows = pl.ds(base_of(other, slab) + 3, TILES, stride=ROWS)
            packet[rows, :] = jnp.where(lax.rem(lane, half) == half - 1, packet[rows, :], value)


def layer_edges(layer):
    along_x, along_y, moved = {}, {}, {}
    for c in range(3):
        base = layer[c]
        next_x = roll(base, -1, 1)
        next_y = roll(base, -1, 0)
        next_xy = roll(next_y, -1, 1)
        moved[c] = {(0, 0): base, (0, 1): next_x, (1, 0): next_y, (1, 1): next_xy}
        along_x[c] = {0: next_x - base, 1: next_xy - next_y}
        along_y[c] = {0: next_y - base, 1: next_xy - next_x}
    return along_x, along_y, moved


def cell_layer(low, high, growth, shear, valid):
    edges = {}
    for dz, (along_x, along_y, _) in enumerate((low, high)):
        for other in range(2):
            edges[(0, (dz, other, 0))] = [along_x[c][other] for c in range(3)]
            edges[(1, (dz, 0, other))] = [along_y[c][other] for c in range(3)]
    for dy in range(2):
        for dx in range(2):
            edges[(2, (0, dy, dx))] = [
                high[2][c][(dy, dx)] - low[2][c][(dy, dx)] for c in range(3)
            ]
    scale = jnp.where(valid, shear * REST_VOLUME, 0.0) * growth
    pulls = tensions(edges, growth, scale, scale * growth)
    levels = []
    for dz in range(2):
        level = []
        for c in range(3):
            pull_x = pulls[(0, (dz, 0, 0))][c] + roll(pulls[(0, (dz, 1, 0))][c], 1, 0)
            pull_y = pulls[(1, (dz, 0, 0))][c] + roll(pulls[(1, (dz, 0, 1))][c], 1, 1)
            level.append((pull_x - roll(pull_x, 1, 1)) + (pull_y - roll(pull_y, 1, 0)))
        levels.append(level)
    for c in range(3):
        at_zero = pulls[(2, (0, 0, 0))][c] + roll(pulls[(2, (0, 1, 0))][c], 1, 0)
        at_one = pulls[(2, (0, 0, 1))][c] + roll(pulls[(2, (0, 1, 1))][c], 1, 0)
        pull_z = at_zero + roll(at_one, 1, 1)
        levels[0][c] = levels[0][c] + pull_z
        levels[1][c] = levels[1][c] - pull_z
    return levels


def inner_cells(width_y, patch_len):
    shape = (width_y, patch_len)
    row_y = lax.broadcasted_iota(jnp.int32, shape, 0)
    return (lane_of(shape) < patch_len - 1) & (row_y < width_y - 1)


def inner_kernel(
    dims,
    disp,
    growth,
    shear,
    velocity,
    slots,
    slot_row,
    count,
    separation,
    before,
    near,
    selector,
):
    slab_len, width_y, patch_len, regions, slabs, pairs = dims
    inside = inner_cells(width_y, patch_len)
    forces = [[None] * 3 for _ in range(slab_len)]
    low = layer_edges([disp[0, c] for c in range(3)])
    for z in range(slab_len - 1):
        high = layer_edges([disp[z + 1, c] for c in range(3)])
        levels = cell_layer(low, high, growth[z], shear[z], inside)
        low = high
        for dz in range(2):
            for c in range(3):
                forces[z + dz][c] = add(forces[z + dz][c], levels[dz][c])
        for c in range(3):
            before[z, c] = velocity[z, c] + STEP_TIME * forces[z][c]
    for c in range(3):
        before[slab_len - 1, c] = velocity[slab_len - 1, c] + STEP_TIME * forces[slab_len - 1][c]

    along = lane_of((1, patch_len)).astype(jnp.float32)

    def fetch(k):
        z, y = split(slots[0, 0, 0, k], width_y)
        for c in range(3):
            point = disp[z, c, pl.ds(y, 1), :]
            if c == 0:
                point = point + along
            near[c, pl.ds(k, 1), :] = (point - separation[0, c, 0, k]) * ROOT

    each(pairs, fetch, 16)
    patch_row = lax.broadcasted_iota(jnp.int32, selector.shape, 0)
    live = lax.broadcasted_iota(jnp.int32, selector.shape, 1) < count[0, 0]
    selector[...] = jnp.where((patch_row == slot_row[0, 0]) & live, 1.0, 0.0)


def outer_kernel(dims, disp, growth, shear, face_a, face_b, lowest, highest, own_columns):
    slab_len, width_y, patch_len, regions, slabs, pairs = dims
    depth = slab_index()
    inside = inner_cells(width_y, patch_len)
    even = lax.rem(depth, 2) == 0
    below = [jnp.where(even, face_b[c], face_a[c]) for c in range(5)]
    above = [jnp.where(even, face_a[c], face_b[c]) for c in range(3)]
    has_below = depth > 0
    last = slab_len - 1
    below_growth = jnp.where(has_below, below[3], 1.0)
    first_nodes = [disp[0, c] for c in range(3)]
    last_nodes = [disp[last, c] for c in range(3)]
    low, high = layer_edges(below[0:3]), layer_edges(first_nodes)
    levels = cell_layer(low, high, below_growth, below[4], inside & has_below)
    for c in range(3):
        lowest[c] = levels[1][c]
    low, high = layer_edges(last_nodes), layer_edges(above)
    levels = cell_layer(low, high, growth[last], shear[last], inside & (depth < slabs - 1))
    for c in range(3):
        highest[c] = levels[0][c]

    half_rows = width_y // 2
    stride = slab_len + 2
    lane_half = lane_of((half_rows, patch_len)) < patch_len // 4
    side_fields = [
        [below[c]] + [disp[z, c] for z in range(slab_len)] + [above[c]] for c in range(3)
    ]
    cell_fields = [
        [below_growth] + [growth[z] for z in range(slab_len)],
        [below[4]] + [shear[z] for z in range(slab_len)],
    ]
    for side, (chosen, lane_from) in enumerate(
        ((side_fields + cell_fields, patch_len - 1), (side_fields, 0))
    ):
        column = column_pack(chosen, lane_from, stride, 0)
        upper = roll(column[half_rows:], patch_len // 4, 1)
        own_columns[side] = jnp.where(lane_half, column[:half_rows], upper)


def border_forces(dims, arrived, relayed, own_columns):
    slab_len, width_y, patch_len, regions, slabs, pairs = dims
    region = lax.axis_index("region")
    depth = slab_index()
    stride = slab_len + 2
    half_rows = width_y // 2
    groups = half_rows // TILES
    width = patch_len // groups
    half = patch_len // 2
    fold_z = lax.rem(lax.rem(lane_of((TILES, patch_len)), width), stride)
    row_group = lax.broadcasted_iota(jnp.int32, (half_rows, patch_len), 0) // TILES
    lower_y = lane_of((half_rows, patch_len)) < half // 2
    gathered = []
    for step in (regions - 1, 1):
        other = lax.rem(region + step, regions)

        def columns(source, slab):
            base = (other * slabs + lax.rem(slab + slabs, slabs)) * (TILES * ROWS)
            return source[pl.ds(base + 3, TILES, stride=ROWS), :]

        total = jnp.zeros((half_rows, patch_len), jnp.float32)
        for part, (direct, across) in enumerate(((arrived, relayed), (relayed, arrived))):
            merged = columns(direct, depth)
            merged = jnp.where(fold_z == 0, columns(across, depth - 1), merged)
            merged = jnp.where(fold_z == slab_len + 1, columns(across, depth + 1), merged)
            merged = jnp.concatenate([merged] * groups, axis=0)
            for g in range(groups):
                here = (row_group == g) & (lower_y if part == 0 else ~lower_y)
                shift = part * (half // 2) - g * width
                total = jnp.where(here, roll(merged, shift, 1), total)
        gathered.append(total)
    from_left, from_right = gathered
    own_last = own_columns[0]
    own_first = own_columns[1]
    shape = (half_rows, patch_len)
    lane = lane_of(shape)
    row = lax.broadcasted_iota(jnp.int32, shape, 0)
    first_row, last_row = row == 0, row == half_rows - 1
    first_side = lane < half
    quarter = half // 2
    z_cell = lax.rem(lane, quarter)
    row_y = row + jnp.where(lax.rem(lane, half) >= quarter, half_rows, 0)

    def at_y(value, step):
        return shift_y(value, step, quarter, first_row, last_row)

    z_global = depth * slab_len + z_cell - 1
    valid = (z_cell <= slab_len) & (z_global >= 0) & (z_global <= slab_len * slabs - 2)
    valid = valid & (row_y < width_y - 1)

    low_x = [
        jnp.where(
            first_side, roll(from_left, -c * stride, 1), roll(own_last, half - c * stride, 1)
        )
        for c in range(5)
    ]
    high_x = [
        jnp.where(
            first_side, roll(own_first, -c * stride, 1), roll(from_right, half - c * stride, 1)
        )
        for c in range(3)
    ]
    growth = jnp.where(valid, low_x[3], 1.0)
    scale = jnp.where(valid, low_x[4] * REST_VOLUME, 0.0) * growth
    corner = {}
    for c in range(3):
        for dx, base in ((0, low_x[c]), (1, high_x[c])):
            up = roll(base, -1, 1)
            corner[(c, 0, 0, dx)] = base
            corner[(c, 0, 1, dx)] = at_y(base, -1)
            corner[(c, 1, 0, dx)] = up
            corner[(c, 1, 1, dx)] = at_y(up, -1)
    edges = {}
    for one in range(2):
        for two in range(2):
            for axis, start in ((0, (one, two, 0)), (1, (one, 0, two)), (2, (0, one, two))):
                end = tuple(a + b for a, b in zip(start, unit(axis)))
                edges[(axis, start)] = [corner[(c, *end)] - corner[(c, *start)] for c in range(3)]
    pulls = tensions(edges, growth, scale, scale * growth)
    forces = []
    for c in range(3):

        def chosen(axis, one):
            at = ((one, 0, 0), (one, 0, 1)) if axis == 1 else ((0, one, 0), (0, one, 1))
            return jnp.where(first_side, pulls[(axis, at[1])][c], pulls[(axis, at[0])][c])

        level = []
        for dz in range(2):
            both = pulls[(0, (dz, 0, 0))][c] + at_y(pulls[(0, (dz, 1, 0))][c], 1)
            both = jnp.where(first_side, -both, both)
            along_y = chosen(1, dz)
            level.append(both + (along_y - at_y(along_y, 1)))
        along_z = chosen(2, 0) + at_y(chosen(2, 1), 1)
        forces.append((level[0] + along_z) + roll(level[1] - along_z, 1, 1))
    return forces


def far_points(dims, source, chosen, tiles):
    slab_len, width_y, patch_len, regions, slabs, pairs = dims
    depth = slab_index()
    half = patch_len // 2
    tall = TILES * ROWS

    def take(m):
        rows = pl.ds(pl.multiple_of((m * slabs + depth) * tall, tall), tall)
        tiles[pl.ds(pl.multiple_of(m * tall, tall), tall), :] = source[rows, :]

    each(regions, take, 16)
    if chosen is None:
        chosen = yield
    lane = lane_of((pairs, patch_len))
    for c in range(3):
        value = picked(chosen, tiles[pl.ds(c, regions * TILES, stride=ROWS), :], 1)
        value = jnp.where(lane < half, value[:pairs], value[pairs:])
        yield value + roll(value, half, 1)


def tile_choice(dims, slots, tiles):
    slab_len, width_y, patch_len, regions, slabs, pairs = dims
    half = patch_len // 2
    rows = regions * TILES
    found = tiles[pl.ds(3, rows, stride=ROWS), :]
    wide = max(pairs, patch_len)
    labels = [
        jnp.broadcast_to(found[:, side * half + half - 1 : side * half + half], (rows, wide))
        for side in range(2)
    ]
    row = lax.broadcasted_iota(jnp.int32, (rows, wide), 0)
    upper = lax.rem(row, TILES) > 0
    others = [jnp.where(upper, roll(label, 1, 0), roll(label, -1, 0)) for label in labels]
    again = [
        upper & (others[0] == labels[0]),
        (labels[1] == labels[0])
        | (labels[1] == others[0])
        | (upper & (others[1] == labels[1])),
    ]
    region_row = lax.broadcasted_iota(jnp.int32, (rows, pairs), 0) // TILES
    named = slots[0, 2].astype(jnp.float32)
    chosen = []
    for label, repeated in zip(labels, again):
        label = jnp.where(repeated, -1.0, label)[:, 0:pairs]
        chosen.append(jnp.where((region_row == slots[0, 1]) & (label == named), 1.0, 0.0))
    return jnp.concatenate([jnp.transpose(value) for value in chosen], axis=0)


def contact_half(dims, near, far, part, write):
    slab_len, width_y, patch_len, regions, slabs, pairs = dims
    half = patch_len // 2
    block = 8
    along = lax.rem(lane_of((block, patch_len)), half) + part * half
    along = along.astype(jnp.float32)

    def some(start):
        rows = pl.ds(start, block)
        mine = [near[c, rows, :] for c in range(3)]
        theirs = [far[c, rows, :] for c in range(3)]
        theirs = [(theirs[0] + along) * ROOT, theirs[1] * ROOT, theirs[2] * ROOT]
        starts = range(0, half, half // NEAR_TURNS)
        turned = [[roll(value, -a, 1) for value in mine] for a in starts]
        sums = [[None] * 3 for _ in starts]
        for b in range(half // NEAR_TURNS):
            other = [roll(value, b, 1) for value in theirs]
            for total, here in zip(sums, turned):
                delta = [here[c] - other[c] for c in range(3)]
                square = delta[0] * delta[0] + delta[1] * delta[1] + delta[2] * delta[2]
                weight = jnp.exp2(-square)
                for c in range(3):
                    total[c] = add(total[c], delta[c] * weight)
        for c in range(3):
            total = None
            for a, sum_a in zip(starts, sums):
                total = add(total, roll(sum_a[c], a, 1))
            write(c, rows, total)

    each(pairs // block, lambda step: some(step * block), 2)


def contact_kernel(
    dims, arrived, near, slots, before, lowest, highest, selector, chosen, moved, far, tiles, pushes
):
    points = far_points(dims, arrived, None, tiles)
    next(points)
    chosen[...] = tile_choice(dims, slots, tiles)
    far[0] = points.send(chosen[...])
    far[1] = next(points)
    far[2] = next(points)

    def write(c, rows, total):
        pushes[c, rows, :] = total

    contact_half(dims, near, far, 0, write)
    slab_len, width_y, patch_len, regions, slabs, pairs = dims
    for c in range(3):
        push = picked(selector[...], pushes[c], 1) * (1.0 / ROOT)
        for z in range(slab_len):
            force = push[z * width_y : (z + 1) * width_y, :]
            if z == 0:
                force = force + lowest[c]
            if z == slab_len - 1:
                force = force + highest[c]
            moved[z, c] = before[z, c] + STEP_TIME * force


def finish_kernel(
    dims,
    arrived,
    relayed,
    moved,
    near,
    chosen,
    own_columns,
    disp,
    selector,
    new_velocity,
    new_disp,
    far,
    tiles,
    total_push,
):
    slab_len, width_y, patch_len, regions, slabs, pairs = dims
    half = patch_len // 2
    borders = border_forces(dims, arrived, relayed, own_columns)
    for c, value in enumerate(far_points(dims, relayed, chosen[...], tiles)):
        far[c] = value

    def write(c, rows, total):
        total_push[c, rows, :] = total

    contact_half(dims, near, far, 1, write)
    half_rows = width_y // 2
    lane = lane_of((half_rows, patch_len))
    last = patch_len - 1
    for c in range(3):
        push = picked(selector[...], total_push[c], 1) * (1.0 / ROOT)
        edge = borders[c]
        for z in range(slab_len):
            for part in range(2):
                at = part * (half // 2) + z + 1
                rows = slice(part * half_rows, (part + 1) * half_rows)
                start = z * width_y + part * half_rows
                force = push[start : start + half_rows, :]
                force = force + jnp.where(lane == 0, roll(edge, -at, 1), 0.0)
                force = force + jnp.where(lane == last, roll(edge, last - half - at, 1), 0.0)
                speed = moved[z, c, rows, :] + STEP_TIME * force
                new_velocity[z, c, rows, :] = speed
                new_disp[z, c, rows, :] = disp[z, c, rows, :] + STEP_TIME * speed


def local(displacement, velocity, growth, shear_modulus, pair_slots, pair_count, separation):
    slab_len, width_y, _, patch_len = displacement.shape
    regions = lax.axis_size("region")
    slabs = lax.axis_size("pair") * lax.axis_size("core")
    pairs = pair_slots.shape[3]
    dims = (slab_len, width_y, patch_len, regions, slabs, pairs)
    f32 = jnp.float32
    i32 = jnp.int32
    disp = jnp.transpose(displacement, (0, 2, 1, 3))
    speed = jnp.transpose(velocity, (0, 2, 1, 3))
    slots = jnp.transpose(pair_slots, (0, 2, 1, 3))
    apart = jnp.transpose(separation, (0, 2, 1, 3))
    plane = (width_y, patch_len)

    packet, face_a, face_b = pl.pallas_call(
        functools.partial(pack_kernel, dims),
        out_shape=(
            jax.ShapeDtypeStruct((regions * slabs * TILES * ROWS, patch_len), f32),
            jax.ShapeDtypeStruct((5, *plane), f32),
            jax.ShapeDtypeStruct((5, *plane), f32),
        ),
        in_specs=[HBM] * 4,
        out_specs=(VMEM, VMEM, VMEM),
        scratch_shapes=[
            pltpu.VMEM(((slab_len * 3 + ROWS) * width_y, patch_len), f32),
            pltpu.VMEM((slab_len, *plane), f32),
            pltpu.VMEM((slab_len, *plane), f32),
            pltpu.SMEM(slots.shape, i32),
            pltpu.SMEM((regions,), i32),
            pltpu.VMEM((2, *plane), f32),
            pltpu.SemaphoreType.DMA((4,)),
        ],
        name="pack",
    )(disp.reshape(slab_len * 3 * width_y, patch_len), growth, shear_modulus, slots)

    links = [[(i, i + 1) for i in range(first, slabs - 1, 2)] for first in (0, 1)]
    links = [link + [(b, a) for a, b in link] for link in links]
    face_a = lax.ppermute(face_a, ("pair", "core"), links[0])
    face_b = lax.ppermute(face_b, ("pair", "core"), links[1])

    packet, pair_count = lax.optimization_barrier((packet, pair_count))
    arrived = lax.all_to_all(packet, ("region", "pair", "core"), 0, 0, tiled=True)

    before, near, selector = pl.pallas_call(
        functools.partial(inner_kernel, dims),
        out_shape=(
            jax.ShapeDtypeStruct((slab_len, 3, *plane), f32),
            jax.ShapeDtypeStruct((3, pairs, patch_len), f32),
            jax.ShapeDtypeStruct((slab_len * width_y, pairs), f32),
        ),
        in_specs=[VMEM] * 4 + [SMEM, VMEM, SMEM, SMEM],
        out_specs=(VMEM,) * 3,
        compiler_params=PARAMS,
        name="inner",
        cost_estimate=pl.CostEstimate(flops=4000 * 1024, bytes_accessed=1 << 20, transcendentals=0),
    )(disp, growth, shear_modulus, speed, slots, slots, pair_count, apart)

    lowest, highest, own_columns = pl.pallas_call(
        functools.partial(outer_kernel, dims),
        out_shape=(
            jax.ShapeDtypeStruct((3, *plane), f32),
            jax.ShapeDtypeStruct((3, *plane), f32),
            jax.ShapeDtypeStruct((2, width_y // 2, patch_len), f32),
        ),
        in_specs=[VMEM] * 5,
        out_specs=(VMEM,) * 3,
        compiler_params=PARAMS,
        name="outer",
        cost_estimate=pl.CostEstimate(flops=2000 * 1024, bytes_accessed=1 << 20, transcendentals=0),
    )(disp, growth, shear_modulus, face_a, face_b)

    arrived, before, lowest = lax.optimization_barrier((arrived, before, lowest))
    relayed = lax.ppermute(arrived, ("pair", "core"), links[0])

    tile_rows = regions * TILES
    chosen, moved = pl.pallas_call(
        functools.partial(contact_kernel, dims),
        out_shape=(
            jax.ShapeDtypeStruct((2 * pairs, tile_rows), f32),
            jax.ShapeDtypeStruct((slab_len, 3, *plane), f32),
        ),
        in_specs=[VMEM] * 7,
        out_specs=(VMEM,) * 2,
        scratch_shapes=[
            pltpu.VMEM((3, pairs, patch_len), f32),
            pltpu.VMEM((tile_rows * ROWS, patch_len), f32),
            pltpu.VMEM((3, pairs, patch_len), f32),
        ],
        compiler_params=PARAMS,
        name="contact",
        cost_estimate=pl.CostEstimate(flops=6000 * 1024, bytes_accessed=1 << 20, transcendentals=0),
    )(arrived, near, slots, before, lowest, highest, selector)

    new_velocity, new_disp = pl.pallas_call(
        functools.partial(finish_kernel, dims),
        out_shape=(
            jax.ShapeDtypeStruct((slab_len, 3, *plane), f32),
            jax.ShapeDtypeStruct((slab_len, 3, *plane), f32),
        ),
        in_specs=[VMEM] * 8,
        out_specs=(VMEM, VMEM),
        scratch_shapes=[
            pltpu.VMEM((3, pairs, patch_len), f32),
            pltpu.VMEM((tile_rows * ROWS, patch_len), f32),
            pltpu.VMEM((3, pairs, patch_len), f32),
        ],
        compiler_params=PARAMS,
        name="finish",
    )(
        arrived,
        relayed,
        moved,
        near,
        chosen,
        own_columns,
        disp,
        selector,
    )
    order = (0, 2, 1, 3)
    return jnp.transpose(new_velocity, order), jnp.transpose(new_disp, order)


def solution(mesh):
    shape = dict(mesh.shape)
    devices = mesh.devices.reshape(shape["region"], shape["depth"] // 2, 2)
    fine = Mesh(devices, ("region", "pair", "core"))
    depth = ("pair", "core")
    in_specs = (
        P(depth, None, None, "region"),
        P(depth, None, None, "region"),
        P(depth, None, "region"),
        P(depth, None, "region"),
        P(depth, "region", None, None),
        P(depth, "region"),
        P(depth, "region", None, None),
    )
    out_specs = (P(depth, None, None, "region"), P(depth, None, None, "region"))
    return jax.shard_map(local, mesh=fine, in_specs=in_specs, out_specs=out_specs, check_vma=False)
```

```python
import functools
import math

import jax
import jax.numpy as jnp
from jax import lax
from jax.experimental import pallas as pl
from jax.experimental.pallas import tpu as pltpu
from jax.sharding import Mesh
from jax.sharding import PartitionSpec as P

CAP = 4
STEP_TIME = 0.2
REST_VOLUME = 1.0 / 6.0
PERMUTATIONS = ((0, 1, 2), (0, 2, 1), (1, 0, 2), (1, 2, 0), (2, 0, 1), (2, 1, 0))
ROWS = 4
TILES = CAP // 2

VMEM = pl.BlockSpec(memory_space=pltpu.VMEM)
SMEM = pl.BlockSpec(memory_space=pltpu.SMEM)
HBM = pl.BlockSpec(memory_space=pltpu.HBM)
PARAMS = pltpu.CompilerParams(vmem_limit_bytes=16 << 20)
NEAR_TURNS = 32
ROOT = math.sqrt(math.log2(math.e))


def add(total, term):
    return term if total is None else total + term


def unit(axis):
    return tuple(1 if position == 2 - axis else 0 for position in range(3))


def tensions(edges, growth, scale_side, scale_up):
    inverse = 1.0 / growth
    columns = {}
    for (axis, start), rows in edges.items():
        made = []
        for row in range(3):
            value = rows[row] + 1.0 if row == axis else rows[row]
            made.append(value * inverse if axis < 2 else value)
        columns[(axis, start)] = made
    pulls = {}
    for first, second, third in PERMUTATIONS:
        middle = unit(first)
        upper = tuple(a + b for a, b in zip(middle, unit(second)))
        keys = {first: (first, (0, 0, 0)), second: (second, middle), third: (third, upper)}
        fe = [[columns[keys[col]][row] for col in range(3)] for row in range(3)]
        cof = [
            [
                fe[(row + 1) % 3][(col + 1) % 3] * fe[(row + 2) % 3][(col + 2) % 3]
                - fe[(row + 1) % 3][(col + 2) % 3] * fe[(row + 2) % 3][(col + 1) % 3]
                for col in range(3)
            ]
            for row in range(3)
        ]
        jacobian = fe[0][0] * cof[0][0] + fe[0][1] * cof[0][1] + fe[0][2] * cof[0][2]
        pressure = 4.0 * jacobian - 5.0
        for col in range(3):
            key = keys[col]
            for row in range(3):
                pulls.setdefault(key, [None] * 3)
                pulls[key][row] = add(pulls[key][row], fe[row][col] + pressure * cof[row][col])
    return {
        key: [value * (scale_side if key[0] < 2 else scale_up) for value in rows]
        for key, rows in pulls.items()
    }


def roll(value, shift, axis):
    size = value.shape[axis]
    shift = shift % size
    return value if shift == 0 else pltpu.roll(value, shift, axis)


def lane_of(shape):
    return lax.broadcasted_iota(jnp.int32, shape, len(shape) - 1)


def column_pack(fields, lane_from, stride, offset):
    shape = fields[0][0].shape
    lane = lane_of(shape)
    packed = jnp.zeros(shape, jnp.float32)
    for c, layers in enumerate(fields):
        for z, field in enumerate(layers):
            to = c * stride + z + offset
            packed = jnp.where(lane == to, roll(field, to - lane_from, 1), packed)
    return packed


def each(count, body, unrolled):
    if count <= unrolled:
        for index in range(count):
            body(index)
    else:

        def one(index, carry):
            body(index)
            return carry

        lax.fori_loop(0, count, one, 0)


def split(value, size):
    if size & (size - 1):
        return lax.div(value, size), lax.rem(value, size)
    return lax.shift_right_logical(value, size.bit_length() - 1), lax.bitwise_and(value, size - 1)


def slab_index():
    return lax.axis_index("pair") * lax.axis_size("core") + lax.axis_index("core")


def thirds(value):
    high = value.astype(jnp.bfloat16)
    rest = value - high.astype(jnp.float32)
    middle = rest.astype(jnp.bfloat16)
    low = (rest - middle.astype(jnp.float32)).astype(jnp.bfloat16)
    return high, middle, low


def picked(chosen, value, contract):
    chosen = chosen.astype(jnp.bfloat16)
    total = None
    for part in thirds(value):
        term = lax.dot_general(
            chosen,
            part,
            (((contract,), (0,)), ((), ())),
            preferred_element_type=jnp.float32,
        )
        total = add(total, term)
    return total


def shift_y(value, step, half_lanes, first_row, last_row):
    moved = roll(value, step, 0)
    return jnp.where(
        first_row if step > 0 else last_row, roll(moved, step * half_lanes, 1), moved
    )


def pack_kernel(
    dims,
    disp_in,
    growth_in,
    shear_in,
    slots_in,
    packet,
    face_a,
    face_b,
    disp,
    growth,
    shear,
    slots,
    counted,
    face,
    sems,
):
    slab_len, width_y, patch_len, regions, slabs, pairs = dims
    region = lax.axis_index("region")
    depth = slab_index()
    core = lax.axis_index("core")
    partner = depth + 1 - 2 * core
    stride = slab_len + 2
    half = patch_len // 2
    moves = [
        pltpu.make_async_copy(source, target, sems.at[index])
        for index, (source, target) in enumerate(
            (
                (slots_in, slots),
                (disp_in, disp.at[0 : slab_len * 3 * width_y]),
                (growth_in, growth),
                (shear_in, shear),
            )
        )
    ]
    for move in moves:
        move.start()
    tall = TILES * ROWS
    span = 1 << pairs.bit_length()
    blank = jnp.zeros((tall, patch_len), jnp.float32)

    def base_of(m, slab):
        return pl.multiple_of((m * slabs + slab) * tall, tall)

    def clear(m):
        counted[m] = m * (slabs * tall * span)
        packet[pl.ds(base_of(m, depth), tall), :] = blank
        packet[pl.ds(base_of(m, partner), tall), :] = blank

    disp[slab_len * 3 * width_y :, :] = jnp.zeros((ROWS * width_y, patch_len), jnp.float32)
    spare = region * (slabs * tall)
    each(regions, clear, 16)
    for move in moves:
        move.wait()

    tile_row = lax.broadcasted_iota(jnp.int32, (ROWS, patch_len), 0)

    lane = lane_of((ROWS, patch_len))

    def place(k):
        own, other = slots[0, 0, 0, k], slots[0, 1, 0, k]
        state = counted[other]
        counted[other] = state + 1
        first, position = split(state, span)
        fits = position < CAP
        first = jnp.where(fits, first, spare)
        side, offset = split(jnp.where(fits, position, 0), TILES)
        first = first + offset * ROWS
        z, y = split(own, width_y)
        tile = disp[pl.ds(z * (3 * width_y) + y, ROWS, stride=width_y), :]
        label = jnp.full((ROWS, patch_len), own, jnp.int32).astype(jnp.float32)
        tile = jnp.where(tile_row == 3, label, tile)
        turned = roll(tile, half, 1)
        mask = (lane >= half) == (side > 0)
        for slab, value in (
            (depth, jnp.where(lane < half, tile, turned)),
            (partner, jnp.where(lane < half, turned, tile)),
        ):
            base = pl.multiple_of(first + slab * tall, ROWS)
            pltpu.store(packet.at[pl.ds(base, ROWS), :], value, mask=mask)

    each(pairs, place, 16)

    even = lax.rem(depth, 2) == 0
    last = slab_len - 1
    for out, from_z in ((face_a, jnp.where(even, last, 0)), (face_b, jnp.where(even, 0, last))):
        for c in range(3):
            start = pl.multiple_of((from_z * 3 + c) * width_y, width_y)
            out[c] = disp[pl.ds(start, width_y), :]
        out[3] = growth[last]
        out[4] = shear[last]

    half_rows = width_y // 2
    groups = half_rows // TILES
    width = patch_len // groups

    def plane(z, c):
        start = (z * 3 + c) * width_y
        return disp[start : start + width_y, :]

    fields = [[plane(z, c) for z in range(slab_len)] for c in range(3)]
    fields = fields + [[growth[z] for z in range(slab_len)], [shear[z] for z in range(slab_len)]]
    sides = ((patch_len - 1, fields, 1), (0, fields[:3], regions - 1))
    lane = lane_of((TILES, patch_len))
    for side, (lane_from, chosen, step) in enumerate(sides):
        ringed = [[layers[-1]] + layers + [layers[0]] for layers in chosen]
        face[side] = column_pack(ringed, lane_from, stride, 0)
        folded = []
        for part in range(2):
            value = jnp.zeros((TILES, patch_len), jnp.float32)
            for g in range(groups):
                start = part * half_rows + g * TILES
                rows = roll(face[side, start : start + TILES, :], g * width, 1)
                value = jnp.where((lane >= g * width) & (lane < (g + 1) * width), rows, value)
            folded.append(value)
        other = lax.rem(region + step, regions)
        for slab in range(slabs):
            value = jnp.where(core == slab % 2, folded[0], folded[1])
            rows = pl.ds(base_of(other, slab) + 3, TILES, stride=ROWS)
            packet[rows, :] = jnp.where(lax.rem(lane, half) == half - 1, packet[rows, :], value)


def layer_edges(layer):
    along_x, along_y, moved = {}, {}, {}
    for c in range(3):
        base = layer[c]
        next_x = roll(base, -1, 1)
        next_y = roll(base, -1, 0)
        next_xy = roll(next_y, -1, 1)
        moved[c] = {(0, 0): base, (0, 1): next_x, (1, 0): next_y, (1, 1): next_xy}
        along_x[c] = {0: next_x - base, 1: next_xy - next_y}
        along_y[c] = {0: next_y - base, 1: next_xy - next_x}
    return along_x, along_y, moved


def cell_layer(low, high, growth, shear, valid):
    edges = {}
    for dz, (along_x, along_y, _) in enumerate((low, high)):
        for other in range(2):
            edges[(0, (dz, other, 0))] = [along_x[c][other] for c in range(3)]
            edges[(1, (dz, 0, other))] = [along_y[c][other] for c in range(3)]
    for dy in range(2):
        for dx in range(2):
            edges[(2, (0, dy, dx))] = [
                high[2][c][(dy, dx)] - low[2][c][(dy, dx)] for c in range(3)
            ]
    scale = jnp.where(valid, shear * REST_VOLUME, 0.0) * growth
    pulls = tensions(edges, growth, scale, scale * growth)
    levels = []
    for dz in range(2):
        level = []
        for c in range(3):
            pull_x = pulls[(0, (dz, 0, 0))][c] + roll(pulls[(0, (dz, 1, 0))][c], 1, 0)
            pull_y = pulls[(1, (dz, 0, 0))][c] + roll(pulls[(1, (dz, 0, 1))][c], 1, 1)
            level.append((pull_x - roll(pull_x, 1, 1)) + (pull_y - roll(pull_y, 1, 0)))
        levels.append(level)
    for c in range(3):
        at_zero = pulls[(2, (0, 0, 0))][c] + roll(pulls[(2, (0, 1, 0))][c], 1, 0)
        at_one = pulls[(2, (0, 0, 1))][c] + roll(pulls[(2, (0, 1, 1))][c], 1, 0)
        pull_z = at_zero + roll(at_one, 1, 1)
        levels[0][c] = levels[0][c] + pull_z
        levels[1][c] = levels[1][c] - pull_z
    return levels


def inner_cells(width_y, patch_len):
    shape = (width_y, patch_len)
    row_y = lax.broadcasted_iota(jnp.int32, shape, 0)
    return (lane_of(shape) < patch_len - 1) & (row_y < width_y - 1)


def inner_kernel(
    dims,
    disp,
    growth,
    shear,
    velocity,
    slots,
    slot_row,
    count,
    separation,
    before,
    near,
    selector,
):
    slab_len, width_y, patch_len, regions, slabs, pairs = dims
    inside = inner_cells(width_y, patch_len)
    forces = [[None] * 3 for _ in range(slab_len)]
    low = layer_edges([disp[0, c] for c in range(3)])
    for z in range(slab_len - 1):
        high = layer_edges([disp[z + 1, c] for c in range(3)])
        levels = cell_layer(low, high, growth[z], shear[z], inside)
        low = high
        for dz in range(2):
            for c in range(3):
                forces[z + dz][c] = add(forces[z + dz][c], levels[dz][c])
        for c in range(3):
            before[z, c] = velocity[z, c] + STEP_TIME * forces[z][c]
    for c in range(3):
        before[slab_len - 1, c] = velocity[slab_len - 1, c] + STEP_TIME * forces[slab_len - 1][c]

    along = lane_of((1, patch_len)).astype(jnp.float32)

    def fetch(k):
        z, y = split(slots[0, 0, 0, k], width_y)
        for c in range(3):
            point = disp[z, c, pl.ds(y, 1), :]
            if c == 0:
                point = point + along
            near[0, c, pl.ds(k, 1), :] = (point - separation[0, c, 0, k]) * ROOT

    each(pairs, fetch, 16)
    for c in range(3):
        value = near[0, c]
        for turn in range(1, NEAR_TURNS):
            near[turn, c] = roll(value, -turn * (patch_len // 2 // NEAR_TURNS), 1)
    patch_row = lax.broadcasted_iota(jnp.int32, selector.shape, 0)
    live = lax.broadcasted_iota(jnp.int32, selector.shape, 1) < count[0, 0]
    selector[...] = jnp.where((patch_row == slot_row[0, 0]) & live, 1.0, 0.0)


def outer_kernel(dims, disp, growth, shear, face_a, face_b, lowest, highest, own_columns):
    slab_len, width_y, patch_len, regions, slabs, pairs = dims
    depth = slab_index()
    inside = inner_cells(width_y, patch_len)
    even = lax.rem(depth, 2) == 0
    below = [jnp.where(even, face_b[c], face_a[c]) for c in range(5)]
    above = [jnp.where(even, face_a[c], face_b[c]) for c in range(3)]
    has_below = depth > 0
    last = slab_len - 1
    below_growth = jnp.where(has_below, below[3], 1.0)
    first_nodes = [disp[0, c] for c in range(3)]
    last_nodes = [disp[last, c] for c in range(3)]
    low, high = layer_edges(below[0:3]), layer_edges(first_nodes)
    levels = cell_layer(low, high, below_growth, below[4], inside & has_below)
    for c in range(3):
        lowest[c] = levels[1][c]
    low, high = layer_edges(last_nodes), layer_edges(above)
    levels = cell_layer(low, high, growth[last], shear[last], inside & (depth < slabs - 1))
    for c in range(3):
        highest[c] = levels[0][c]

    half_rows = width_y // 2
    stride = slab_len + 2
    lane_half = lane_of((half_rows, patch_len)) < patch_len // 4
    side_fields = [
        [below[c]] + [disp[z, c] for z in range(slab_len)] + [above[c]] for c in range(3)
    ]
    cell_fields = [
        [below_growth] + [growth[z] for z in range(slab_len)],
        [below[4]] + [shear[z] for z in range(slab_len)],
    ]
    for side, (chosen, lane_from) in enumerate(
        ((side_fields + cell_fields, patch_len - 1), (side_fields, 0))
    ):
        column = column_pack(chosen, lane_from, stride, 0)
        upper = roll(column[half_rows:], patch_len // 4, 1)
        own_columns[side] = jnp.where(lane_half, column[:half_rows], upper)


def border_forces(dims, arrived, relayed, own_columns):
    slab_len, width_y, patch_len, regions, slabs, pairs = dims
    region = lax.axis_index("region")
    depth = slab_index()
    stride = slab_len + 2
    half_rows = width_y // 2
    groups = half_rows // TILES
    width = patch_len // groups
    half = patch_len // 2
    fold_z = lax.rem(lax.rem(lane_of((TILES, patch_len)), width), stride)
    row_group = lax.broadcasted_iota(jnp.int32, (half_rows, patch_len), 0) // TILES
    lower_y = lane_of((half_rows, patch_len)) < half // 2
    gathered = []
    for step in (regions - 1, 1):
        other = lax.rem(region + step, regions)

        def columns(source, slab):
            base = (other * slabs + lax.rem(slab + slabs, slabs)) * (TILES * ROWS)
            return source[pl.ds(base + 3, TILES, stride=ROWS), :]

        total = jnp.zeros((half_rows, patch_len), jnp.float32)
        for part, (direct, across) in enumerate(((arrived, relayed), (relayed, arrived))):
            merged = columns(direct, depth)
            merged = jnp.where(fold_z == 0, columns(across, depth - 1), merged)
            merged = jnp.where(fold_z == slab_len + 1, columns(across, depth + 1), merged)
            merged = jnp.concatenate([merged] * groups, axis=0)
            for g in range(groups):
                here = (row_group == g) & (lower_y if part == 0 else ~lower_y)
                shift = part * (half // 2) - g * width
                total = jnp.where(here, roll(merged, shift, 1), total)
        gathered.append(total)
    from_left, from_right = gathered
    own_last = own_columns[0]
    own_first = own_columns[1]
    shape = (half_rows, patch_len)
    lane = lane_of(shape)
    row = lax.broadcasted_iota(jnp.int32, shape, 0)
    first_row, last_row = row == 0, row == half_rows - 1
    first_side = lane < half
    quarter = half // 2
    z_cell = lax.rem(lane, quarter)
    row_y = row + jnp.where(lax.rem(lane, half) >= quarter, half_rows, 0)

    def at_y(value, step):
        return shift_y(value, step, quarter, first_row, last_row)

    z_global = depth * slab_len + z_cell - 1
    valid = (z_cell <= slab_len) & (z_global >= 0) & (z_global <= slab_len * slabs - 2)
    valid = valid & (row_y < width_y - 1)

    low_x = [
        jnp.where(
            first_side, roll(from_left, -c * stride, 1), roll(own_last, half - c * stride, 1)
        )
        for c in range(5)
    ]
    high_x = [
        jnp.where(
            first_side, roll(own_first, -c * stride, 1), roll(from_right, half - c * stride, 1)
        )
        for c in range(3)
    ]
    growth = jnp.where(valid, low_x[3], 1.0)
    scale = jnp.where(valid, low_x[4] * REST_VOLUME, 0.0) * growth
    corner = {}
    for c in range(3):
        for dx, base in ((0, low_x[c]), (1, high_x[c])):
            up = roll(base, -1, 1)
            corner[(c, 0, 0, dx)] = base
            corner[(c, 0, 1, dx)] = at_y(base, -1)
            corner[(c, 1, 0, dx)] = up
            corner[(c, 1, 1, dx)] = at_y(up, -1)
    edges = {}
    for one in range(2):
        for two in range(2):
            for axis, start in ((0, (one, two, 0)), (1, (one, 0, two)), (2, (0, one, two))):
                end = tuple(a + b for a, b in zip(start, unit(axis)))
                edges[(axis, start)] = [corner[(c, *end)] - corner[(c, *start)] for c in range(3)]
    pulls = tensions(edges, growth, scale, scale * growth)
    forces = []
    for c in range(3):

        def chosen(axis, one):
            at = ((one, 0, 0), (one, 0, 1)) if axis == 1 else ((0, one, 0), (0, one, 1))
            return jnp.where(first_side, pulls[(axis, at[1])][c], pulls[(axis, at[0])][c])

        level = []
        for dz in range(2):
            both = pulls[(0, (dz, 0, 0))][c] + at_y(pulls[(0, (dz, 1, 0))][c], 1)
            both = jnp.where(first_side, -both, both)
            along_y = chosen(1, dz)
            level.append(both + (along_y - at_y(along_y, 1)))
        along_z = chosen(2, 0) + at_y(chosen(2, 1), 1)
        forces.append((level[0] + along_z) + roll(level[1] - along_z, 1, 1))
    return forces


def far_points(dims, source, chosen, tiles):
    slab_len, width_y, patch_len, regions, slabs, pairs = dims
    depth = slab_index()
    half = patch_len // 2
    tall = TILES * ROWS

    def take(m):
        rows = pl.ds(pl.multiple_of((m * slabs + depth) * tall, tall), tall)
        tiles[pl.ds(pl.multiple_of(m * tall, tall), tall), :] = source[rows, :]

    each(regions, take, 16)
    if chosen is None:
        chosen = yield
    lane = lane_of((pairs, patch_len))
    for c in range(3):
        value = picked(chosen, tiles[pl.ds(c, regions * TILES, stride=ROWS), :], 1)
        value = jnp.where(lane < half, value[:pairs], value[pairs:])
        yield value + roll(value, half, 1)


def tile_choice(dims, slots, tiles):
    slab_len, width_y, patch_len, regions, slabs, pairs = dims
    half = patch_len // 2
    rows = regions * TILES
    found = tiles[pl.ds(3, rows, stride=ROWS), :]
    wide = max(pairs, patch_len)
    labels = [
        jnp.broadcast_to(found[:, side * half + half - 1 : side * half + half], (rows, wide))
        for side in range(2)
    ]
    row = lax.broadcasted_iota(jnp.int32, (rows, wide), 0)
    upper = lax.rem(row, TILES) > 0
    others = [jnp.where(upper, roll(label, 1, 0), roll(label, -1, 0)) for label in labels]
    again = [
        upper & (others[0] == labels[0]),
        (labels[1] == labels[0])
        | (labels[1] == others[0])
        | (upper & (others[1] == labels[1])),
    ]
    region_row = lax.broadcasted_iota(jnp.int32, (rows, pairs), 0) // TILES
    named = slots[0, 2].astype(jnp.float32)
    chosen = []
    for label, repeated in zip(labels, again):
        label = jnp.where(repeated, -1.0, label)[:, 0:pairs]
        chosen.append(jnp.where((region_row == slots[0, 1]) & (label == named), 1.0, 0.0))
    return jnp.concatenate([jnp.transpose(value) for value in chosen], axis=0)


def contact_half(dims, near, far, part, write):
    slab_len, width_y, patch_len, regions, slabs, pairs = dims
    half = patch_len // 2
    block = 8
    along = lax.rem(lane_of((block, patch_len)), half) + part * half
    along = along.astype(jnp.float32)

    def some(start):
        rows = pl.ds(start, block)
        theirs = [far[c, rows, :] for c in range(3)]
        theirs = [(theirs[0] + along) * ROOT, theirs[1] * ROOT, theirs[2] * ROOT]
        starts = range(0, half, half // NEAR_TURNS)
        turned = [[near[turn, c, rows, :] for c in range(3)] for turn in range(NEAR_TURNS)]
        sums = [[None] * 3 for _ in starts]
        for b in range(half // NEAR_TURNS):
            other = [roll(value, b, 1) for value in theirs]
            for total, here in zip(sums, turned):
                delta = [here[c] - other[c] for c in range(3)]
                square = delta[0] * delta[0] + delta[1] * delta[1] + delta[2] * delta[2]
                weight = jnp.exp2(-square)
                for c in range(3):
                    total[c] = add(total[c], delta[c] * weight)
        for c in range(3):
            total = None
            for a, sum_a in zip(starts, sums):
                total = add(total, roll(sum_a[c], a, 1))
            write(c, rows, total)

    each(pairs // block, lambda step: some(step * block), 2)


def contact_kernel(
    dims, arrived, near, slots, before, lowest, highest, selector, chosen, moved, far, tiles, pushes
):
    points = far_points(dims, arrived, None, tiles)
    next(points)
    chosen[...] = tile_choice(dims, slots, tiles)
    far[0] = points.send(chosen[...])
    far[1] = next(points)
    far[2] = next(points)

    def write(c, rows, total):
        pushes[c, rows, :] = total

    contact_half(dims, near, far, 0, write)
    slab_len, width_y, patch_len, regions, slabs, pairs = dims
    for c in range(3):
        push = picked(selector[...], pushes[c], 1) * (1.0 / ROOT)
        for z in range(slab_len):
            force = push[z * width_y : (z + 1) * width_y, :]
            if z == 0:
                force = force + lowest[c]
            if z == slab_len - 1:
                force = force + highest[c]
            moved[z, c] = before[z, c] + STEP_TIME * force


def finish_kernel(
    dims,
    arrived,
    relayed,
    moved,
    near,
    chosen,
    own_columns,
    disp,
    selector,
    new_velocity,
    new_disp,
    far,
    tiles,
    total_push,
):
    slab_len, width_y, patch_len, regions, slabs, pairs = dims
    half = patch_len // 2
    borders = border_forces(dims, arrived, relayed, own_columns)
    for c, value in enumerate(far_points(dims, relayed, chosen[...], tiles)):
        far[c] = value

    def write(c, rows, total):
        total_push[c, rows, :] = total

    contact_half(dims, near, far, 1, write)
    half_rows = width_y // 2
    lane = lane_of((half_rows, patch_len))
    last = patch_len - 1
    for c in range(3):
        push = picked(selector[...], total_push[c], 1) * (1.0 / ROOT)
        edge = borders[c]
        for z in range(slab_len):
            for part in range(2):
                at = part * (half // 2) + z + 1
                rows = slice(part * half_rows, (part + 1) * half_rows)
                start = z * width_y + part * half_rows
                force = push[start : start + half_rows, :]
                force = force + jnp.where(lane == 0, roll(edge, -at, 1), 0.0)
                force = force + jnp.where(lane == last, roll(edge, last - half - at, 1), 0.0)
                speed = moved[z, c, rows, :] + STEP_TIME * force
                new_velocity[z, c, rows, :] = speed
                new_disp[z, c, rows, :] = disp[z, c, rows, :] + STEP_TIME * speed


def local(displacement, velocity, growth, shear_modulus, pair_slots, pair_count, separation):
    slab_len, width_y, _, patch_len = displacement.shape
    regions = lax.axis_size("region")
    slabs = lax.axis_size("pair") * lax.axis_size("core")
    pairs = pair_slots.shape[3]
    dims = (slab_len, width_y, patch_len, regions, slabs, pairs)
    f32 = jnp.float32
    i32 = jnp.int32
    disp = jnp.transpose(displacement, (0, 2, 1, 3))
    speed = jnp.transpose(velocity, (0, 2, 1, 3))
    slots = jnp.transpose(pair_slots, (0, 2, 1, 3))
    apart = jnp.transpose(separation, (0, 2, 1, 3))
    plane = (width_y, patch_len)

    packet, face_a, face_b = pl.pallas_call(
        functools.partial(pack_kernel, dims),
        out_shape=(
            jax.ShapeDtypeStruct((regions * slabs * TILES * ROWS, patch_len), f32),
            jax.ShapeDtypeStruct((5, *plane), f32),
            jax.ShapeDtypeStruct((5, *plane), f32),
        ),
        in_specs=[HBM] * 4,
        out_specs=(VMEM, VMEM, VMEM),
        scratch_shapes=[
            pltpu.VMEM(((slab_len * 3 + ROWS) * width_y, patch_len), f32),
            pltpu.VMEM((slab_len, *plane), f32),
            pltpu.VMEM((slab_len, *plane), f32),
            pltpu.SMEM(slots.shape, i32),
            pltpu.SMEM((regions,), i32),
            pltpu.VMEM((2, *plane), f32),
            pltpu.SemaphoreType.DMA((4,)),
        ],
        name="pack",
    )(disp.reshape(slab_len * 3 * width_y, patch_len), growth, shear_modulus, slots)

    links = [[(i, i + 1) for i in range(first, slabs - 1, 2)] for first in (0, 1)]
    links = [link + [(b, a) for a, b in link] for link in links]
    face_a = lax.ppermute(face_a, ("pair", "core"), links[0])
    face_b = lax.ppermute(face_b, ("pair", "core"), links[1])

    packet, pair_count = lax.optimization_barrier((packet, pair_count))
    arrived = lax.all_to_all(packet, ("region", "pair", "core"), 0, 0, tiled=True)

    before, near, selector = pl.pallas_call(
        functools.partial(inner_kernel, dims),
        out_shape=(
            jax.ShapeDtypeStruct((slab_len, 3, *plane), f32),
            jax.ShapeDtypeStruct((NEAR_TURNS, 3, pairs, patch_len), f32),
            jax.ShapeDtypeStruct((slab_len * width_y, pairs), f32),
        ),
        in_specs=[VMEM] * 4 + [SMEM, VMEM, SMEM, SMEM],
        out_specs=(VMEM,) * 3,
        compiler_params=PARAMS,
        name="inner",
        cost_estimate=pl.CostEstimate(flops=4000 * 1024, bytes_accessed=1 << 20, transcendentals=0),
    )(disp, growth, shear_modulus, speed, slots, slots, pair_count, apart)

    lowest, highest, own_columns = pl.pallas_call(
        functools.partial(outer_kernel, dims),
        out_shape=(
            jax.ShapeDtypeStruct((3, *plane), f32),
            jax.ShapeDtypeStruct((3, *plane), f32),
            jax.ShapeDtypeStruct((2, width_y // 2, patch_len), f32),
        ),
        in_specs=[VMEM] * 5,
        out_specs=(VMEM,) * 3,
        compiler_params=PARAMS,
        name="outer",
        cost_estimate=pl.CostEstimate(flops=2000 * 1024, bytes_accessed=1 << 20, transcendentals=0),
    )(disp, growth, shear_modulus, face_a, face_b)

    arrived, before, lowest = lax.optimization_barrier((arrived, before, lowest))
    relayed = lax.ppermute(arrived, ("pair", "core"), links[0])

    tile_rows = regions * TILES
    chosen, moved = pl.pallas_call(
        functools.partial(contact_kernel, dims),
        out_shape=(
            jax.ShapeDtypeStruct((2 * pairs, tile_rows), f32),
            jax.ShapeDtypeStruct((slab_len, 3, *plane), f32),
        ),
        in_specs=[VMEM] * 7,
        out_specs=(VMEM,) * 2,
        scratch_shapes=[
            pltpu.VMEM((3, pairs, patch_len), f32),
            pltpu.VMEM((tile_rows * ROWS, patch_len), f32),
            pltpu.VMEM((3, pairs, patch_len), f32),
        ],
        compiler_params=PARAMS,
        name="contact",
        cost_estimate=pl.CostEstimate(flops=6000 * 1024, bytes_accessed=1 << 20, transcendentals=0),
    )(arrived, near, slots, before, lowest, highest, selector)

    new_velocity, new_disp = pl.pallas_call(
        functools.partial(finish_kernel, dims),
        out_shape=(
            jax.ShapeDtypeStruct((slab_len, 3, *plane), f32),
            jax.ShapeDtypeStruct((slab_len, 3, *plane), f32),
        ),
        in_specs=[VMEM] * 8,
        out_specs=(VMEM, VMEM),
        scratch_shapes=[
            pltpu.VMEM((3, pairs, patch_len), f32),
            pltpu.VMEM((tile_rows * ROWS, patch_len), f32),
            pltpu.VMEM((3, pairs, patch_len), f32),
        ],
        compiler_params=PARAMS,
        name="finish",
    )(
        arrived,
        relayed,
        moved,
        near,
        chosen,
        own_columns,
        disp,
        selector,
    )
    order = (0, 2, 1, 3)
    return jnp.transpose(new_velocity, order), jnp.transpose(new_disp, order)


def solution(mesh):
    shape = dict(mesh.shape)
    devices = mesh.devices.reshape(shape["region"], shape["depth"] // 2, 2)
    fine = Mesh(devices, ("region", "pair", "core"))
    depth = ("pair", "core")
    in_specs = (
        P(depth, None, None, "region"),
        P(depth, None, None, "region"),
        P(depth, None, "region"),
        P(depth, None, "region"),
        P(depth, "region", None, None),
        P(depth, "region"),
        P(depth, "region", None, None),
    )
    out_specs = (P(depth, None, None, "region"), P(depth, None, None, "region"))
    return jax.shard_map(local, mesh=fine, in_specs=in_specs, out_specs=out_specs, check_vma=False)
```

```python
import functools
import math

import jax
import jax.numpy as jnp
from jax import lax
from jax.experimental import pallas as pl
from jax.experimental.pallas import tpu as pltpu
from jax.sharding import Mesh
from jax.sharding import PartitionSpec as P

CAP = 4
STEP_TIME = 0.2
REST_VOLUME = 1.0 / 6.0
PERMUTATIONS = ((0, 1, 2), (0, 2, 1), (1, 0, 2), (1, 2, 0), (2, 0, 1), (2, 1, 0))
ROWS = 4
TILES = CAP // 2

VMEM = pl.BlockSpec(memory_space=pltpu.VMEM)
SMEM = pl.BlockSpec(memory_space=pltpu.SMEM)
HBM = pl.BlockSpec(memory_space=pltpu.HBM)
PARAMS = pltpu.CompilerParams(vmem_limit_bytes=16 << 20)
NEAR_TURNS = 32
ROOT = math.sqrt(math.log2(math.e))


def add(total, term):
    return term if total is None else total + term


def unit(axis):
    return tuple(1 if position == 2 - axis else 0 for position in range(3))


def tensions(edges, growth, scale_side, scale_up):
    inverse = 1.0 / growth
    columns = {}
    for (axis, start), rows in edges.items():
        made = []
        for row in range(3):
            value = rows[row] + 1.0 if row == axis else rows[row]
            made.append(value * inverse if axis < 2 else value)
        columns[(axis, start)] = made
    pulls = {}
    for first, second, third in PERMUTATIONS:
        middle = unit(first)
        upper = tuple(a + b for a, b in zip(middle, unit(second)))
        keys = {first: (first, (0, 0, 0)), second: (second, middle), third: (third, upper)}
        fe = [[columns[keys[col]][row] for col in range(3)] for row in range(3)]
        cof = [
            [
                fe[(row + 1) % 3][(col + 1) % 3] * fe[(row + 2) % 3][(col + 2) % 3]
                - fe[(row + 1) % 3][(col + 2) % 3] * fe[(row + 2) % 3][(col + 1) % 3]
                for col in range(3)
            ]
            for row in range(3)
        ]
        jacobian = fe[0][0] * cof[0][0] + fe[0][1] * cof[0][1] + fe[0][2] * cof[0][2]
        pressure = 4.0 * jacobian - 5.0
        for col in range(3):
            key = keys[col]
            for row in range(3):
                pulls.setdefault(key, [None] * 3)
                pulls[key][row] = add(pulls[key][row], fe[row][col] + pressure * cof[row][col])
    return {
        key: [value * (scale_side if key[0] < 2 else scale_up) for value in rows]
        for key, rows in pulls.items()
    }


def roll(value, shift, axis):
    size = value.shape[axis]
    shift = shift % size
    return value if shift == 0 else pltpu.roll(value, shift, axis)


def lane_of(shape):
    return lax.broadcasted_iota(jnp.int32, shape, len(shape) - 1)


def column_pack(fields, lane_from, stride, offset):
    shape = fields[0][0].shape
    lane = lane_of(shape)
    packed = jnp.zeros(shape, jnp.float32)
    for c, layers in enumerate(fields):
        for z, field in enumerate(layers):
            to = c * stride + z + offset
            packed = jnp.where(lane == to, roll(field, to - lane_from, 1), packed)
    return packed


def each(count, body, unrolled):
    if count <= unrolled:
        for index in range(count):
            body(index)
    else:

        def one(index, carry):
            body(index)
            return carry

        lax.fori_loop(0, count, one, 0)


def split(value, size):
    if size & (size - 1):
        return lax.div(value, size), lax.rem(value, size)
    return lax.shift_right_logical(value, size.bit_length() - 1), lax.bitwise_and(value, size - 1)


def slab_index():
    return lax.axis_index("pair") * lax.axis_size("core") + lax.axis_index("core")


def thirds(value):
    high = value.astype(jnp.bfloat16)
    rest = value - high.astype(jnp.float32)
    middle = rest.astype(jnp.bfloat16)
    low = (rest - middle.astype(jnp.float32)).astype(jnp.bfloat16)
    return high, middle, low


def picked(chosen, value, contract):
    chosen = chosen.astype(jnp.bfloat16)
    total = None
    for part in thirds(value):
        term = lax.dot_general(
            chosen,
            part,
            (((contract,), (0,)), ((), ())),
            preferred_element_type=jnp.float32,
        )
        total = add(total, term)
    return total


def shift_y(value, step, half_lanes, first_row, last_row):
    moved = roll(value, step, 0)
    return jnp.where(
        first_row if step > 0 else last_row, roll(moved, step * half_lanes, 1), moved
    )


def pack_kernel(
    dims,
    disp_in,
    growth_in,
    shear_in,
    slots_in,
    packet,
    face_a,
    face_b,
    disp,
    growth,
    shear,
    slots,
    counted,
    face,
    sems,
):
    slab_len, width_y, patch_len, regions, slabs, pairs = dims
    region = lax.axis_index("region")
    depth = slab_index()
    core = lax.axis_index("core")
    partner = depth + 1 - 2 * core
    stride = slab_len + 2
    half = patch_len // 2
    moves = [
        pltpu.make_async_copy(source, target, sems.at[index])
        for index, (source, target) in enumerate(
            (
                (slots_in, slots),
                (disp_in, disp.at[0 : slab_len * 3 * width_y]),
                (growth_in, growth),
                (shear_in, shear),
            )
        )
    ]
    for move in moves:
        move.start()
    tall = TILES * ROWS
    span = 1 << pairs.bit_length()
    blank = jnp.zeros((tall, patch_len), jnp.float32)

    def base_of(m, slab):
        return pl.multiple_of((m * slabs + slab) * tall, tall)

    def clear(m):
        counted[m] = m * (slabs * tall * span)
        packet[pl.ds(base_of(m, depth), tall), :] = blank
        packet[pl.ds(base_of(m, partner), tall), :] = blank

    disp[slab_len * 3 * width_y :, :] = jnp.zeros((ROWS * width_y, patch_len), jnp.float32)
    spare = region * (slabs * tall)
    each(regions, clear, 16)
    for move in moves:
        move.wait()

    tile_row = lax.broadcasted_iota(jnp.int32, (ROWS, patch_len), 0)

    lane = lane_of((ROWS, patch_len))

    def place(k):
        own, other = slots[0, 0, 0, k], slots[0, 1, 0, k]
        state = counted[other]
        counted[other] = state + 1
        first, position = split(state, span)
        fits = position < CAP
        first = jnp.where(fits, first, spare)
        side, offset = split(jnp.where(fits, position, 0), TILES)
        first = first + offset * ROWS
        z, y = split(own, width_y)
        tile = disp[pl.ds(z * (3 * width_y) + y, ROWS, stride=width_y), :]
        label = jnp.full((ROWS, patch_len), own, jnp.int32).astype(jnp.float32)
        tile = jnp.where(tile_row == 3, label, tile)
        turned = roll(tile, half, 1)
        mask = (lane >= half) == (side > 0)
        for slab, value in (
            (depth, jnp.where(lane < half, tile, turned)),
            (partner, jnp.where(lane < half, turned, tile)),
        ):
            base = pl.multiple_of(first + slab * tall, ROWS)
            pltpu.store(packet.at[pl.ds(base, ROWS), :], value, mask=mask)

    each(pairs, place, 16)

    even = lax.rem(depth, 2) == 0
    last = slab_len - 1
    for out, from_z in ((face_a, jnp.where(even, last, 0)), (face_b, jnp.where(even, 0, last))):
        for c in range(3):
            start = pl.multiple_of((from_z * 3 + c) * width_y, width_y)
            out[c] = disp[pl.ds(start, width_y), :]
        out[3] = growth[last]
        out[4] = shear[last]

    half_rows = width_y // 2
    groups = half_rows // TILES
    width = patch_len // groups

    def plane(z, c):
        start = (z * 3 + c) * width_y
        return disp[start : start + width_y, :]

    fields = [[plane(z, c) for z in range(slab_len)] for c in range(3)]
    fields = fields + [[growth[z] for z in range(slab_len)], [shear[z] for z in range(slab_len)]]
    sides = ((patch_len - 1, fields, 1), (0, fields[:3], regions - 1))
    lane = lane_of((TILES, patch_len))
    for side, (lane_from, chosen, step) in enumerate(sides):
        ringed = [[layers[-1]] + layers + [layers[0]] for layers in chosen]
        face[side] = column_pack(ringed, lane_from, stride, 0)
        folded = []
        for part in range(2):
            value = jnp.zeros((TILES, patch_len), jnp.float32)
            for g in range(groups):
                start = part * half_rows + g * TILES
                rows = roll(face[side, start : start + TILES, :], g * width, 1)
                value = jnp.where((lane >= g * width) & (lane < (g + 1) * width), rows, value)
            folded.append(value)
        other = lax.rem(region + step, regions)
        for slab in range(slabs):
            value = jnp.where(core == slab % 2, folded[0], folded[1])
            rows = pl.ds(base_of(other, slab) + 3, TILES, stride=ROWS)
            packet[rows, :] = jnp.where(lax.rem(lane, half) == half - 1, packet[rows, :], value)


def layer_edges(layer):
    along_x, along_y, moved = {}, {}, {}
    for c in range(3):
        base = layer[c]
        next_x = roll(base, -1, 1)
        next_y = roll(base, -1, 0)
        next_xy = roll(next_y, -1, 1)
        moved[c] = {(0, 0): base, (0, 1): next_x, (1, 0): next_y, (1, 1): next_xy}
        along_x[c] = {0: next_x - base, 1: next_xy - next_y}
        along_y[c] = {0: next_y - base, 1: next_xy - next_x}
    return along_x, along_y, moved


def cell_layer(low, high, growth, shear, valid):
    edges = {}
    for dz, (along_x, along_y, _) in enumerate((low, high)):
        for other in range(2):
            edges[(0, (dz, other, 0))] = [along_x[c][other] for c in range(3)]
            edges[(1, (dz, 0, other))] = [along_y[c][other] for c in range(3)]
    for dy in range(2):
        for dx in range(2):
            edges[(2, (0, dy, dx))] = [
                high[2][c][(dy, dx)] - low[2][c][(dy, dx)] for c in range(3)
            ]
    scale = jnp.where(valid, shear * REST_VOLUME, 0.0) * growth
    pulls = tensions(edges, growth, scale, scale * growth)
    levels = []
    for dz in range(2):
        level = []
        for c in range(3):
            pull_x = pulls[(0, (dz, 0, 0))][c] + roll(pulls[(0, (dz, 1, 0))][c], 1, 0)
            pull_y = pulls[(1, (dz, 0, 0))][c] + roll(pulls[(1, (dz, 0, 1))][c], 1, 1)
            level.append((pull_x - roll(pull_x, 1, 1)) + (pull_y - roll(pull_y, 1, 0)))
        levels.append(level)
    for c in range(3):
        at_zero = pulls[(2, (0, 0, 0))][c] + roll(pulls[(2, (0, 1, 0))][c], 1, 0)
        at_one = pulls[(2, (0, 0, 1))][c] + roll(pulls[(2, (0, 1, 1))][c], 1, 0)
        pull_z = at_zero + roll(at_one, 1, 1)
        levels[0][c] = levels[0][c] + pull_z
        levels[1][c] = levels[1][c] - pull_z
    return levels


def inner_cells(width_y, patch_len):
    shape = (width_y, patch_len)
    row_y = lax.broadcasted_iota(jnp.int32, shape, 0)
    return (lane_of(shape) < patch_len - 1) & (row_y < width_y - 1)


def inner_kernel(
    dims,
    disp,
    growth,
    shear,
    velocity,
    slots,
    slot_row,
    count,
    separation,
    before,
    near,
    selector,
):
    slab_len, width_y, patch_len, regions, slabs, pairs = dims
    inside = inner_cells(width_y, patch_len)
    forces = [[None] * 3 for _ in range(slab_len)]
    low = layer_edges([disp[0, c] for c in range(3)])
    for z in range(slab_len - 1):
        high = layer_edges([disp[z + 1, c] for c in range(3)])
        levels = cell_layer(low, high, growth[z], shear[z], inside)
        low = high
        for dz in range(2):
            for c in range(3):
                forces[z + dz][c] = add(forces[z + dz][c], levels[dz][c])
        for c in range(3):
            before[z, c] = velocity[z, c] + STEP_TIME * forces[z][c]
    for c in range(3):
        before[slab_len - 1, c] = velocity[slab_len - 1, c] + STEP_TIME * forces[slab_len - 1][c]

    along = lane_of((1, patch_len)).astype(jnp.float32)

    def fetch(k):
        z, y = split(slots[0, 0, 0, k], width_y)
        for c in range(3):
            point = disp[z, c, pl.ds(y, 1), :]
            if c == 0:
                point = point + along
            near[0, c, pl.ds(k, 1), :] = (point - separation[0, c, 0, k]) * ROOT

    each(pairs, fetch, 16)
    for c in range(3):
        value = near[0, c]
        for turn in range(1, NEAR_TURNS):
            near[turn, c] = roll(value, -turn * (patch_len // 2 // NEAR_TURNS), 1)
    patch_row = lax.broadcasted_iota(jnp.int32, selector.shape, 0)
    live = lax.broadcasted_iota(jnp.int32, selector.shape, 1) < count[0, 0]
    selector[...] = jnp.where((patch_row == slot_row[0, 0]) & live, 1.0, 0.0)


def outer_kernel(dims, disp, growth, shear, face_a, face_b, lowest, highest, own_columns):
    slab_len, width_y, patch_len, regions, slabs, pairs = dims
    depth = slab_index()
    inside = inner_cells(width_y, patch_len)
    even = lax.rem(depth, 2) == 0
    below = [jnp.where(even, face_b[c], face_a[c]) for c in range(5)]
    above = [jnp.where(even, face_a[c], face_b[c]) for c in range(3)]
    has_below = depth > 0
    last = slab_len - 1
    below_growth = jnp.where(has_below, below[3], 1.0)
    first_nodes = [disp[0, c] for c in range(3)]
    last_nodes = [disp[last, c] for c in range(3)]
    low, high = layer_edges(below[0:3]), layer_edges(first_nodes)
    levels = cell_layer(low, high, below_growth, below[4], inside & has_below)
    for c in range(3):
        lowest[c] = levels[1][c]
    low, high = layer_edges(last_nodes), layer_edges(above)
    levels = cell_layer(low, high, growth[last], shear[last], inside & (depth < slabs - 1))
    for c in range(3):
        highest[c] = levels[0][c]

    half_rows = width_y // 2
    stride = slab_len + 2
    lane_half = lane_of((half_rows, patch_len)) < patch_len // 4
    side_fields = [
        [below[c]] + [disp[z, c] for z in range(slab_len)] + [above[c]] for c in range(3)
    ]
    cell_fields = [
        [below_growth] + [growth[z] for z in range(slab_len)],
        [below[4]] + [shear[z] for z in range(slab_len)],
    ]
    for side, (chosen, lane_from) in enumerate(
        ((side_fields + cell_fields, patch_len - 1), (side_fields, 0))
    ):
        column = column_pack(chosen, lane_from, stride, 0)
        upper = roll(column[half_rows:], patch_len // 4, 1)
        own_columns[side] = jnp.where(lane_half, column[:half_rows], upper)


def border_forces(dims, arrived, relayed, own_columns):
    slab_len, width_y, patch_len, regions, slabs, pairs = dims
    region = lax.axis_index("region")
    depth = slab_index()
    stride = slab_len + 2
    half_rows = width_y // 2
    groups = half_rows // TILES
    width = patch_len // groups
    half = patch_len // 2
    fold_z = lax.rem(lax.rem(lane_of((TILES, patch_len)), width), stride)
    row_group = lax.broadcasted_iota(jnp.int32, (half_rows, patch_len), 0) // TILES
    lower_y = lane_of((half_rows, patch_len)) < half // 2
    gathered = []
    for step in (regions - 1, 1):
        other = lax.rem(region + step, regions)

        def columns(source, slab):
            base = (other * slabs + lax.rem(slab + slabs, slabs)) * (TILES * ROWS)
            return source[pl.ds(base + 3, TILES, stride=ROWS), :]

        total = jnp.zeros((half_rows, patch_len), jnp.float32)
        for part, (direct, across) in enumerate(((arrived, relayed), (relayed, arrived))):
            merged = columns(direct, depth)
            merged = jnp.where(fold_z == 0, columns(across, depth - 1), merged)
            merged = jnp.where(fold_z == slab_len + 1, columns(across, depth + 1), merged)
            merged = jnp.concatenate([merged] * groups, axis=0)
            for g in range(groups):
                here = (row_group == g) & (lower_y if part == 0 else ~lower_y)
                shift = part * (half // 2) - g * width
                total = jnp.where(here, roll(merged, shift, 1), total)
        gathered.append(total)
    from_left, from_right = gathered
    own_last = own_columns[0]
    own_first = own_columns[1]
    shape = (half_rows, patch_len)
    lane = lane_of(shape)
    row = lax.broadcasted_iota(jnp.int32, shape, 0)
    first_row, last_row = row == 0, row == half_rows - 1
    first_side = lane < half
    quarter = half // 2
    z_cell = lax.rem(lane, quarter)
    row_y = row + jnp.where(lax.rem(lane, half) >= quarter, half_rows, 0)

    def at_y(value, step):
        return shift_y(value, step, quarter, first_row, last_row)

    z_global = depth * slab_len + z_cell - 1
    valid = (z_cell <= slab_len) & (z_global >= 0) & (z_global <= slab_len * slabs - 2)
    valid = valid & (row_y < width_y - 1)

    low_x = [
        jnp.where(
            first_side, roll(from_left, -c * stride, 1), roll(own_last, half - c * stride, 1)
        )
        for c in range(5)
    ]
    high_x = [
        jnp.where(
            first_side, roll(own_first, -c * stride, 1), roll(from_right, half - c * stride, 1)
        )
        for c in range(3)
    ]
    growth = jnp.where(valid, low_x[3], 1.0)
    scale = jnp.where(valid, low_x[4] * REST_VOLUME, 0.0) * growth
    corner = {}
    for c in range(3):
        for dx, base in ((0, low_x[c]), (1, high_x[c])):
            up = roll(base, -1, 1)
            corner[(c, 0, 0, dx)] = base
            corner[(c, 0, 1, dx)] = at_y(base, -1)
            corner[(c, 1, 0, dx)] = up
            corner[(c, 1, 1, dx)] = at_y(up, -1)
    edges = {}
    for one in range(2):
        for two in range(2):
            for axis, start in ((0, (one, two, 0)), (1, (one, 0, two)), (2, (0, one, two))):
                end = tuple(a + b for a, b in zip(start, unit(axis)))
                edges[(axis, start)] = [corner[(c, *end)] - corner[(c, *start)] for c in range(3)]
    pulls = tensions(edges, growth, scale, scale * growth)
    forces = []
    for c in range(3):

        def chosen(axis, one):
            at = ((one, 0, 0), (one, 0, 1)) if axis == 1 else ((0, one, 0), (0, one, 1))
            return jnp.where(first_side, pulls[(axis, at[1])][c], pulls[(axis, at[0])][c])

        level = []
        for dz in range(2):
            both = pulls[(0, (dz, 0, 0))][c] + at_y(pulls[(0, (dz, 1, 0))][c], 1)
            both = jnp.where(first_side, -both, both)
            along_y = chosen(1, dz)
            level.append(both + (along_y - at_y(along_y, 1)))
        along_z = chosen(2, 0) + at_y(chosen(2, 1), 1)
        forces.append((level[0] + along_z) + roll(level[1] - along_z, 1, 1))
    return forces


def far_points(dims, source, chosen, tiles):
    slab_len, width_y, patch_len, regions, slabs, pairs = dims
    depth = slab_index()
    half = patch_len // 2
    tall = TILES * ROWS

    def take(m):
        rows = pl.ds(pl.multiple_of((m * slabs + depth) * tall, tall), tall)
        tiles[pl.ds(pl.multiple_of(m * tall, tall), tall), :] = source[rows, :]

    each(regions, take, 16)
    if chosen is None:
        chosen = yield
    lane = lane_of((pairs, patch_len))
    for c in range(3):
        value = picked(chosen, tiles[pl.ds(c, regions * TILES, stride=ROWS), :], 1)
        value = jnp.where(lane < half, value[:pairs], value[pairs:])
        yield value + roll(value, half, 1)


def tile_choice(dims, slots, tiles):
    slab_len, width_y, patch_len, regions, slabs, pairs = dims
    half = patch_len // 2
    rows = regions * TILES
    found = tiles[pl.ds(3, rows, stride=ROWS), :]
    wide = max(pairs, patch_len)
    labels = [
        jnp.broadcast_to(found[:, side * half + half - 1 : side * half + half], (rows, wide))
        for side in range(2)
    ]
    row = lax.broadcasted_iota(jnp.int32, (rows, wide), 0)
    upper = lax.rem(row, TILES) > 0
    others = [jnp.where(upper, roll(label, 1, 0), roll(label, -1, 0)) for label in labels]
    again = [
        upper & (others[0] == labels[0]),
        (labels[1] == labels[0])
        | (labels[1] == others[0])
        | (upper & (others[1] == labels[1])),
    ]
    region_row = lax.broadcasted_iota(jnp.int32, (rows, pairs), 0) // TILES
    named = slots[0, 2].astype(jnp.float32)
    chosen = []
    for label, repeated in zip(labels, again):
        label = jnp.where(repeated, -1.0, label)[:, 0:pairs]
        chosen.append(jnp.where((region_row == slots[0, 1]) & (label == named), 1.0, 0.0))
    return jnp.concatenate([jnp.transpose(value) for value in chosen], axis=0)


def contact_half(dims, near, far, part, write):
    slab_len, width_y, patch_len, regions, slabs, pairs = dims
    half = patch_len // 2
    block = 8
    along = lax.rem(lane_of((block, patch_len)), half) + part * half
    along = along.astype(jnp.float32)

    def some(start):
        rows = pl.ds(start, block)
        theirs = [far[c, rows, :] for c in range(3)]
        theirs = [(theirs[0] + along) * ROOT, theirs[1] * ROOT, theirs[2] * ROOT]
        starts = range(0, half, half // NEAR_TURNS)
        turned = [[near[turn, c, rows, :] for c in range(3)] for turn in range(NEAR_TURNS)]
        sums = [[None] * 3 for _ in starts]
        for b in range(half // NEAR_TURNS):
            other = [roll(value, b, 1) for value in theirs]
            for total, here in zip(sums, turned):
                delta = [here[c] - other[c] for c in range(3)]
                square = delta[0] * delta[0] + delta[1] * delta[1] + delta[2] * delta[2]
                weight = jnp.exp2(-square)
                for c in range(3):
                    total[c] = add(total[c], delta[c] * weight)
        for c in range(3):
            total = None
            for a, sum_a in zip(starts, sums):
                total = add(total, roll(sum_a[c], a, 1))
            write(c, rows, total)

    each(pairs // block, lambda step: some(step * block), 2)


def contact_kernel(
    dims, arrived, near, slots, before, lowest, highest, selector, chosen, moved, far, tiles, pushes
):
    points = far_points(dims, arrived, None, tiles)
    next(points)
    chosen[...] = tile_choice(dims, slots, tiles)
    far[0] = points.send(chosen[...])
    far[1] = next(points)
    far[2] = next(points)

    def write(c, rows, total):
        pushes[c, rows, :] = total

    contact_half(dims, near, far, 0, write)
    slab_len, width_y, patch_len, regions, slabs, pairs = dims
    for c in range(3):
        push = picked(selector[...], pushes[c], 1) * (1.0 / ROOT)
        for z in range(slab_len):
            force = push[z * width_y : (z + 1) * width_y, :]
            if z == 0:
                force = force + lowest[c]
            if z == slab_len - 1:
                force = force + highest[c]
            moved[z, c] = before[z, c] + STEP_TIME * force


def finish_kernel(
    dims,
    arrived,
    relayed,
    moved,
    near,
    chosen,
    own_columns,
    disp,
    selector,
    new_velocity,
    new_disp,
    far,
    tiles,
    total_push,
):
    slab_len, width_y, patch_len, regions, slabs, pairs = dims
    half = patch_len // 2
    for c, value in enumerate(far_points(dims, relayed, chosen[...], tiles)):
        far[c] = value

    def write(c, rows, total):
        total_push[c, rows, :] = total

    contact_half(dims, near, far, 1, write)
    borders = border_forces(dims, arrived, relayed, own_columns)
    half_rows = width_y // 2
    lane = lane_of((half_rows, patch_len))
    last = patch_len - 1
    for c in range(3):
        push = picked(selector[...], total_push[c], 1) * (1.0 / ROOT)
        edge = borders[c]
        for z in range(slab_len):
            for part in range(2):
                at = part * (half // 2) + z + 1
                rows = slice(part * half_rows, (part + 1) * half_rows)
                start = z * width_y + part * half_rows
                force = push[start : start + half_rows, :]
                force = force + jnp.where(lane == 0, roll(edge, -at, 1), 0.0)
                force = force + jnp.where(lane == last, roll(edge, last - half - at, 1), 0.0)
                speed = moved[z, c, rows, :] + STEP_TIME * force
                new_velocity[z, c, rows, :] = speed
                new_disp[z, c, rows, :] = disp[z, c, rows, :] + STEP_TIME * speed


def local(displacement, velocity, growth, shear_modulus, pair_slots, pair_count, separation):
    slab_len, width_y, _, patch_len = displacement.shape
    regions = lax.axis_size("region")
    slabs = lax.axis_size("pair") * lax.axis_size("core")
    pairs = pair_slots.shape[3]
    dims = (slab_len, width_y, patch_len, regions, slabs, pairs)
    f32 = jnp.float32
    i32 = jnp.int32
    disp = jnp.transpose(displacement, (0, 2, 1, 3))
    speed = jnp.transpose(velocity, (0, 2, 1, 3))
    slots = jnp.transpose(pair_slots, (0, 2, 1, 3))
    apart = jnp.transpose(separation, (0, 2, 1, 3))
    plane = (width_y, patch_len)

    packet, face_a, face_b = pl.pallas_call(
        functools.partial(pack_kernel, dims),
        out_shape=(
            jax.ShapeDtypeStruct((regions * slabs * TILES * ROWS, patch_len), f32),
            jax.ShapeDtypeStruct((5, *plane), f32),
            jax.ShapeDtypeStruct((5, *plane), f32),
        ),
        in_specs=[HBM] * 4,
        out_specs=(VMEM, VMEM, VMEM),
        scratch_shapes=[
            pltpu.VMEM(((slab_len * 3 + ROWS) * width_y, patch_len), f32),
            pltpu.VMEM((slab_len, *plane), f32),
            pltpu.VMEM((slab_len, *plane), f32),
            pltpu.SMEM(slots.shape, i32),
            pltpu.SMEM((regions,), i32),
            pltpu.VMEM((2, *plane), f32),
            pltpu.SemaphoreType.DMA((4,)),
        ],
        name="pack",
    )(disp.reshape(slab_len * 3 * width_y, patch_len), growth, shear_modulus, slots)

    links = [[(i, i + 1) for i in range(first, slabs - 1, 2)] for first in (0, 1)]
    links = [link + [(b, a) for a, b in link] for link in links]
    face_a = lax.ppermute(face_a, ("pair", "core"), links[0])
    face_b = lax.ppermute(face_b, ("pair", "core"), links[1])

    packet, pair_count = lax.optimization_barrier((packet, pair_count))
    arrived = lax.all_to_all(packet, ("region", "pair", "core"), 0, 0, tiled=True)

    before, near, selector = pl.pallas_call(
        functools.partial(inner_kernel, dims),
        out_shape=(
            jax.ShapeDtypeStruct((slab_len, 3, *plane), f32),
            jax.ShapeDtypeStruct((NEAR_TURNS, 3, pairs, patch_len), f32),
            jax.ShapeDtypeStruct((slab_len * width_y, pairs), f32),
        ),
        in_specs=[VMEM] * 4 + [SMEM, VMEM, SMEM, SMEM],
        out_specs=(VMEM,) * 3,
        compiler_params=PARAMS,
        name="inner",
        cost_estimate=pl.CostEstimate(flops=4000 * 1024, bytes_accessed=1 << 20, transcendentals=0),
    )(disp, growth, shear_modulus, speed, slots, slots, pair_count, apart)

    lowest, highest, own_columns = pl.pallas_call(
        functools.partial(outer_kernel, dims),
        out_shape=(
            jax.ShapeDtypeStruct((3, *plane), f32),
            jax.ShapeDtypeStruct((3, *plane), f32),
            jax.ShapeDtypeStruct((2, width_y // 2, patch_len), f32),
        ),
        in_specs=[VMEM] * 5,
        out_specs=(VMEM,) * 3,
        compiler_params=PARAMS,
        name="outer",
        cost_estimate=pl.CostEstimate(flops=2000 * 1024, bytes_accessed=1 << 20, transcendentals=0),
    )(disp, growth, shear_modulus, face_a, face_b)

    arrived, before, lowest = lax.optimization_barrier((arrived, before, lowest))
    relayed = lax.ppermute(arrived, ("pair", "core"), links[0])

    tile_rows = regions * TILES
    chosen, moved = pl.pallas_call(
        functools.partial(contact_kernel, dims),
        out_shape=(
            jax.ShapeDtypeStruct((2 * pairs, tile_rows), f32),
            jax.ShapeDtypeStruct((slab_len, 3, *plane), f32),
        ),
        in_specs=[VMEM] * 7,
        out_specs=(VMEM,) * 2,
        scratch_shapes=[
            pltpu.VMEM((3, pairs, patch_len), f32),
            pltpu.VMEM((tile_rows * ROWS, patch_len), f32),
            pltpu.VMEM((3, pairs, patch_len), f32),
        ],
        compiler_params=PARAMS,
        name="contact",
        cost_estimate=pl.CostEstimate(flops=6000 * 1024, bytes_accessed=1 << 20, transcendentals=0),
    )(arrived, near, slots, before, lowest, highest, selector)

    new_velocity, new_disp = pl.pallas_call(
        functools.partial(finish_kernel, dims),
        out_shape=(
            jax.ShapeDtypeStruct((slab_len, 3, *plane), f32),
            jax.ShapeDtypeStruct((slab_len, 3, *plane), f32),
        ),
        in_specs=[VMEM] * 8,
        out_specs=(VMEM, VMEM),
        scratch_shapes=[
            pltpu.VMEM((3, pairs, patch_len), f32),
            pltpu.VMEM((tile_rows * ROWS, patch_len), f32),
            pltpu.VMEM((3, pairs, patch_len), f32),
        ],
        compiler_params=PARAMS,
        name="finish",
    )(
        arrived,
        relayed,
        moved,
        near,
        chosen,
        own_columns,
        disp,
        selector,
    )
    order = (0, 2, 1, 3)
    return jnp.transpose(new_velocity, order), jnp.transpose(new_disp, order)


def solution(mesh):
    shape = dict(mesh.shape)
    devices = mesh.devices.reshape(shape["region"], shape["depth"] // 2, 2)
    fine = Mesh(devices, ("region", "pair", "core"))
    depth = ("pair", "core")
    in_specs = (
        P(depth, None, None, "region"),
        P(depth, None, None, "region"),
        P(depth, None, "region"),
        P(depth, None, "region"),
        P(depth, "region", None, None),
        P(depth, "region"),
        P(depth, "region", None, None),
    )
    out_specs = (P(depth, None, None, "region"), P(depth, None, None, "region"))
    return jax.shard_map(local, mesh=fine, in_specs=in_specs, out_specs=out_specs, check_vma=False)
```

```python
import functools
import math

import jax
import jax.numpy as jnp
from jax import lax
from jax.experimental import pallas as pl
from jax.experimental.pallas import tpu as pltpu
from jax.sharding import Mesh
from jax.sharding import PartitionSpec as P

CAP = 4
STEP_TIME = 0.2
REST_VOLUME = 1.0 / 6.0
PERMUTATIONS = ((0, 1, 2), (0, 2, 1), (1, 0, 2), (1, 2, 0), (2, 0, 1), (2, 1, 0))
ROWS = 4
TILES = CAP // 2

VMEM = pl.BlockSpec(memory_space=pltpu.VMEM)
SMEM = pl.BlockSpec(memory_space=pltpu.SMEM)
HBM = pl.BlockSpec(memory_space=pltpu.HBM)
PARAMS = pltpu.CompilerParams(vmem_limit_bytes=16 << 20)
NEAR_TURNS = 32
ROOT = math.sqrt(math.log2(math.e))


def add(total, term):
    return term if total is None else total + term


def unit(axis):
    return tuple(1 if position == 2 - axis else 0 for position in range(3))


def tensions(edges, growth, scale_side, scale_up):
    inverse = 1.0 / growth
    columns = {}
    for (axis, start), rows in edges.items():
        made = []
        for row in range(3):
            value = rows[row] + 1.0 if row == axis else rows[row]
            made.append(value * inverse if axis < 2 else value)
        columns[(axis, start)] = made
    pulls = {}
    for first, second, third in PERMUTATIONS:
        middle = unit(first)
        upper = tuple(a + b for a, b in zip(middle, unit(second)))
        keys = {first: (first, (0, 0, 0)), second: (second, middle), third: (third, upper)}
        fe = [[columns[keys[col]][row] for col in range(3)] for row in range(3)]
        cof = [
            [
                fe[(row + 1) % 3][(col + 1) % 3] * fe[(row + 2) % 3][(col + 2) % 3]
                - fe[(row + 1) % 3][(col + 2) % 3] * fe[(row + 2) % 3][(col + 1) % 3]
                for col in range(3)
            ]
            for row in range(3)
        ]
        jacobian = fe[0][0] * cof[0][0] + fe[0][1] * cof[0][1] + fe[0][2] * cof[0][2]
        pressure = 4.0 * jacobian - 5.0
        for col in range(3):
            key = keys[col]
            for row in range(3):
                pulls.setdefault(key, [None] * 3)
                pulls[key][row] = add(pulls[key][row], fe[row][col] + pressure * cof[row][col])
    return {
        key: [value * (scale_side if key[0] < 2 else scale_up) for value in rows]
        for key, rows in pulls.items()
    }


def roll(value, shift, axis):
    size = value.shape[axis]
    shift = shift % size
    return value if shift == 0 else pltpu.roll(value, shift, axis)


def lane_of(shape):
    return lax.broadcasted_iota(jnp.int32, shape, len(shape) - 1)


def column_pack(fields, lane_from, stride, offset):
    shape = fields[0][0].shape
    lane = lane_of(shape)
    packed = jnp.zeros(shape, jnp.float32)
    for c, layers in enumerate(fields):
        for z, field in enumerate(layers):
            to = c * stride + z + offset
            packed = jnp.where(lane == to, roll(field, to - lane_from, 1), packed)
    return packed


def each(count, body, unrolled):
    if count <= unrolled:
        for index in range(count):
            body(index)
    else:

        def one(index, carry):
            body(index)
            return carry

        lax.fori_loop(0, count, one, 0)


def split(value, size):
    if size & (size - 1):
        return lax.div(value, size), lax.rem(value, size)
    return lax.shift_right_logical(value, size.bit_length() - 1), lax.bitwise_and(value, size - 1)


def slab_index():
    return lax.axis_index("pair") * lax.axis_size("core") + lax.axis_index("core")


def thirds(value):
    high = value.astype(jnp.bfloat16)
    rest = value - high.astype(jnp.float32)
    middle = rest.astype(jnp.bfloat16)
    low = (rest - middle.astype(jnp.float32)).astype(jnp.bfloat16)
    return high, middle, low


def picked(chosen, value, contract):
    chosen = chosen.astype(jnp.bfloat16)
    total = None
    for part in thirds(value):
        term = lax.dot_general(
            chosen,
            part,
            (((contract,), (0,)), ((), ())),
            preferred_element_type=jnp.float32,
        )
        total = add(total, term)
    return total


def shift_y(value, step, half_lanes, first_row, last_row):
    moved = roll(value, step, 0)
    return jnp.where(
        first_row if step > 0 else last_row, roll(moved, step * half_lanes, 1), moved
    )


def pack_kernel(
    dims,
    disp_in,
    growth_in,
    shear_in,
    slots_in,
    packet,
    face_a,
    face_b,
    disp,
    growth,
    shear,
    slots,
    counted,
    face,
    sems,
):
    slab_len, width_y, patch_len, regions, slabs, pairs = dims
    region = lax.axis_index("region")
    depth = slab_index()
    core = lax.axis_index("core")
    partner = depth + 1 - 2 * core
    stride = slab_len + 2
    half = patch_len // 2
    moves = [
        pltpu.make_async_copy(source, target, sems.at[index])
        for index, (source, target) in enumerate(
            (
                (slots_in, slots),
                (disp_in, disp.at[0 : slab_len * 3 * width_y]),
                (growth_in, growth),
                (shear_in, shear),
            )
        )
    ]
    for move in moves:
        move.start()
    tall = TILES * ROWS
    span = 1 << pairs.bit_length()
    blank = jnp.zeros((tall, patch_len), jnp.float32)

    def base_of(m, slab):
        return pl.multiple_of((m * slabs + slab) * tall, tall)

    def clear(m):
        counted[m] = m * (slabs * tall * span)
        packet[pl.ds(base_of(m, depth), tall), :] = blank
        packet[pl.ds(base_of(m, partner), tall), :] = blank

    disp[slab_len * 3 * width_y :, :] = jnp.zeros((ROWS * width_y, patch_len), jnp.float32)
    spare = region * (slabs * tall)
    each(regions, clear, 16)
    for move in moves:
        move.wait()

    tile_row = lax.broadcasted_iota(jnp.int32, (ROWS, patch_len), 0)

    lane = lane_of((ROWS, patch_len))

    def place(k):
        own, other = slots[0, 0, 0, k], slots[0, 1, 0, k]
        state = counted[other]
        counted[other] = state + 1
        first, position = split(state, span)
        fits = position < CAP
        first = jnp.where(fits, first, spare)
        side, offset = split(jnp.where(fits, position, 0), TILES)
        first = first + offset * ROWS
        z, y = split(own, width_y)
        tile = disp[pl.ds(z * (3 * width_y) + y, ROWS, stride=width_y), :]
        label = jnp.full((ROWS, patch_len), own, jnp.int32).astype(jnp.float32)
        tile = jnp.where(tile_row == 3, label, tile)
        turned = roll(tile, half, 1)
        mask = (lane >= half) == (side > 0)
        for slab, value in (
            (depth, jnp.where(lane < half, tile, turned)),
            (partner, jnp.where(lane < half, turned, tile)),
        ):
            base = pl.multiple_of(first + slab * tall, ROWS)
            pltpu.store(packet.at[pl.ds(base, ROWS), :], value, mask=mask)

    each(pairs, place, 16)

    even = lax.rem(depth, 2) == 0
    last = slab_len - 1
    for out, from_z in ((face_a, jnp.where(even, last, 0)), (face_b, jnp.where(even, 0, last))):
        for c in range(3):
            start = pl.multiple_of((from_z * 3 + c) * width_y, width_y)
            out[c] = disp[pl.ds(start, width_y), :]
        out[3] = growth[last]
        out[4] = shear[last]

    half_rows = width_y // 2
    groups = half_rows // TILES
    width = patch_len // groups

    def plane(z, c):
        start = (z * 3 + c) * width_y
        return disp[start : start + width_y, :]

    fields = [[plane(z, c) for z in range(slab_len)] for c in range(3)]
    fields = fields + [[growth[z] for z in range(slab_len)], [shear[z] for z in range(slab_len)]]
    sides = ((patch_len - 1, fields, 1), (0, fields[:3], regions - 1))
    lane = lane_of((TILES, patch_len))
    for side, (lane_from, chosen, step) in enumerate(sides):
        ringed = [[layers[-1]] + layers + [layers[0]] for layers in chosen]
        face[side] = column_pack(ringed, lane_from, stride, 0)
        folded = []
        for part in range(2):
            value = jnp.zeros((TILES, patch_len), jnp.float32)
            for g in range(groups):
                start = part * half_rows + g * TILES
                rows = roll(face[side, start : start + TILES, :], g * width, 1)
                value = jnp.where((lane >= g * width) & (lane < (g + 1) * width), rows, value)
            folded.append(value)
        other = lax.rem(region + step, regions)
        for slab in range(slabs):
            value = jnp.where(core == slab % 2, folded[0], folded[1])
            rows = pl.ds(base_of(other, slab) + 3, TILES, stride=ROWS)
            packet[rows, :] = jnp.where(lax.rem(lane, half) == half - 1, packet[rows, :], value)


def layer_edges(layer):
    along_x, along_y, moved = {}, {}, {}
    for c in range(3):
        base = layer[c]
        next_x = roll(base, -1, 1)
        next_y = roll(base, -1, 0)
        next_xy = roll(next_y, -1, 1)
        moved[c] = {(0, 0): base, (0, 1): next_x, (1, 0): next_y, (1, 1): next_xy}
        along_x[c] = {0: next_x - base, 1: next_xy - next_y}
        along_y[c] = {0: next_y - base, 1: next_xy - next_x}
    return along_x, along_y, moved


def cell_layer(low, high, growth, shear, valid):
    edges = {}
    for dz, (along_x, along_y, _) in enumerate((low, high)):
        for other in range(2):
            edges[(0, (dz, other, 0))] = [along_x[c][other] for c in range(3)]
            edges[(1, (dz, 0, other))] = [along_y[c][other] for c in range(3)]
    for dy in range(2):
        for dx in range(2):
            edges[(2, (0, dy, dx))] = [
                high[2][c][(dy, dx)] - low[2][c][(dy, dx)] for c in range(3)
            ]
    scale = jnp.where(valid, shear * REST_VOLUME, 0.0) * growth
    pulls = tensions(edges, growth, scale, scale * growth)
    levels = []
    for dz in range(2):
        level = []
        for c in range(3):
            pull_x = pulls[(0, (dz, 0, 0))][c] + roll(pulls[(0, (dz, 1, 0))][c], 1, 0)
            pull_y = pulls[(1, (dz, 0, 0))][c] + roll(pulls[(1, (dz, 0, 1))][c], 1, 1)
            level.append((pull_x - roll(pull_x, 1, 1)) + (pull_y - roll(pull_y, 1, 0)))
        levels.append(level)
    for c in range(3):
        at_zero = pulls[(2, (0, 0, 0))][c] + roll(pulls[(2, (0, 1, 0))][c], 1, 0)
        at_one = pulls[(2, (0, 0, 1))][c] + roll(pulls[(2, (0, 1, 1))][c], 1, 0)
        pull_z = at_zero + roll(at_one, 1, 1)
        levels[0][c] = levels[0][c] + pull_z
        levels[1][c] = levels[1][c] - pull_z
    return levels


def inner_cells(width_y, patch_len):
    shape = (width_y, patch_len)
    row_y = lax.broadcasted_iota(jnp.int32, shape, 0)
    return (lane_of(shape) < patch_len - 1) & (row_y < width_y - 1)


def inner_kernel(
    dims,
    disp,
    growth,
    shear,
    velocity,
    slots,
    slot_row,
    count,
    separation,
    before,
    near,
    selector,
):
    slab_len, width_y, patch_len, regions, slabs, pairs = dims
    inside = inner_cells(width_y, patch_len)
    forces = [[None] * 3 for _ in range(slab_len)]
    low = layer_edges([disp[0, c] for c in range(3)])
    for z in range(slab_len - 1):
        high = layer_edges([disp[z + 1, c] for c in range(3)])
        levels = cell_layer(low, high, growth[z], shear[z], inside)
        low = high
        for dz in range(2):
            for c in range(3):
                forces[z + dz][c] = add(forces[z + dz][c], levels[dz][c])
        for c in range(3):
            before[z, c] = velocity[z, c] + STEP_TIME * forces[z][c]
    for c in range(3):
        before[slab_len - 1, c] = velocity[slab_len - 1, c] + STEP_TIME * forces[slab_len - 1][c]

    along = lane_of((1, patch_len)).astype(jnp.float32)

    def fetch(k):
        z, y = split(slots[0, 0, 0, k], width_y)
        for c in range(3):
            point = disp[z, c, pl.ds(y, 1), :]
            if c == 0:
                point = point + along
            near[0, c, pl.ds(k, 1), :] = (point - separation[0, c, 0, k]) * ROOT

    each(pairs, fetch, 16)
    for c in range(3):
        value = near[0, c]
        for turn in range(1, NEAR_TURNS):
            near[turn, c] = roll(value, -turn * (patch_len // 2 // NEAR_TURNS), 1)
    patch_row = lax.broadcasted_iota(jnp.int32, selector.shape, 0)
    live = lax.broadcasted_iota(jnp.int32, selector.shape, 1) < count[0, 0]
    selector[...] = jnp.where((patch_row == slot_row[0, 0]) & live, 1.0, 0.0)


def outer_kernel(dims, disp, growth, shear, face_a, face_b, lowest, highest, own_columns):
    slab_len, width_y, patch_len, regions, slabs, pairs = dims
    depth = slab_index()
    inside = inner_cells(width_y, patch_len)
    even = lax.rem(depth, 2) == 0
    below = [jnp.where(even, face_b[c], face_a[c]) for c in range(5)]
    above = [jnp.where(even, face_a[c], face_b[c]) for c in range(3)]
    has_below = depth > 0
    last = slab_len - 1
    below_growth = jnp.where(has_below, below[3], 1.0)
    first_nodes = [disp[0, c] for c in range(3)]
    last_nodes = [disp[last, c] for c in range(3)]
    low, high = layer_edges(below[0:3]), layer_edges(first_nodes)
    levels = cell_layer(low, high, below_growth, below[4], inside & has_below)
    for c in range(3):
        lowest[c] = levels[1][c]
    low, high = layer_edges(last_nodes), layer_edges(above)
    levels = cell_layer(low, high, growth[last], shear[last], inside & (depth < slabs - 1))
    for c in range(3):
        highest[c] = levels[0][c]

    half_rows = width_y // 2
    stride = slab_len + 2
    lane_half = lane_of((half_rows, patch_len)) < patch_len // 4
    side_fields = [
        [below[c]] + [disp[z, c] for z in range(slab_len)] + [above[c]] for c in range(3)
    ]
    cell_fields = [
        [below_growth] + [growth[z] for z in range(slab_len)],
        [below[4]] + [shear[z] for z in range(slab_len)],
    ]
    for side, (chosen, lane_from) in enumerate(
        ((side_fields + cell_fields, patch_len - 1), (side_fields, 0))
    ):
        column = column_pack(chosen, lane_from, stride, 0)
        upper = roll(column[half_rows:], patch_len // 4, 1)
        own_columns[side] = jnp.where(lane_half, column[:half_rows], upper)


def border_forces(dims, arrived, relayed, own_columns):
    slab_len, width_y, patch_len, regions, slabs, pairs = dims
    region = lax.axis_index("region")
    depth = slab_index()
    stride = slab_len + 2
    half_rows = width_y // 2
    groups = half_rows // TILES
    width = patch_len // groups
    half = patch_len // 2
    fold_z = lax.rem(lax.rem(lane_of((TILES, patch_len)), width), stride)
    row_group = lax.broadcasted_iota(jnp.int32, (half_rows, patch_len), 0) // TILES
    lower_y = lane_of((half_rows, patch_len)) < half // 2
    gathered = []
    for step in (regions - 1, 1):
        other = lax.rem(region + step, regions)

        def columns(source, slab):
            base = (other * slabs + lax.rem(slab + slabs, slabs)) * (TILES * ROWS)
            return source[pl.ds(base + 3, TILES, stride=ROWS), :]

        total = jnp.zeros((half_rows, patch_len), jnp.float32)
        for part, (direct, across) in enumerate(((arrived, relayed), (relayed, arrived))):
            merged = columns(direct, depth)
            merged = jnp.where(fold_z == 0, columns(across, depth - 1), merged)
            merged = jnp.where(fold_z == slab_len + 1, columns(across, depth + 1), merged)
            merged = jnp.concatenate([merged] * groups, axis=0)
            for g in range(groups):
                here = (row_group == g) & (lower_y if part == 0 else ~lower_y)
                shift = part * (half // 2) - g * width
                total = jnp.where(here, roll(merged, shift, 1), total)
        gathered.append(total)
    from_left, from_right = gathered
    own_last = own_columns[0]
    own_first = own_columns[1]
    shape = (half_rows, patch_len)
    lane = lane_of(shape)
    row = lax.broadcasted_iota(jnp.int32, shape, 0)
    first_row, last_row = row == 0, row == half_rows - 1
    first_side = lane < half
    quarter = half // 2
    z_cell = lax.rem(lane, quarter)
    row_y = row + jnp.where(lax.rem(lane, half) >= quarter, half_rows, 0)

    def at_y(value, step):
        return shift_y(value, step, quarter, first_row, last_row)

    z_global = depth * slab_len + z_cell - 1
    valid = (z_cell <= slab_len) & (z_global >= 0) & (z_global <= slab_len * slabs - 2)
    valid = valid & (row_y < width_y - 1)

    low_x = [
        jnp.where(
            first_side, roll(from_left, -c * stride, 1), roll(own_last, half - c * stride, 1)
        )
        for c in range(5)
    ]
    high_x = [
        jnp.where(
            first_side, roll(own_first, -c * stride, 1), roll(from_right, half - c * stride, 1)
        )
        for c in range(3)
    ]
    growth = jnp.where(valid, low_x[3], 1.0)
    scale = jnp.where(valid, low_x[4] * REST_VOLUME, 0.0) * growth
    corner = {}
    for c in range(3):
        for dx, base in ((0, low_x[c]), (1, high_x[c])):
            up = roll(base, -1, 1)
            corner[(c, 0, 0, dx)] = base
            corner[(c, 0, 1, dx)] = at_y(base, -1)
            corner[(c, 1, 0, dx)] = up
            corner[(c, 1, 1, dx)] = at_y(up, -1)
    edges = {}
    for one in range(2):
        for two in range(2):
            for axis, start in ((0, (one, two, 0)), (1, (one, 0, two)), (2, (0, one, two))):
                end = tuple(a + b for a, b in zip(start, unit(axis)))
                edges[(axis, start)] = [corner[(c, *end)] - corner[(c, *start)] for c in range(3)]
    pulls = tensions(edges, growth, scale, scale * growth)
    forces = []
    for c in range(3):

        def chosen(axis, one):
            at = ((one, 0, 0), (one, 0, 1)) if axis == 1 else ((0, one, 0), (0, one, 1))
            return jnp.where(first_side, pulls[(axis, at[1])][c], pulls[(axis, at[0])][c])

        level = []
        for dz in range(2):
            both = pulls[(0, (dz, 0, 0))][c] + at_y(pulls[(0, (dz, 1, 0))][c], 1)
            both = jnp.where(first_side, -both, both)
            along_y = chosen(1, dz)
            level.append(both + (along_y - at_y(along_y, 1)))
        along_z = chosen(2, 0) + at_y(chosen(2, 1), 1)
        forces.append((level[0] + along_z) + roll(level[1] - along_z, 1, 1))
    return forces


def far_points(dims, source, chosen, tiles):
    slab_len, width_y, patch_len, regions, slabs, pairs = dims
    depth = slab_index()
    half = patch_len // 2
    tall = TILES * ROWS

    def take(m):
        rows = pl.ds(pl.multiple_of((m * slabs + depth) * tall, tall), tall)
        tiles[pl.ds(pl.multiple_of(m * tall, tall), tall), :] = source[rows, :]

    each(regions, take, 16)
    if chosen is None:
        chosen = yield
    lane = lane_of((pairs, patch_len))
    for c in range(3):
        value = picked(chosen, tiles[pl.ds(c, regions * TILES, stride=ROWS), :], 1)
        value = jnp.where(lane < half, value[:pairs], value[pairs:])
        yield value + roll(value, half, 1)


def tile_choice(dims, slots, tiles):
    slab_len, width_y, patch_len, regions, slabs, pairs = dims
    half = patch_len // 2
    rows = regions * TILES
    found = tiles[pl.ds(3, rows, stride=ROWS), :]
    wide = max(pairs, patch_len)
    labels = [
        jnp.broadcast_to(found[:, side * half + half - 1 : side * half + half], (rows, wide))
        for side in range(2)
    ]
    row = lax.broadcasted_iota(jnp.int32, (rows, wide), 0)
    upper = lax.rem(row, TILES) > 0
    others = [jnp.where(upper, roll(label, 1, 0), roll(label, -1, 0)) for label in labels]
    again = [
        upper & (others[0] == labels[0]),
        (labels[1] == labels[0])
        | (labels[1] == others[0])
        | (upper & (others[1] == labels[1])),
    ]
    region_row = lax.broadcasted_iota(jnp.int32, (rows, pairs), 0) // TILES
    named = slots[0, 2].astype(jnp.float32)
    chosen = []
    for label, repeated in zip(labels, again):
        label = jnp.where(repeated, -1.0, label)[:, 0:pairs]
        chosen.append(jnp.where((region_row == slots[0, 1]) & (label == named), 1.0, 0.0))
    return jnp.concatenate([jnp.transpose(value) for value in chosen], axis=0)


def contact_half(dims, near, far, part, write):
    slab_len, width_y, patch_len, regions, slabs, pairs = dims
    half = patch_len // 2
    block = 8
    along = lax.rem(lane_of((block, patch_len)), half) + part * half
    along = along.astype(jnp.float32)

    def some(start):
        rows = pl.ds(start, block)
        theirs = [far[c, rows, :] for c in range(3)]
        theirs = [(theirs[0] + along) * ROOT, theirs[1] * ROOT, theirs[2] * ROOT]
        count = half // NEAR_TURNS
        others = [[roll(value, b, 1) for value in theirs] for b in range(count)]
        total = [None] * 3
        for turn in range(NEAR_TURNS):
            here = [near[turn, c, rows, :] for c in range(3)]
            sums = [None] * 3
            for other in others:
                delta = [here[c] - other[c] for c in range(3)]
                square = delta[0] * delta[0] + delta[1] * delta[1] + delta[2] * delta[2]
                weight = jnp.exp2(-square)
                for c in range(3):
                    sums[c] = add(sums[c], delta[c] * weight)
            for c in range(3):
                total[c] = add(total[c], roll(sums[c], turn * count, 1))
        for c in range(3):
            write(c, rows, total[c])

    each(pairs // block, lambda step: some(step * block), 2)


def contact_kernel(
    dims, arrived, near, slots, before, lowest, highest, selector, chosen, moved, far, tiles, pushes
):
    points = far_points(dims, arrived, None, tiles)
    next(points)
    chosen[...] = tile_choice(dims, slots, tiles)
    far[0] = points.send(chosen[...])
    far[1] = next(points)
    far[2] = next(points)

    def write(c, rows, total):
        pushes[c, rows, :] = total

    contact_half(dims, near, far, 0, write)
    slab_len, width_y, patch_len, regions, slabs, pairs = dims
    for c in range(3):
        push = picked(selector[...], pushes[c], 1) * (1.0 / ROOT)
        for z in range(slab_len):
            force = push[z * width_y : (z + 1) * width_y, :]
            if z == 0:
                force = force + lowest[c]
            if z == slab_len - 1:
                force = force + highest[c]
            moved[z, c] = before[z, c] + STEP_TIME * force


def finish_kernel(
    dims,
    arrived,
    relayed,
    moved,
    near,
    chosen,
    own_columns,
    disp,
    selector,
    new_velocity,
    new_disp,
    far,
    tiles,
    total_push,
):
    slab_len, width_y, patch_len, regions, slabs, pairs = dims
    half = patch_len // 2
    for c, value in enumerate(far_points(dims, relayed, chosen[...], tiles)):
        far[c] = value

    def write(c, rows, total):
        total_push[c, rows, :] = total

    contact_half(dims, near, far, 1, write)
    borders = border_forces(dims, arrived, relayed, own_columns)
    half_rows = width_y // 2
    lane = lane_of((half_rows, patch_len))
    last = patch_len - 1
    for c in range(3):
        push = picked(selector[...], total_push[c], 1) * (1.0 / ROOT)
        edge = borders[c]
        for z in range(slab_len):
            for part in range(2):
                at = part * (half // 2) + z + 1
                rows = slice(part * half_rows, (part + 1) * half_rows)
                start = z * width_y + part * half_rows
                force = push[start : start + half_rows, :]
                force = force + jnp.where(lane == 0, roll(edge, -at, 1), 0.0)
                force = force + jnp.where(lane == last, roll(edge, last - half - at, 1), 0.0)
                speed = moved[z, c, rows, :] + STEP_TIME * force
                new_velocity[z, c, rows, :] = speed
                new_disp[z, c, rows, :] = disp[z, c, rows, :] + STEP_TIME * speed


def local(displacement, velocity, growth, shear_modulus, pair_slots, pair_count, separation):
    slab_len, width_y, _, patch_len = displacement.shape
    regions = lax.axis_size("region")
    slabs = lax.axis_size("pair") * lax.axis_size("core")
    pairs = pair_slots.shape[3]
    dims = (slab_len, width_y, patch_len, regions, slabs, pairs)
    f32 = jnp.float32
    i32 = jnp.int32
    disp = jnp.transpose(displacement, (0, 2, 1, 3))
    speed = jnp.transpose(velocity, (0, 2, 1, 3))
    slots = jnp.transpose(pair_slots, (0, 2, 1, 3))
    apart = jnp.transpose(separation, (0, 2, 1, 3))
    plane = (width_y, patch_len)

    packet, face_a, face_b = pl.pallas_call(
        functools.partial(pack_kernel, dims),
        out_shape=(
            jax.ShapeDtypeStruct((regions * slabs * TILES * ROWS, patch_len), f32),
            jax.ShapeDtypeStruct((5, *plane), f32),
            jax.ShapeDtypeStruct((5, *plane), f32),
        ),
        in_specs=[HBM] * 4,
        out_specs=(VMEM, VMEM, VMEM),
        scratch_shapes=[
            pltpu.VMEM(((slab_len * 3 + ROWS) * width_y, patch_len), f32),
            pltpu.VMEM((slab_len, *plane), f32),
            pltpu.VMEM((slab_len, *plane), f32),
            pltpu.SMEM(slots.shape, i32),
            pltpu.SMEM((regions,), i32),
            pltpu.VMEM((2, *plane), f32),
            pltpu.SemaphoreType.DMA((4,)),
        ],
        name="pack",
    )(disp.reshape(slab_len * 3 * width_y, patch_len), growth, shear_modulus, slots)

    links = [[(i, i + 1) for i in range(first, slabs - 1, 2)] for first in (0, 1)]
    links = [link + [(b, a) for a, b in link] for link in links]
    face_a = lax.ppermute(face_a, ("pair", "core"), links[0])
    face_b = lax.ppermute(face_b, ("pair", "core"), links[1])

    packet, pair_count = lax.optimization_barrier((packet, pair_count))
    arrived = lax.all_to_all(packet, ("region", "pair", "core"), 0, 0, tiled=True)

    before, near, selector = pl.pallas_call(
        functools.partial(inner_kernel, dims),
        out_shape=(
            jax.ShapeDtypeStruct((slab_len, 3, *plane), f32),
            jax.ShapeDtypeStruct((NEAR_TURNS, 3, pairs, patch_len), f32),
            jax.ShapeDtypeStruct((slab_len * width_y, pairs), f32),
        ),
        in_specs=[VMEM] * 4 + [SMEM, VMEM, SMEM, SMEM],
        out_specs=(VMEM,) * 3,
        compiler_params=PARAMS,
        name="inner",
        cost_estimate=pl.CostEstimate(flops=4000 * 1024, bytes_accessed=1 << 20, transcendentals=0),
    )(disp, growth, shear_modulus, speed, slots, slots, pair_count, apart)

    lowest, highest, own_columns = pl.pallas_call(
        functools.partial(outer_kernel, dims),
        out_shape=(
            jax.ShapeDtypeStruct((3, *plane), f32),
            jax.ShapeDtypeStruct((3, *plane), f32),
            jax.ShapeDtypeStruct((2, width_y // 2, patch_len), f32),
        ),
        in_specs=[VMEM] * 5,
        out_specs=(VMEM,) * 3,
        compiler_params=PARAMS,
        name="outer",
        cost_estimate=pl.CostEstimate(flops=2000 * 1024, bytes_accessed=1 << 20, transcendentals=0),
    )(disp, growth, shear_modulus, face_a, face_b)

    arrived, before, lowest = lax.optimization_barrier((arrived, before, lowest))
    relayed = lax.ppermute(arrived, ("pair", "core"), links[0])

    tile_rows = regions * TILES
    chosen, moved = pl.pallas_call(
        functools.partial(contact_kernel, dims),
        out_shape=(
            jax.ShapeDtypeStruct((2 * pairs, tile_rows), f32),
            jax.ShapeDtypeStruct((slab_len, 3, *plane), f32),
        ),
        in_specs=[VMEM] * 7,
        out_specs=(VMEM,) * 2,
        scratch_shapes=[
            pltpu.VMEM((3, pairs, patch_len), f32),
            pltpu.VMEM((tile_rows * ROWS, patch_len), f32),
            pltpu.VMEM((3, pairs, patch_len), f32),
        ],
        compiler_params=PARAMS,
        name="contact",
        cost_estimate=pl.CostEstimate(flops=6000 * 1024, bytes_accessed=1 << 20, transcendentals=0),
    )(arrived, near, slots, before, lowest, highest, selector)

    new_velocity, new_disp = pl.pallas_call(
        functools.partial(finish_kernel, dims),
        out_shape=(
            jax.ShapeDtypeStruct((slab_len, 3, *plane), f32),
            jax.ShapeDtypeStruct((slab_len, 3, *plane), f32),
        ),
        in_specs=[VMEM] * 8,
        out_specs=(VMEM, VMEM),
        scratch_shapes=[
            pltpu.VMEM((3, pairs, patch_len), f32),
            pltpu.VMEM((tile_rows * ROWS, patch_len), f32),
            pltpu.VMEM((3, pairs, patch_len), f32),
        ],
        compiler_params=PARAMS,
        name="finish",
    )(
        arrived,
        relayed,
        moved,
        near,
        chosen,
        own_columns,
        disp,
        selector,
    )
    order = (0, 2, 1, 3)
    return jnp.transpose(new_velocity, order), jnp.transpose(new_disp, order)


def solution(mesh):
    shape = dict(mesh.shape)
    devices = mesh.devices.reshape(shape["region"], shape["depth"] // 2, 2)
    fine = Mesh(devices, ("region", "pair", "core"))
    depth = ("pair", "core")
    in_specs = (
        P(depth, None, None, "region"),
        P(depth, None, None, "region"),
        P(depth, None, "region"),
        P(depth, None, "region"),
        P(depth, "region", None, None),
        P(depth, "region"),
        P(depth, "region", None, None),
    )
    out_specs = (P(depth, None, None, "region"), P(depth, None, None, "region"))
    return jax.shard_map(local, mesh=fine, in_specs=in_specs, out_specs=out_specs, check_vma=False)
```
